32 devices in a mesh: dp: 16 (over z, x, core), tensor: 2 (over y).
Axes of the slice: x: 2, y: 2, z: 4, core: 2. Of those that a mesh axis runs over, the one named last changes fastest.
Arguments:
- tokens: bfloat16 [2, 4096, 2048], P(None, ('dp', 'tensor')), may hold values from -6 to 6
- segment_ids: int32 [2, 4096], P(None, 'dp'), may hold values from 0 to 2, as said below
- decay_rates: float32 [16], P('tensor'), may hold values from 0.002 to 0.08
- gain_attn: bfloat16 [2048], P('dp'), may hold values from 0.25 to 1.75
- w_query: bfloat16 [2048, 2048], P('dp', 'tensor'), may hold values from -0.125 to 0.125
- w_key: bfloat16 [2048, 2048], P('dp', 'tensor'), may hold values from -0.125 to 0.125
- w_value: bfloat16 [2048, 2048], P('dp', 'tensor'), may hold values from -0.125 to 0.125
- w_gate: bfloat16 [2048, 2048], P('dp', 'tensor'), may hold values from -0.125 to 0.125
- w_out: bfloat16 [2048, 2048], P('tensor', 'dp'), may hold values from -0.125 to 0.125
- gain_ffn: bfloat16 [2048], P('dp'), may hold values from 0.25 to 1.75
- w_left: bfloat16 [2048, 5632], P('dp', 'tensor'), may hold values from -0.125 to 0.125
- w_right: bfloat16 [2048, 5632], P('dp', 'tensor'), may hold values from -0.125 to 0.125
- w_down: bfloat16 [5632, 2048], P('tensor', 'dp'), may hold values from -0.078125 to 0.078125
- cotangent: bfloat16 [2, 4096, 2048], P(None, ('dp', 'tensor')), may hold values from -6 to 6
Outputs:
- output: bfloat16 [2, 4096, 2048], P(None, ('dp', 'tensor'))
- grad_tokens: float32 [2, 4096, 2048], P(None, ('dp', 'tensor'))
- grad_gain_attn: float32 [2048], P('dp')
- grad_w_query: float32 [2048, 2048], P('dp', 'tensor')
- grad_w_key: float32 [2048, 2048], P('dp', 'tensor')
- grad_w_value: float32 [2048, 2048], P('dp', 'tensor')
- grad_w_gate: float32 [2048, 2048], P('dp', 'tensor')
- grad_w_out: float32 [2048, 2048], P('tensor', 'dp')
- grad_gain_ffn: float32 [2048], P('dp')
- grad_w_left: float32 [2048, 5632], P('dp', 'tensor')
- grad_w_right: float32 [2048, 5632], P('dp', 'tensor')
- grad_w_down: float32 [5632, 2048], P('tensor', 'dp')
The draws below stay inside these ranges and needn't reach their ends.
Inputs may be any that keep to these rules, and one draw needn't show every extreme that they name: `segment_ids`: each micro-batch's 4096 tokens are 16 sequences of 256 tokens; within a sequence the ids never fall and 0, 1 and 2 each mark one document of at least 32 tokens; document 1 holds the sequence's two middle tokens.
All inputs are finite; a program needn't handle non-finite values.
Results may differ from the reference program's by a relative error of at most 0.015.
Values may be sent and summed in bfloat16 or wider, within the bound.
A program may use at most 256 MiB of HBM per device.

```python
import math
import jax
import jax.numpy as jnp
from jax import lax

D = 2048
HEADS = 16
HEAD_DIM = 128
FF = 5632
SEQ = 256
MB = 2
TOKENS = 4096


def draw_segment_ids(key, part):
    sequences = MB * (TOKENS // SEQ)
    first_key, second_key = jax.random.split(key)
    first_cut = jax.random.randint(first_key, (sequences, 1), SEQ // 8, 3 * SEQ // 8)
    second_cut = jax.random.randint(second_key, (sequences, 1), 5 * SEQ // 8, 7 * SEQ // 8)
    places = jnp.arange(SEQ)[None, :]
    labels = (places >= first_cut).astype(jnp.int32) + (places >= second_cut).astype(jnp.int32)
    return labels.reshape(MB, TOKENS)


def block_levels(rng, dims, cuts, least, top_value):
    def one(axis_at, blocks):
        heights = jax.random.uniform(jax.random.fold_in(jax.random.fold_in(rng, 6), axis_at), (blocks,), jnp.float32, least / len(cuts), top_value / len(cuts))
        return jnp.repeat(jnp.exp(heights), dims[axis_at] // blocks).reshape((-1,) + (1,) * (len(dims) - axis_at - 1))

    factor_of = one(*cuts[0])
    for cut in cuts[1:]:
        factor_of = factor_of * one(*cut)
    return factor_of


def normal_values(rng, dims, width, bound, shards=(), dtype=jnp.bfloat16):
    values = width * jax.random.normal(rng, dims, jnp.float32)
    if shards:
        values = values * block_levels(rng, dims, shards, -0.22, 0.18)
    return jnp.clip(values, -bound, bound).astype(dtype)


def setup_inputs(seed: int = 0) -> dict:
    arg_keys = jax.random.split(jax.random.key(seed), 15)
    return {
        "tokens": normal_values(arg_keys[0], (MB, TOKENS, D), 1.0, 6.0, ((1, 32),)),
        "segment_ids": draw_segment_ids(jax.random.fold_in(arg_keys[14], 71), 0),
        "decay_rates": jnp.clip(jnp.exp(math.log(0.08) - 3.6888794 * jax.random.uniform(arg_keys[2], (HEADS,), jnp.float32) ** block_levels(arg_keys[2], (HEADS,), ((0, 2),), -0.2, 0.2)), 0.002, 0.08),
        "gain_attn": jnp.clip(1.0 + 0.15 * jax.random.normal(arg_keys[3], (D,), jnp.float32), 0.25, 1.75).astype(jnp.bfloat16),
        "w_query": normal_values(arg_keys[4], (D, D), D ** -0.5, 0.125, ((0, 16), (1, 2))),
        "w_key": normal_values(arg_keys[5], (D, D), D ** -0.5, 0.125, ((0, 16), (1, 2))),
        "w_value": normal_values(arg_keys[6], (D, D), D ** -0.5, 0.125, ((0, 16), (1, 2))),
        "w_gate": normal_values(arg_keys[7], (D, D), D ** -0.5, 0.125, ((0, 16), (1, 2))),
        "w_out": normal_values(arg_keys[8], (D, D), D ** -0.5, 0.125, ((0, 2), (1, 16))),
        "gain_ffn": jnp.clip(1.0 + 0.15 * jax.random.normal(arg_keys[9], (D,), jnp.float32), 0.25, 1.75).astype(jnp.bfloat16),
        "w_left": normal_values(arg_keys[10], (D, FF), D ** -0.5, 0.125, ((0, 16), (1, 2))),
        "w_right": normal_values(arg_keys[11], (D, FF), D ** -0.5, 0.125, ((0, 16), (1, 2))),
        "w_down": normal_values(arg_keys[12], (FF, D), FF ** -0.5, 0.078125, ((0, 2), (1, 16))),
        "cotangent": normal_values(arg_keys[13], (MB, TOKENS, D), 1.0, 6.0, ((1, 32),)),
    }


@jax.custom_vjp
def low(v):
    return lax.optimization_barrier(v.astype(jnp.bfloat16)).astype(jnp.float32)

@jax.custom_vjp
def low_back(v):
    return v

def low_keep(v):
    return (low(v), None)

def low_pass(kept, grad):
    return (grad,)

def back_keep(v):
    return (v, None)

def back_low(kept, grad):
    return (low(grad),)
low.defvjp(low_keep, low_pass)
low_back.defvjp(back_keep, back_low)
EPSILON = 1e-06
HIGHEST = lax.Precision.HIGHEST

def scaled(values):
    return values * lax.rsqrt(lax.optimization_barrier(jnp.mean(values * values, axis=-1, keepdims=True)) + EPSILON)

def product(former, latter):
    return jnp.dot(former, latter, precision=HIGHEST, preferred_element_type=jnp.float32)

def layer_forward(params, inputs, segments, decay_rates):
    gain_attn, w_query, w_key, w_value, w_gate, w_out, gain_ffn, w_left, w_right, w_down = params
    length = inputs.shape[0]
    normed = low(scaled(inputs) * gain_attn)
    query_pre = low_back(product(normed, w_query))
    key_pre = low_back(product(normed, w_key))
    queries = low(jax.nn.silu(query_pre)).reshape(length, HEADS, HEAD_DIM)
    key_rows = low(jax.nn.silu(key_pre)).reshape(length, HEADS, HEAD_DIM)
    value_rows = low(low_back(product(normed, w_value))).reshape(length, HEADS, HEAD_DIM)
    gate_proj = low_back(product(normed, w_gate))
    scores = low_back(jnp.einsum('ihd,jhd->hij', queries, key_rows, precision=HIGHEST))
    places = jnp.arange(length)
    offset = (places[:, None] - places[None, :]).astype(jnp.float32)
    allowed = (offset >= 0.0) & (segments[:, None] == segments[None, :])
    decay_table = jnp.exp(-decay_rates[:, None, None] * jnp.maximum(offset, 0.0)[None])
    masked = jnp.where(allowed[None], decay_table, 0.0)
    weights = low(scores * masked)
    mixed_heads = low_back(jnp.einsum('hij,jhd->ihd', weights, value_rows, precision=HIGHEST).reshape(length, D))
    branch = low(scaled(mixed_heads) * gate_proj)
    middle = inputs + low_back(product(branch, w_out))
    normed_ffn = low(scaled(middle) * gain_ffn)
    left_proj = low_back(product(normed_ffn, w_left))
    right_proj = low_back(product(normed_ffn, w_right))
    joined = low(left_proj * right_proj)
    return middle + low_back(product(joined, w_down))

def reference(tokens, segment_ids, decay_rates, gain_attn, w_query, w_key, w_value, w_gate, w_out, gain_ffn, w_left, w_right, w_down, cotangent):
    sequences = tokens.shape[0] * tokens.shape[1] // SEQ
    inputs = tokens.astype(jnp.float32).reshape(sequences, SEQ, D)
    segments = segment_ids.reshape(sequences, SEQ)
    params = tuple((element.astype(jnp.float32) for element in (gain_attn, w_query, w_key, w_value, w_gate, w_out, gain_ffn, w_left, w_right, w_down)))
    checked = jax.checkpoint(layer_forward)

    def forward(inputs, params):

        def single(element):
            return checked(params, element[0], element[1], decay_rates)
        return lax.map(single, (inputs, segments))
    result, pullback = jax.vjp(forward, inputs, params)
    grad_inputs, grad_params = pullback(cotangent.astype(jnp.float32).reshape(sequences, SEQ, D))
    outline = tokens.shape
    return (result.reshape(outline).astype(jnp.bfloat16), grad_inputs.reshape(outline), grad_params[0], grad_params[1], grad_params[2], grad_params[3], grad_params[4], grad_params[5], grad_params[6], grad_params[7], grad_params[8], grad_params[9])
```

```python
import jax
import jax.numpy as jnp
from jax import lax
from jax.sharding import PartitionSpec as P

EPSILON = 1e-06


def scaled_rows(values):
    inverse = lax.rsqrt(jnp.mean(values * values, axis=-1, keepdims=True) + EPSILON)
    return (values * inverse, inverse)


def times_transposed(former, latter):
    return lax.dot_general(
        former, latter, (((1,), (1,)), ((), ())), preferred_element_type=jnp.float32
    )


def transposed_times(former, latter):
    return lax.dot_general(
        former, latter, (((0,), (0,)), ((), ())), preferred_element_type=jnp.float32
    )


def silu_slope(values):
    sigmoid = jax.nn.sigmoid(values)
    return sigmoid * (1.0 + values * (1.0 - sigmoid))


def norm_backward(grad_normed, unit_rows, inverse, gain_values):
    scaled_grad = grad_normed * gain_values
    return inverse * (
        scaled_grad - unit_rows * jnp.mean(scaled_grad * unit_rows, axis=-1, keepdims=True)
    )


def fetch_attention(gain_attn, joined_in, w_out):
    return (
        lax.all_gather(gain_attn, "dp", axis=0, tiled=True),
        lax.all_gather(joined_in, "dp", axis=0, tiled=True),
        lax.all_gather(w_out, "dp", axis=1, tiled=True),
    )


def fetch_feedforward(gain_ffn, joined_pair, w_down):
    return (
        lax.all_gather(gain_ffn, "dp", axis=0, tiled=True),
        lax.all_gather(joined_pair, "dp", axis=0, tiled=True),
        lax.all_gather(w_down, "dp", axis=1, tiled=True),
    )


def local(
    tokens,
    segment_ids,
    decay_rates,
    gain_attn,
    w_query,
    w_key,
    w_value,
    w_gate,
    w_out,
    gain_ffn,
    w_left,
    w_right,
    w_down,
    cotangent,
):
    batches, local_rows, model_width = tokens.shape
    length = segment_ids.shape[1]
    local_heads = decay_rates.shape[0]
    local_width = w_query.shape[1]
    head_width = local_width // local_heads
    local_units = w_left.shape[1]
    joined_in = jnp.concatenate([w_query, w_key, w_value, w_gate], axis=1)
    joined_pair = jnp.concatenate([w_left, w_right], axis=1)
    places = jnp.arange(length)
    offset = (places[:, None] - places[None, :]).astype(jnp.float32)
    decay_table = jnp.exp(-decay_rates[:, None, None] * jnp.maximum(offset, 0.0)[None])
    rows = batches * length
    flat = lambda values: values.reshape(rows, values.shape[-1])
    gain_full, weight_in, weight_out = fetch_attention(gain_attn, joined_in, w_out)
    inputs = tokens.astype(jnp.float32)
    unit_attn, inverse_attn = scaled_rows(inputs)
    normed = (unit_attn * gain_full.astype(jnp.float32)).astype(jnp.bfloat16)
    normed_all = flat(lax.all_gather(normed, "tensor", axis=1, tiled=True))
    upstream_all = flat(lax.all_gather(cotangent, "tensor", axis=1, tiled=True))
    projected = jnp.dot(normed_all, weight_in, preferred_element_type=jnp.float32)
    query_pre = projected[:, :local_width]
    key_pre = projected[:, local_width : 2 * local_width]
    heads = lambda values: values.astype(jnp.bfloat16).reshape(
        batches, length, local_heads, head_width
    )
    value_rows = heads(projected[:, 2 * local_width : 3 * local_width])
    gate_proj = projected[:, 3 * local_width :]
    queries = heads(jax.nn.silu(query_pre))
    key_rows = heads(jax.nn.silu(key_pre))
    allowed = (offset >= 0.0)[None] & (segment_ids[:, :, None] == segment_ids[:, None, :])
    masked = jnp.where(allowed[:, None], decay_table[None], 0.0)
    scores = jnp.einsum("bihd,bjhd->bhij", queries, key_rows, preferred_element_type=jnp.float32)
    weights = (scores * masked).astype(jnp.bfloat16)
    mixed_heads = flat(
        jnp.einsum(
            "bhij,bjhd->bihd", weights, value_rows, preferred_element_type=jnp.float32
        ).reshape(batches, length, local_width)
    )
    square_sum = lax.psum(jnp.sum(mixed_heads * mixed_heads, axis=-1), "tensor")
    inverse_mixed = lax.rsqrt(square_sum / model_width + EPSILON)[:, None]
    unit_mixed = mixed_heads * inverse_mixed
    branch = (unit_mixed * gate_proj).astype(jnp.bfloat16)

    def scatter_rows(values):
        return lax.psum_scatter(
            values.astype(jnp.bfloat16).reshape(batches, length, model_width),
            "tensor",
            scatter_dimension=1,
            tiled=True,
        ).astype(jnp.float32)

    middle = inputs + scatter_rows(
        jnp.dot(branch, weight_out, preferred_element_type=jnp.float32)
    )
    gain_ffn_full, weight_pair, weight_down = fetch_feedforward(gain_ffn, joined_pair, w_down)
    unit_ffn, inverse_ffn = scaled_rows(middle)
    normed_ffn = (unit_ffn * gain_ffn_full.astype(jnp.float32)).astype(jnp.bfloat16)
    normed_ffn_all = flat(lax.all_gather(normed_ffn, "tensor", axis=1, tiled=True))
    both_proj = jnp.dot(normed_ffn_all, weight_pair, preferred_element_type=jnp.float32)
    left_proj = both_proj[:, :local_units]
    right_proj = both_proj[:, local_units:]
    joined = (left_proj * right_proj).astype(jnp.bfloat16)
    result = middle + scatter_rows(
        jnp.dot(joined, weight_down, preferred_element_type=jnp.float32)
    )

    def over_dp(values, dimension):
        return lax.psum_scatter(
            values.astype(jnp.bfloat16), "dp", scatter_dimension=dimension, tiled=True
        ).astype(jnp.float32)

    grad_down = over_dp(transposed_times(joined, upstream_all), 1)
    grad_joined = times_transposed(upstream_all, weight_down)
    grad_left = (grad_joined * right_proj).astype(jnp.bfloat16)
    grad_right = (grad_joined * left_proj).astype(jnp.bfloat16)
    grad_pair = jnp.concatenate([grad_left, grad_right], axis=1)
    grad_pair_all = over_dp(transposed_times(normed_ffn_all, grad_pair), 0)
    grad_normed_ffn = scatter_rows(times_transposed(grad_pair, weight_pair))
    total_gain_ffn = jnp.sum(grad_normed_ffn * unit_ffn, axis=(0, 1))
    grad_middle = cotangent.astype(jnp.float32) + norm_backward(
        grad_normed_ffn, unit_ffn, inverse_ffn, gain_ffn_full.astype(jnp.float32)
    )
    grad_attn_out = grad_middle.astype(jnp.bfloat16)
    grad_out_all = flat(lax.all_gather(grad_attn_out, "tensor", axis=1, tiled=True))
    grad_out = over_dp(transposed_times(branch, grad_out_all), 1)
    grad_branch = times_transposed(grad_out_all, weight_out)
    grad_unit = grad_branch * gate_proj
    grad_gate = (grad_branch * unit_mixed).astype(jnp.bfloat16)
    dot_sum = lax.psum(jnp.sum(grad_unit * unit_mixed, axis=-1), "tensor")
    grad_mixed = heads(
        inverse_mixed * (grad_unit - unit_mixed * (dot_sum / model_width)[:, None])
    )
    grad_weights = jnp.einsum(
        "bihd,bjhd->bhij", grad_mixed, value_rows, preferred_element_type=jnp.float32
    )
    grad_scores = (grad_weights * masked).astype(jnp.bfloat16)
    joined_heads = lambda values: values.reshape(rows, local_width)
    grad_queries = joined_heads(
        jnp.einsum("bhij,bjhd->bihd", grad_scores, key_rows, preferred_element_type=jnp.float32)
    )
    grad_keys = joined_heads(
        jnp.einsum("bhij,bihd->bjhd", grad_scores, queries, preferred_element_type=jnp.float32)
    )
    grad_values = joined_heads(
        jnp.einsum("bhij,bihd->bjhd", weights, grad_mixed, preferred_element_type=jnp.float32)
    ).astype(jnp.bfloat16)
    grad_query_pre = (grad_queries * silu_slope(query_pre)).astype(jnp.bfloat16)
    grad_key_pre = (grad_keys * silu_slope(key_pre)).astype(jnp.bfloat16)
    grad_projected = jnp.concatenate([grad_query_pre, grad_key_pre, grad_values, grad_gate], axis=1)
    grad_in = over_dp(transposed_times(normed_all, grad_projected), 0)
    grad_normed = scatter_rows(times_transposed(grad_projected, weight_in))
    total_gain_attn = jnp.sum(grad_normed * unit_attn, axis=(0, 1))
    grad_tokens = grad_middle + norm_backward(
        grad_normed, unit_attn, inverse_attn, gain_full.astype(jnp.float32)
    )
    gains = lax.psum_scatter(
        lax.psum(jnp.stack([total_gain_attn, total_gain_ffn]), "tensor"),
        "dp",
        scatter_dimension=1,
        tiled=True,
    )
    return (
        result.astype(jnp.bfloat16),
        grad_tokens,
        gains[0],
        grad_in[:, :local_width],
        grad_in[:, local_width : 2 * local_width],
        grad_in[:, 2 * local_width : 3 * local_width],
        grad_in[:, 3 * local_width :],
        grad_out,
        gains[1],
        grad_pair_all[:, :local_units],
        grad_pair_all[:, local_units:],
        grad_down,
    )


def solution(mesh):
    return jax.shard_map(
        local,
        mesh=mesh,
        in_specs=(
            P(None, ("dp", "tensor"), None),
            P(None, "dp"),
            P("tensor"),
            P("dp"),
            P("dp", "tensor"),
            P("dp", "tensor"),
            P("dp", "tensor"),
            P("dp", "tensor"),
            P("tensor", "dp"),
            P("dp"),
            P("dp", "tensor"),
            P("dp", "tensor"),
            P("tensor", "dp"),
            P(None, ("dp", "tensor"), None),
        ),
        out_specs=(
            P(None, ("dp", "tensor"), None),
            P(None, ("dp", "tensor"), None),
            P("dp"),
            P("dp", "tensor"),
            P("dp", "tensor"),
            P("dp", "tensor"),
            P("dp", "tensor"),
            P("tensor", "dp"),
            P("dp"),
            P("dp", "tensor"),
            P("dp", "tensor"),
            P("tensor", "dp"),
        ),
        check_vma=False,
    )
```

```python
import functools

import jax
import jax.numpy as jnp
from jax import lax
from jax.experimental import pallas as pl
from jax.experimental.pallas import tpu as pltpu
from jax.sharding import PartitionSpec as P

EPSILON = 1e-06
LAYERS = 4
CORES = 2
LANES = 128
AHEAD = 3
SUMS = 3
FETCH = 3
MESH = pl.DeviceIdType.MESH


class Place:
    def __init__(self, mids):
        place = lax.axis_index("dp")
        self.mids = mids
        self.t = lax.axis_index("tensor")
        self.k = lax.rem(place, CORES)
        self.m = lax.rem(lax.div(place, CORES), mids)
        self.z = lax.div(place, CORES * mids)

    def device(self, z, m, k):
        return ((z * self.mids + m) * CORES + k, self.t)

    def layer(self, step):
        return lax.rem(self.z + step, LAYERS)

    def mid(self, step):
        return lax.rem(self.m + step, self.mids)

    def row(self, core, batch, half, part):
        return pl.multiple_of(((core * 2 + batch) * 2 + half) * part, part)

    def weight_peers(self):
        peers = [self.device(self.z, self.m, 1 - self.k)]
        for step in range(1, LAYERS):
            for core in range(CORES):
                peers.append(self.device(self.layer(step), self.m, core))
        for step in range(1, self.mids):
            peers.append(self.device(self.z, self.mid(step), self.k))
        return peers


def greet(peers):
    barrier = pltpu.get_barrier_semaphore()
    for peer in peers:
        pl.semaphore_signal(barrier, inc=1, device_id=peer, device_id_type=MESH)
    pl.semaphore_wait(barrier, len(peers))


def remote(source, target, send, receive, peer):
    return pltpu.make_async_remote_copy(
        src_ref=source,
        dst_ref=target,
        send_sem=send,
        recv_sem=receive,
        device_id=peer,
        device_id_type=MESH,
    )


class Gather:
    def __init__(self, place, source, target, sems):
        self.source, self.target = source, target
        self.send, self.receive, self.local = sems
        here = place
        self.hops = []
        sibling = 1 - here.k
        own = target.at[here.z, here.m, here.k]
        self.hops.append(
            remote(
                source.at[sibling],
                own,
                self.send.at[0],
                self.receive.at[0],
                here.device(here.z, here.m, sibling),
            )
        )
        self.arrivals = self.hops[:]
        for step in range(1, LAYERS):
            for core in range(CORES):
                slot = 1 + (step - 1) * CORES
                hop = functools.partial(
                    remote,
                    source.at[core],
                    own,
                    self.send.at[slot + core],
                    peer=here.device(here.layer(step), here.m, core),
                )
                self.hops.append(hop(self.receive.at[slot + here.k]))
                self.arrivals.append(hop(self.receive.at[slot + core]))
        self.keep = pltpu.make_async_copy(source.at[here.k], own, self.local)
        base = 1 + (LAYERS - 1) * CORES
        row = target.at[:, here.m]
        self.crossings = [
            remote(
                row,
                row,
                self.send.at[base + step - 1],
                self.receive.at[base + step - 1],
                here.device(here.z, here.mid(step), here.k),
            )
            for step in range(1, here.mids)
        ]

    def start(self):
        self.keep.start()
        for hop in self.hops:
            hop.start()

    def cross(self):
        self.keep.wait()
        for hop in self.arrivals:
            hop.wait_recv()
        for crossing in self.crossings:
            crossing.start()

    def arrive(self):
        for crossing in self.crossings:
            crossing.wait_recv()

    def finish(self):
        for hop in self.hops + self.crossings:
            hop.wait_send()


class Reduce:
    def __init__(self, place, source, crossed, landed, output, slots, sems):
        self.place, self.source, self.crossed, self.landed = place, source, crossed, landed
        self.output = output
        self.own_slot, self.cross_slot, self.sum_slot, self.land_slot, self.out_slot = slots
        send, receive, local = sems
        here = place
        self.crossings = [
            remote(
                source.at[:, here.mid(step)],
                crossed.at[step - 1],
                send.at[step - 1],
                receive.at[step - 1],
                here.device(here.z, here.mid(step), here.k),
            )
            for step in range(1, here.mids)
        ]
        base = here.mids - 1
        sibling = 1 - here.k
        self.hops = [
            remote(
                self.sum_slot.at[here.z, sibling],
                landed.at[here.k, 0],
                send.at[base],
                receive.at[base],
                here.device(here.z, here.m, sibling),
            )
        ]
        self.arrivals = self.hops[:]
        for step in range(1, LAYERS):
            for core in range(CORES):
                slot = base + 1 + (step - 1) * CORES
                hop = functools.partial(
                    remote,
                    self.sum_slot.at[here.layer(step), core],
                    landed.at[here.k, step],
                    send.at[slot + core],
                    peer=here.device(here.layer(step), here.m, core),
                )
                self.hops.append(hop(receive.at[slot + here.k]))
                self.arrivals.append(hop(receive.at[slot + core]))
        self.keep = pltpu.make_async_copy(
            self.sum_slot.at[here.z, here.k], landed.at[here.k, 0], local.at[0]
        )
        self.load_own = pltpu.make_async_copy(source.at[:, here.m], self.own_slot, local.at[1])
        self.load_cross = pltpu.make_async_copy(crossed, self.cross_slot, local.at[2])
        self.load_land = pltpu.make_async_copy(landed, self.land_slot, local.at[3])
        self.store = pltpu.make_async_copy(self.out_slot, output, local.at[4])

    def start(self):
        for crossing in self.crossings:
            crossing.start()

    def load(self):
        self.load_own.start()
        for crossing in self.crossings:
            crossing.wait_recv()
        self.load_cross.start()

    def add(self):
        self.load_own.wait()
        self.load_cross.wait()

        @pl.loop(0, LAYERS * CORES)
        def _(at):
            layer, core = lax.div(at, CORES), lax.rem(at, CORES)
            total = self.own_slot[layer, core].astype(jnp.float32)
            for step in range(1, self.place.mids):
                total += self.cross_slot[step - 1, layer, core].astype(jnp.float32)
            self.sum_slot[layer, core] = total.astype(jnp.bfloat16)

        self.keep.start()
        for hop in self.hops:
            hop.start()

    def release(self):
        for hop in self.hops:
            hop.wait_send()

    def fetch(self):
        self.keep.wait()
        for hop in self.arrivals:
            hop.wait_recv()
        self.load_land.start()

    def total(self):
        self.load_land.wait()

        @pl.loop(0, CORES)
        def _(core):
            total = self.land_slot[core, 0].astype(jnp.float32)
            for step in range(1, LAYERS):
                total += self.land_slot[core, step].astype(jnp.float32)
            self.out_slot[core] = total

        self.store.start()

    def finish(self):
        for crossing in self.crossings:
            crossing.wait_send()


def dots(left, right, left_axis, right_axis):
    return lax.dot_general(
        left, right, (((left_axis,), (right_axis,)), ((), ())), preferred_element_type=jnp.float32
    )


class Reducer:
    def __init__(self, chunks):
        self.chunks = chunks
        self.produced = self.started = self.ticks = 0

    def launch(self):
        while self.started < min(self.produced, self.ticks + AHEAD + 1):
            self.chunks[self.started].start()
            self.started += 1

    def produce(self):
        self.produced += 1
        self.launch()

    def tick(self):
        at, chunks = self.ticks, self.chunks
        count = len(chunks)
        if at < count:
            assert at < self.started
            chunks[at].load()
        if 1 <= at <= count:
            if at - 1 >= SUMS:
                chunks[at - 1 - SUMS].release()
            chunks[at - 1].add()
        if FETCH <= at < count + FETCH:
            chunks[at - FETCH].fetch()
        if FETCH + 1 <= at:
            if at - FETCH - 1 >= 2:
                chunks[at - FETCH - 3].store.wait()
            chunks[at - FETCH - 1].total()
        self.ticks += 1
        self.launch()

    def drain(self):
        count = len(self.chunks)
        while self.ticks < count + FETCH + 1:
            self.tick()
        for chunk in self.chunks[-2:]:
            chunk.store.wait()
        for chunk in self.chunks[-SUMS:]:
            chunk.release()
        for chunk in self.chunks:
            chunk.finish()


class Spread:
    def __init__(self, here, buffer, part, send, receive):
        sibling = here.device(here.z, here.m, 1 - here.k)
        other = (here.device(here.z, here.m, here.k)[0], 1 - here.t)
        self.across, self.beside, self.onward = [], [], []
        for batch in range(2):
            own = buffer.at[pl.ds(here.row(here.k, batch, here.t, part), part)]
            theirs = buffer.at[pl.ds(here.row(here.k, batch, 1 - here.t, part), part)]
            self.across.append(remote(own, own, send.at[batch], receive.at[batch], other))
            self.beside.append(remote(own, own, send.at[2 + batch], receive.at[2 + batch], sibling))
            self.onward.append(
                remote(theirs, theirs, send.at[4 + batch], receive.at[4 + batch], sibling)
            )

    def start(self, batch):
        self.across[batch].start()
        self.beside[batch].start()

    def forward(self):
        for batch in range(2):
            self.across[batch].wait_recv()
            self.onward[batch].start()

    def arrive(self):
        for copy in self.beside + self.onward:
            copy.wait_recv()

    def finish(self):
        for copy in self.across + self.beside + self.onward:
            copy.wait_send()


def backward_kernel(mids, *refs):
    f32, bf16 = jnp.float32, jnp.bfloat16
    (
        rates,
        onehot,
        gains,
        inverse,
        tokens,
        middle,
        cotangent,
        normed_ffn_hbm,
        upstream_hbm,
        normed_hbm,
        act_hbm,
        partial_hbm,
        result_hbm,
        saved_hbm,
        values_hbm,
        weights_hbm,
        out_f,
        out_qkv,
        out_go,
        out_gain,
        grad_tokens,
        result,
        p_f,
        p_qkv,
        p_go,
        p_gain,
        *rest,
    ) = refs
    crossed, landed, rest = rest[:4], rest[4:8], rest[8:]
    (
        normed,
        upstream,
        grad_out,
        act,
        stage,
        own_slot,
        cross_slot,
        sum_slot,
        land_slot,
        out_slot,
        saved,
        values,
        weights,
        projected,
        branch,
        total,
        part,
        part_in,
        across,
        across_in,
        kept,
        grad_middle,
        dot_sum,
        table,
        same,
        columns,
        send,
        receive,
        local,
        row_send,
        row_receive,
        load_sem,
        stage_sem,
        free,
    ) = rest
    rows, width = normed.shape
    half = rows // CORES
    part_rows = half // 4
    length = 2 * part_rows
    heads, units = saved_hbm.shape[0], act_hbm.shape[0]
    here = Place(mids)
    sibling = here.device(here.z, here.m, 1 - here.k)
    other = (here.device(here.z, here.m, here.k)[0], 1 - here.t)
    greet(here.weight_peers() + [other])

    chunks = []
    lists = [(p_f, index, 0, out_f, act.shape[-1]) for index in range(units)]
    for index in range(heads):
        lists.append((p_qkv, index, 1, out_qkv, 3 * LANES))
        lists.append((p_go, index, 2, out_go, 2 * LANES))
    lists.append((p_gain, 0, 3, out_gain, LANES))
    for at, (source, index, kind, output, wide) in enumerate(lists):
        slots = [
            slot.at[(at % slot.shape[0],) + (slice(None),) * (len(slot.shape) - 2) + (pl.ds(0, wide),)]
            for slot in (own_slot, cross_slot, sum_slot, land_slot, out_slot)
        ]
        chunks.append(
            Reduce(
                here,
                source.at[index],
                crossed[kind].at[index],
                landed[kind].at[index],
                output.at[index],
                slots,
                (send.at[at], receive.at[at], local.at[at]),
            )
        )
    reducer = Reducer(chunks)

    def load(source, target, at):
        return pltpu.make_async_copy(source, target, load_sem.at[at])

    loads = {
        "normed_ffn": load(normed_ffn_hbm, normed, 0),
        "upstream": load(upstream_hbm, upstream, 1),
        "part": load(partial_hbm.at[pl.ds(here.k * half, half)], part, 2),
        "normed": load(normed_hbm, normed, 3),
    }
    acts = [load(act_hbm.at[at], act.at[at % 2], 4 + at % 2) for at in range(units)]
    head_loads = [
        (
            load(saved_hbm.at[at], saved.at[at % 2], 6 + at % 2),
            load(values_hbm.at[at], values.at[at % 2], 8 + at % 2),
            load(weights_hbm.at[at], weights.at[at % 2], 10 + at % 2),
        )
        for at in range(heads)
    ]
    loads["normed_ffn"].start()
    acts[0].start()
    loads["upstream"].start()
    loads["part"].start()

    def swap_beside(source, at):
        return remote(source, part_in, row_send.at[12 + at], row_receive.at[12 + at], sibling)

    def swap_across(batch, at):
        block = pl.ds(batch * part_rows, part_rows)
        return remote(
            across.at[block],
            across_in.at[block],
            row_send.at[15 + 2 * at + batch],
            row_receive.at[15 + 2 * at + batch],
            other,
        )

    beside = swap_beside(partial_hbm.at[pl.ds((1 - here.k) * half, half)], 0)
    beside.start()

    down = lax.broadcasted_iota(jnp.int32, (length, length), 0)
    right = lax.broadcasted_iota(jnp.int32, (length, length), 1)
    offset = (down - right).astype(f32)
    for head in range(heads):
        decay = jnp.exp(-rates[head] * jnp.maximum(offset, 0.0))
        table[head] = jnp.where(down >= right, decay, 0.0)
    for sequence in range(rows // length):
        marks = onehot[pl.ds(sequence * length, length), :]
        same[sequence] = dots(marks, marks, 1, 1)

    per_block = 2 * LANES
    group = per_block // (CORES * p_f.shape[4])
    turns = mids // group

    def store_block(slot, at, first, value):
        layer, chip = lax.div(at, turns), lax.rem(at, turns) * group
        shaped = value.astype(bf16).reshape(group, CORES, p_f.shape[4], value.shape[-1])
        stage[slot, layer, pl.ds(chip, group), :, :, pl.ds(first, value.shape[-1])] = shaped

    def stage_out(slot, target):
        wide = target.shape[-1]
        return pltpu.make_async_copy(
            stage.at[slot, :, :, :, :, pl.ds(0, wide)], target, stage_sem.at[slot]
        )

    pending = [None, None]

    def flush(slot):
        if pending[slot] is not None:
            pending[slot].wait()
            pending[slot] = None
            reducer.produce()

    def unit_chunk(at):
        slot = at % 2
        if at + 1 < units:
            acts[at + 1].start()
        acts[at].wait()
        flush(slot)

        @pl.loop(0, width // per_block)
        def _(block):
            where = pl.ds(pl.multiple_of(block * per_block, per_block), per_block)
            store_block(slot, block, 0, dots(normed[:, where], act[slot, :, : 2 * LANES], 0, 0))
            store_block(
                slot, block, 2 * LANES, dots(upstream[:, where], act[slot, :, 2 * LANES :], 0, 0)
            )

        flush(1 - slot)
        pending[slot] = stage_out(slot, p_f.at[at])
        pending[slot].start()

    step_rows = 16

    def row_loop(count):
        return pl.loop(0, count // step_rows)

    def at_rows(base, index):
        return pl.ds(pl.multiple_of(base + index * step_rows, step_rows), step_rows)

    def reduce_beside(own):
        def leave(batch):
            @row_loop(part_rows)
            def _(index):
                base = batch * length + (1 - here.t) * part_rows
                value = own(base, index) + part_in[at_rows(base, index), :].astype(f32)
                across[at_rows(batch * part_rows, index), :] = value.astype(bf16)

        def keep(batch):
            @row_loop(part_rows)
            def _(index):
                base = batch * length + here.t * part_rows
                value = own(base, index) + part_in[at_rows(base, index), :].astype(f32)
                kept[at_rows(batch * part_rows, index), :] = value

        return leave, keep

    loads["normed_ffn"].wait()
    loads["upstream"].wait()
    unit_chunk(0)
    unit_chunk(1)
    loads["part"].wait()
    beside.wait_recv()
    leave, keep = reduce_beside(lambda base, index: part[at_rows(base, index), :].astype(f32))
    crossings = [swap_across(batch, 0) for batch in range(2)]
    for batch in range(2):
        leave(batch)
        crossings[batch].start()
    for batch in range(2):
        keep(batch)
    for at in range(2, 6):
        unit_chunk(at)
    reducer.tick()
    columns[...] = jnp.zeros_like(columns)
    rows_go = Spread(here, grad_out, part_rows, row_send.at[pl.ds(0, 6)], row_receive.at[pl.ds(0, 6)])
    rows_dot = Spread(here, dot_sum, part_rows, row_send.at[pl.ds(6, 6)], row_receive.at[pl.ds(6, 6)])

    for batch in range(2):
        crossings[batch].wait_recv()
        base = here.row(here.k, batch, here.t, part_rows)

        @row_loop(part_rows)
        def _(index):
            here_rows = at_rows(batch * part_rows, index)
            grad = kept[here_rows, :] + across_in[here_rows, :].astype(f32)
            mid = middle[here_rows, :]
            scale = lax.rsqrt(jnp.mean(mid * mid, axis=-1, keepdims=True) + EPSILON)
            unit = mid * scale
            weighted = grad * unit
            columns[1] += weighted[:8] + weighted[8:]
            scaled = grad * gains[1:2, :]
            slope = cotangent[here_rows, :].astype(f32) + scale * (
                scaled - unit * jnp.mean(scaled * unit, axis=-1, keepdims=True)
            )
            grad_middle[here_rows, :] = slope
            rounded = slope.astype(bf16)
            grad_out[at_rows(base, index), :] = rounded
            attended = mid - tokens[here_rows, :].astype(f32)
            inner = jnp.mean(rounded.astype(f32) * attended, axis=-1, keepdims=True)
            dot_sum[at_rows(base, index), :] = jnp.broadcast_to(inner, (step_rows, LANES))

        rows_go.start(batch)
        rows_dot.start(batch)
    for at in range(6, 9):
        unit_chunk(at)
    reducer.tick()
    rows_go.forward()
    rows_dot.forward()
    for at in range(9, units):
        unit_chunk(at)
    for copy in head_loads[0]:
        copy.start()
    loads["normed"].start()
    reducer.tick()
    rows_go.arrive()
    rows_dot.arrive()
    loads["normed"].wait()
    beside.wait_send()
    beside = swap_beside(result_hbm.at[pl.ds((1 - here.k) * half, half)], 1)
    beside.start()
    load_part = load(result_hbm.at[pl.ds(here.k * half, half)], part, 2)
    load_part.start()

    for head in range(heads):
        slot = head % 2
        if head + 1 < heads:
            for copy in head_loads[head + 1]:
                copy.start()
        for copy in head_loads[head]:
            copy.wait()

        @pl.loop(0, rows // length)
        def _(sequence):
            where = pl.ds(pl.multiple_of(sequence * length, length), length)
            query_pre = saved[slot, where, 0:LANES]
            key_pre = saved[slot, where, LANES : 2 * LANES]
            gate = saved[slot, where, 2 * LANES : 3 * LANES]
            scale = inverse[where, :]
            unit = saved[slot, where, 3 * LANES : 4 * LANES] * scale
            grad_branch = dots(grad_out[where, :], weights[slot, :, 4 * LANES :], 1, 0)
            grad_unit = grad_branch * gate
            branch[where, :] = (unit * gate).astype(bf16)
            projected[where, 3 * LANES :] = (grad_branch * unit).astype(bf16)
            grad_mixed = (scale * (grad_unit - unit * dot_sum[where, :])).astype(bf16)
            query_gate = 1.0 / (1.0 + jnp.exp(-query_pre))
            key_gate = 1.0 / (1.0 + jnp.exp(-key_pre))
            queries = (query_pre * query_gate).astype(bf16)
            keys = (key_pre * key_gate).astype(bf16)
            masked = table[head] * same[sequence]
            mixing = (dots(queries, keys, 1, 1) * masked).astype(bf16)
            grad_scores = (
                dots(grad_mixed, values[slot, where, :], 1, 1) * masked
            ).astype(bf16)
            grad_queries = dots(grad_scores, keys, 1, 0)
            grad_keys = dots(grad_scores, queries, 0, 0)
            projected[where, 0:LANES] = (
                grad_queries * (query_gate * (1.0 + query_pre * (1.0 - query_gate)))
            ).astype(bf16)
            projected[where, LANES : 2 * LANES] = (
                grad_keys * (key_gate * (1.0 + key_pre * (1.0 - key_gate)))
            ).astype(bf16)
            projected[where, 2 * LANES : 3 * LANES] = dots(mixing, grad_mixed, 0, 0).astype(bf16)
            product = dots(projected[where, :], weights[slot, :, : 4 * LANES], 1, 1)
            if head == 0:
                total[where, :] = product
            else:
                total[where, :] += product

        flush(0)
        flush(1)
        reducer.tick()

        @pl.loop(0, width // per_block)
        def _(block):
            where = pl.ds(pl.multiple_of(block * per_block, per_block), per_block)
            product = dots(normed[:, where], projected[...], 0, 0)
            store_block(0, block, 0, product[:, : 3 * LANES])
            store_block(1, block, 0, product[:, 3 * LANES :])
            store_block(1, block, LANES, dots(grad_out[:, where], branch[...], 0, 0))

        pending[0] = stage_out(0, p_qkv.at[head])
        pending[1] = stage_out(1, p_go.at[head])
        pending[0].start()
        pending[1].start()
        if head == heads - 1:
            beside.wait_send()

            @row_loop(half)
            def _(index):
                part[at_rows(0, index), :] = total[
                    at_rows((1 - here.k) * half, index), :
                ].astype(bf16)

            pl.semaphore_wait(free.at[0], 1)
            beside = swap_beside(part, 2)
            beside.start()
        flush(0)
        flush(1)
        if head == 0:
            load_part.wait()
            beside.wait_recv()
            leave, keep = reduce_beside(
                lambda base, index: part[at_rows(base, index), :].astype(f32)
            )
            for crossing in crossings:
                crossing.wait_send()
            crossings = [swap_across(batch, 1) for batch in range(2)]
            for batch in range(2):
                leave(batch)
                crossings[batch].start()
            for batch in range(2):
                keep(batch)
            pl.semaphore_signal(free.at[0], inc=1, device_id=sibling, device_id_type=MESH)
        if head == 2:
            for crossing in crossings:
                crossing.wait_recv()
                crossing.wait_send()

            @row_loop(2 * part_rows)
            def _(index):
                here_rows = at_rows(0, index)
                value = kept[here_rows, :] + across_in[here_rows, :].astype(f32)
                across[here_rows, :] = (middle[here_rows, :] + value).astype(bf16)

            store_result = load(across, result, 12)
            store_result.start()
            pl.semaphore_signal(free.at[1], inc=1, device_id=other, device_id_type=MESH)
        if head % 2 == 1:
            reducer.tick()

    beside.wait_recv()
    leave, keep = reduce_beside(
        lambda base, index: total[at_rows(here.k * half + base, index), :]
    )
    crossings = [swap_across(batch, 2) for batch in range(2)]
    store_result.wait()
    pl.semaphore_wait(free.at[1], 1)
    for batch in range(2):
        leave(batch)
        crossings[batch].start()
    for batch in range(2):
        keep(batch)
    reducer.tick()
    for batch in range(2):
        crossings[batch].wait_recv()

        @row_loop(part_rows)
        def _(index):
            here_rows = at_rows(batch * part_rows, index)
            grad = kept[here_rows, :] + across_in[here_rows, :].astype(f32)
            value = tokens[here_rows, :].astype(f32)
            scale = lax.rsqrt(jnp.mean(value * value, axis=-1, keepdims=True) + EPSILON)
            unit = value * scale
            weighted = grad * unit
            columns[0] += weighted[:8] + weighted[8:]
            scaled = grad * gains[0:1, :]
            grad_tokens[here_rows, :] = grad_middle[here_rows, :] + scale * (
                scaled - unit * jnp.mean(scaled * unit, axis=-1, keepdims=True)
            )

    lane = lax.broadcasted_iota(jnp.int32, (8, LANES), 1)

    @pl.loop(0, width // per_block)
    def _(block):
        where = pl.ds(pl.multiple_of(block * per_block, per_block), per_block)
        first = jnp.where(lane == 0, 1.0, 0.0).astype(bf16)
        second = jnp.where(lane == 1, 1.0, 0.0).astype(bf16)
        value = dots(columns[0, :, where].astype(bf16), first, 0, 0)
        value += dots(columns[1, :, where].astype(bf16), second, 0, 0)
        store_block(0, block, 0, value)

    pending[0] = stage_out(0, p_gain.at[0])
    pending[0].start()
    flush(0)
    reducer.drain()
    beside.wait_send()
    for crossing in crossings:
        crossing.wait_send()
    rows_go.finish()
    rows_dot.finish()


def backward(mids, small, large):
    f32, bf16 = jnp.float32, jnp.bfloat16
    shape = jax.ShapeDtypeStruct
    rates, onehot, gains, inverse, tokens, middle, cotangent = small
    normed_ffn, upstream, normed, act, partial, result, saved, values, weights = large
    rows, width = normed.shape
    heads, units = saved.shape[0], act.shape[0]
    block_rows = width // (LAYERS * mids * CORES)
    widths = ((units, 3 * LANES), (heads, 3 * LANES), (heads, 2 * LANES), (1, LANES))
    chunks = sum(count for count, _ in widths)
    hops = mids + (LAYERS - 1) * CORES
    anywhere = pl.BlockSpec(memory_space=pl.ANY)
    vmem = pl.BlockSpec(memory_space=pltpu.VMEM)
    smem = pl.BlockSpec(memory_space=pltpu.SMEM)
    widest = 3 * LANES
    half, own = rows // CORES, rows // (2 * CORES)
    length = own
    outs = [shape((count, CORES, block_rows, wide), f32) for count, wide in widths]
    sums = [shape((count, LAYERS, mids, CORES, block_rows, wide), bf16) for count, wide in widths]
    cross = [
        shape((count, mids - 1, LAYERS, CORES, block_rows, wide), bf16) for count, wide in widths
    ]
    land = [shape((count, CORES, LAYERS, block_rows, wide), bf16) for count, wide in widths]
    return pl.pallas_call(
        functools.partial(backward_kernel, mids),
        name="backward",
        out_shape=(*outs, shape((own, width), f32), shape((own, width), bf16), *sums, *cross, *land),
        in_specs=[smem] + [vmem] * 6 + [anywhere] * 9,
        out_specs=(anywhere,) * 4 + (vmem,) + (anywhere,) * 13,
        scratch_shapes=[
            pltpu.VMEM((rows, width), bf16),
            pltpu.VMEM((rows, width), bf16),
            pltpu.VMEM((rows, width), bf16),
            pltpu.VMEM((2, rows, widest), bf16),
            pltpu.VMEM((2, LAYERS, mids, CORES, block_rows, widest), bf16),
            pltpu.VMEM((2, LAYERS, CORES, block_rows, widest), bf16),
            pltpu.VMEM((2, mids - 1, LAYERS, CORES, block_rows, widest), bf16),
            pltpu.VMEM((SUMS, LAYERS, CORES, block_rows, widest), bf16),
            pltpu.VMEM((2, CORES, LAYERS, block_rows, widest), bf16),
            pltpu.VMEM((2, CORES, block_rows, widest), f32),
            pltpu.VMEM((2, rows, 4 * LANES), f32),
            pltpu.VMEM((2, rows, LANES), bf16),
            pltpu.VMEM((2, width, 5 * LANES), bf16),
            pltpu.VMEM((rows, 4 * LANES), bf16),
            pltpu.VMEM((rows, LANES), bf16),
            pltpu.VMEM((rows, width), f32),
            pltpu.VMEM((half, width), bf16),
            pltpu.VMEM((half, width), bf16),
            pltpu.VMEM((own, width), bf16),
            pltpu.VMEM((own, width), bf16),
            pltpu.VMEM((own, width), f32),
            pltpu.VMEM((own, width), f32),
            pltpu.VMEM((rows, LANES), f32),
            pltpu.VMEM((heads, length, length), f32),
            pltpu.VMEM((rows // length, length, length), f32),
            pltpu.VMEM((2, 8, width), f32),
            pltpu.SemaphoreType.DMA((chunks, hops)),
            pltpu.SemaphoreType.DMA((chunks, hops)),
            pltpu.SemaphoreType.DMA((chunks, 5)),
            pltpu.SemaphoreType.DMA((21,)),
            pltpu.SemaphoreType.DMA((21,)),
            pltpu.SemaphoreType.DMA((13,)),
            pltpu.SemaphoreType.DMA((2,)),
            pltpu.SemaphoreType.REGULAR((2,)),
        ],
        compiler_params=pltpu.CompilerParams(
            collective_id=1, has_side_effects=True, vmem_limit_bytes=63 * 2**20
        ),
    )(*small, *large)[:6]


class Gatherer:
    def __init__(self, chunks):
        self.chunks = chunks
        self.started = self.crossed = 0

    def launch(self):
        while self.started < min(len(self.chunks), self.crossed + AHEAD + 1):
            self.chunks[self.started].start()
            self.started += 1

    def cross(self, count=1):
        for _ in range(count):
            if self.crossed < len(self.chunks):
                self.chunks[self.crossed].cross()
                self.crossed += 1
                self.launch()

    def arrive(self, at):
        self.cross(at + 1 - self.crossed)
        self.chunks[at].arrive()


def forward_kernel(mids, *refs):
    f32, bf16 = jnp.float32, jnp.bfloat16
    (
        rates,
        own_marks,
        tokens,
        cotangent,
        shard_g,
        shard_a,
        shard_f,
        full_g,
        full_a,
        full_f,
        normed_hbm,
        normed_ffn_hbm,
        upstream_hbm,
        act_hbm,
        partial_hbm,
        result_hbm,
        saved_hbm,
        values_hbm,
        marks,
        gains,
        inverse,
        middle,
        normed,
        normed_ffn,
        upstream,
        total,
        grad_total,
        weights,
        out_weights,
        saved,
        values,
        act,
        branch,
        part,
        part_in,
        across,
        across_in,
        kept,
        squares,
        squares_in,
        squares_across,
        squares_across_in,
        table,
        same,
        gain_columns,
        send,
        receive,
        local,
        row_send,
        row_receive,
        load_sem,
        store_sem,
    ) = refs
    rows, width = normed.shape
    half = rows // CORES
    part_rows = half // 4
    length = 2 * part_rows
    heads, units = full_a.shape[0], full_f.shape[0]
    here = Place(mids)
    sibling = here.device(here.z, here.m, 1 - here.k)
    other = (here.device(here.z, here.m, here.k)[0], 1 - here.t)
    greet(here.weight_peers() + [other])

    chunks = []
    for source, target in ((shard_g, full_g), (shard_a, full_a), (shard_f, full_f)):
        for index in range(source.shape[0]):
            at = len(chunks)
            chunks.append(
                Gather(
                    here,
                    source.at[index],
                    target.at[index],
                    (send.at[at], receive.at[at], local.at[at]),
                )
            )
    gatherer = Gatherer(chunks)
    gatherer.launch()

    step_rows = 16

    def row_loop(count):
        return pl.loop(0, count // step_rows)

    def at_rows(base, index):
        return pl.ds(pl.multiple_of(base + index * step_rows, step_rows), step_rows)

    def spread(buffer, at):
        window = pl.ds(6 * at, 6)
        return Spread(here, buffer, part_rows, row_send.at[window], row_receive.at[window])

    rows_normed, rows_up = spread(normed, 0), spread(upstream, 1)
    rows_ffn, rows_inverse = spread(normed_ffn, 2), spread(inverse, 3)
    lone = lambda source, target, at, peer: remote(
        source, target, row_send.at[24 + at], row_receive.at[24 + at], peer
    )

    own_half = pl.ds(pl.multiple_of(here.k * half, half), half)
    far_half = pl.ds(pl.multiple_of((1 - here.k) * half, half), half)
    marks[own_half, :] = own_marks[...]
    marks_copy = lone(own_marks, marks.at[own_half], 0, sibling)
    marks_copy.start()

    gatherer.arrive(0)
    load_gain = pltpu.make_async_copy(full_g.at[0], gain_columns, load_sem.at[0])
    load_gain.start()
    load_gain.wait()
    down = lax.broadcasted_iota(jnp.int32, (8, LANES), 0)
    right = lax.broadcasted_iota(jnp.int32, (8, LANES), 1)
    pick = jnp.where(down == right, 1.0, 0.0).astype(bf16)
    gains[...] = dots(pick, gain_columns[...].reshape(width, LANES), 1, 1)

    for batch in range(2):
        base = here.row(here.k, batch, here.t, part_rows)

        @row_loop(part_rows)
        def _(index):
            here_rows = at_rows(batch * part_rows, index)
            value = tokens[here_rows, :].astype(f32)
            scale = lax.rsqrt(jnp.mean(value * value, axis=-1, keepdims=True) + EPSILON)
            normed[at_rows(base, index), :] = (value * scale * gains[0:1, :]).astype(bf16)

        rows_normed.start(batch)
    for batch in range(2):
        base = here.row(here.k, batch, here.t, part_rows)
        upstream[pl.ds(base, part_rows), :] = cotangent[pl.ds(batch * part_rows, part_rows), :]
        rows_up.start(batch)

    down = lax.broadcasted_iota(jnp.int32, (length, length), 0)
    right = lax.broadcasted_iota(jnp.int32, (length, length), 1)
    offset = (down - right).astype(f32)
    for head in range(heads):
        decay = jnp.exp(-rates[head] * jnp.maximum(offset, 0.0))
        table[head] = jnp.where(down >= right, decay, 0.0)
    marks_copy.wait_recv()
    for sequence in range(rows // length):
        mark = marks[pl.ds(sequence * length, length), :]
        same[sequence] = dots(mark, mark, 1, 1)
    squares[...] = jnp.zeros_like(squares)

    def weight(slot, first, last):
        return weights[slot, :, :, :, :, first * LANES : last * LANES].reshape(
            width, (last - first) * LANES
        )

    def store(source, target, at):
        copy = pltpu.make_async_copy(source, target, store_sem.at[at])
        copy.start()
        return copy

    stores = []
    gatherer.cross()
    rows_normed.forward()
    rows_normed.arrive()
    stores.append(store(normed, normed_hbm, 0))
    gatherer.cross()
    rows_up.forward()

    pending = [[], []]
    for head in range(heads):
        slot = head % 2
        gatherer.arrive(1 + head)
        load = pltpu.make_async_copy(full_a.at[head], weights.at[slot], load_sem.at[slot])
        load_out = pltpu.make_async_copy(
            full_a.at[head, :, :, :, :, pl.ds(4 * LANES, LANES)],
            out_weights.at[:, :, :, :, pl.ds(head * LANES, LANES)],
            load_sem.at[2 + head],
        )
        load.start()
        load_out.start()
        for copy in pending[slot]:
            copy.wait()
        load.wait()

        @pl.loop(0, rows // length)
        def _(sequence):
            where = pl.ds(pl.multiple_of(sequence * length, length), length)
            product = dots(normed[where, :], weight(slot, 0, 4), 1, 0)
            query_pre, key_pre = product[:, :LANES], product[:, LANES : 2 * LANES]
            value = product[:, 2 * LANES : 3 * LANES].astype(bf16)
            gate = product[:, 3 * LANES :]
            queries = (query_pre / (1.0 + jnp.exp(-query_pre))).astype(bf16)
            keys = (key_pre / (1.0 + jnp.exp(-key_pre))).astype(bf16)
            masked = table[head] * same[sequence]
            mixing = (dots(queries, keys, 1, 1) * masked).astype(bf16)
            mixed = dots(mixing, value, 1, 0)
            saved[slot, where, : 2 * LANES] = product[:, : 2 * LANES]
            saved[slot, where, 2 * LANES : 3 * LANES] = gate
            saved[slot, where, 3 * LANES :] = mixed
            values[slot, where, :] = value
            branch[where, head * LANES : (head + 1) * LANES] = (mixed * gate).astype(bf16)
            squares[where, :] += jnp.broadcast_to(
                jnp.sum(mixed * mixed, axis=-1, keepdims=True), (length, LANES)
            )

        pending[slot] = [
            store(saved.at[slot], saved_hbm.at[head], 4 + slot),
            store(values.at[slot], values_hbm.at[head], 6 + slot),
        ]
        load_out.wait()
        gatherer.cross()
    stores += pending[0] + pending[1]

    @pl.loop(0, half // length)
    def _(block):
        base = (1 - here.k) * half + block * length
        where = pl.ds(pl.multiple_of(base, length), length)
        to = pl.ds(pl.multiple_of(block * length, length), length)
        part[to, :] = dots(branch[where, :], out_weights[...].reshape(width, -1), 1, 1).astype(bf16)

    beside = lone(part, part_in, 1, sibling)
    beside.start()
    beside_squares = lone(squares.at[far_half], squares_in, 2, sibling)
    beside_squares.start()

    @pl.loop(0, half // length)
    def _(block):
        base = here.k * half + block * length
        where = pl.ds(pl.multiple_of(base, length), length)
        total[where, :] = dots(branch[where, :], out_weights[...].reshape(width, -1), 1, 1)

    beside.wait_recv()
    beside_squares.wait_recv()
    crossings = []
    for batch in range(2):
        block = pl.ds(batch * part_rows, part_rows)
        crossings.append(
            (
                lone(across.at[block], across_in.at[block], 3 + batch, other),
                lone(squares_across.at[block], squares_across_in.at[block], 5 + batch, other),
            )
        )

        @row_loop(part_rows)
        def _(index):
            base = batch * length + (1 - here.t) * part_rows
            value = total[at_rows(here.k * half + base, index), :]
            value += part_in[at_rows(base, index), :].astype(f32)
            to = at_rows(batch * part_rows, index)
            across[to, :] = value.astype(bf16)
            squares_across[to, :] = (
                squares[at_rows(here.k * half + base, index), :]
                + squares_in[at_rows(base, index), :]
            )

        for copy in crossings[batch]:
            copy.start()
    for batch in range(2):

        @row_loop(part_rows)
        def _(index):
            base = batch * length + here.t * part_rows
            value = total[at_rows(here.k * half + base, index), :]
            to = at_rows(batch * part_rows, index)
            kept[to, :] = value + part_in[at_rows(base, index), :].astype(f32)

    gatherer.cross()
    rows_up.arrive()
    stores.append(store(upstream, upstream_hbm, 1))
    for batch in range(2):
        for copy in crossings[batch]:
            copy.wait_recv()
        base = here.row(here.k, batch, here.t, part_rows)

        @row_loop(part_rows)
        def _(index):
            here_rows = at_rows(batch * part_rows, index)
            from_rows = batch * length + here.t * part_rows
            square = (
                squares[at_rows(here.k * half + from_rows, index), :]
                + squares_in[at_rows(from_rows, index), :]
                + squares_across_in[here_rows, :]
            )
            scale = lax.rsqrt(square / width + EPSILON)
            inverse[at_rows(base, index), :] = scale
            attended = (kept[here_rows, :] + across_in[here_rows, :].astype(f32)) * scale[:, :1]
            mid = tokens[here_rows, :].astype(f32) + attended
            middle[here_rows, :] = mid
            scale = lax.rsqrt(jnp.mean(mid * mid, axis=-1, keepdims=True) + EPSILON)
            normed_ffn[at_rows(base, index), :] = (mid * scale * gains[1:2, :]).astype(bf16)

        rows_ffn.start(batch)
        rows_inverse.start(batch)
    gatherer.cross()
    rows_ffn.forward()
    rows_inverse.forward()
    gatherer.cross()
    rows_ffn.arrive()
    rows_inverse.arrive()
    stores.append(store(normed_ffn, normed_ffn_hbm, 2))

    pending = [None, None]
    for at in range(units):
        slot = at % 2
        gatherer.arrive(1 + heads + at)
        load = pltpu.make_async_copy(
            full_f.at[at], weights.at[slot, :, :, :, :, pl.ds(0, 3 * LANES)], load_sem.at[slot]
        )
        load.start()
        if pending[slot] is not None:
            pending[slot].wait()
        gatherer.cross()
        load.wait()

        @pl.loop(0, rows // length)
        def _(block):
            where = pl.ds(pl.multiple_of(block * length, length), length)
            product = dots(normed_ffn[where, :], weight(slot, 0, 2), 1, 0)
            left, right = product[:, :LANES], product[:, LANES:]
            grad_joined = dots(upstream[where, :], weight(slot, 2, 3), 1, 0)
            act[slot, where, :LANES] = (grad_joined * right).astype(bf16)
            act[slot, where, LANES : 2 * LANES] = (grad_joined * left).astype(bf16)
            act[slot, where, 2 * LANES :] = (left * right).astype(bf16)
            out = dots(act[slot, where, 2 * LANES :], weight(slot, 2, 3), 1, 1)
            grad = dots(act[slot, where, : 2 * LANES], weight(slot, 0, 2), 1, 1)
            if at == 0:
                total[where, :] = out
                grad_total[where, :] = grad
            else:
                total[where, :] += out
                grad_total[where, :] += grad

        pending[slot] = store(act.at[slot], act_hbm.at[at], 8 + slot)

    for copy in stores:
        copy.wait()
    rows_normed.finish()
    rows_ffn.finish()

    @row_loop(rows)
    def _(index):
        normed[at_rows(0, index), :] = grad_total[at_rows(0, index), :].astype(bf16)

    grads = store(normed, partial_hbm, 0)

    @row_loop(rows)
    def _(index):
        normed_ffn[at_rows(0, index), :] = total[at_rows(0, index), :].astype(bf16)

    outs = store(normed_ffn, result_hbm, 1)
    for copy in pending + [grads, outs]:
        copy.wait()
    for chunk in chunks:
        chunk.finish()
    rows_up.finish()
    rows_inverse.finish()
    marks_copy.wait_send()
    beside.wait_send()
    beside_squares.wait_send()
    for pair in crossings:
        for copy in pair:
            copy.wait_send()


def forward(mids, rates, marks, tokens, cotangent, shards):
    f32, bf16 = jnp.float32, jnp.bfloat16
    shape = jax.ShapeDtypeStruct
    own, width = tokens.shape
    rows, half = 4 * own, 2 * own
    length = own
    heads, units = shards[1].shape[0], shards[2].shape[0]
    block_rows = shards[0].shape[2]
    full = [shape((w.shape[0], LAYERS, mids) + w.shape[1:], bf16) for w in shards]
    chunks = 1 + heads + units
    hops = 1 + (LAYERS - 1) * CORES + mids - 1
    anywhere = pl.BlockSpec(memory_space=pl.ANY)
    vmem = pl.BlockSpec(memory_space=pltpu.VMEM)
    smem = pl.BlockSpec(memory_space=pltpu.SMEM)
    block = (LAYERS, mids, CORES, block_rows)
    return pl.pallas_call(
        functools.partial(forward_kernel, mids),
        name="forward",
        out_shape=(
            *full,
            *[shape((rows, width), bf16)] * 3,
            shape((units, rows, 3 * LANES), bf16),
            *[shape((rows, width), bf16)] * 2,
            shape((heads, rows, 4 * LANES), f32),
            shape((heads, rows, LANES), bf16),
            shape((rows, LANES), bf16),
            shape((8, width), f32),
            shape((rows, LANES), f32),
            shape((own, width), f32),
        ),
        in_specs=[smem] + [vmem] * 3 + [anywhere] * 3,
        out_specs=(anywhere,) * 11 + (vmem,) * 4,
        scratch_shapes=[
            pltpu.VMEM((rows, width), bf16),
            pltpu.VMEM((rows, width), bf16),
            pltpu.VMEM((rows, width), bf16),
            pltpu.VMEM((rows, width), f32),
            pltpu.VMEM((rows, width), f32),
            pltpu.VMEM((2, *block, 5 * LANES), bf16),
            pltpu.VMEM((*block, heads * LANES), bf16),
            pltpu.VMEM((2, rows, 4 * LANES), f32),
            pltpu.VMEM((2, rows, LANES), bf16),
            pltpu.VMEM((2, rows, 3 * LANES), bf16),
            pltpu.VMEM((rows, heads * LANES), bf16),
            pltpu.VMEM((half, width), bf16),
            pltpu.VMEM((half, width), bf16),
            pltpu.VMEM((own, width), bf16),
            pltpu.VMEM((own, width), bf16),
            pltpu.VMEM((own, width), f32),
            pltpu.VMEM((rows, LANES), f32),
            pltpu.VMEM((half, LANES), f32),
            pltpu.VMEM((own, LANES), f32),
            pltpu.VMEM((own, LANES), f32),
            pltpu.VMEM((heads, length, length), f32),
            pltpu.VMEM((rows // length, length, length), f32),
            pltpu.VMEM((*block, LANES), bf16),
            pltpu.SemaphoreType.DMA((chunks, hops)),
            pltpu.SemaphoreType.DMA((chunks, hops)),
            pltpu.SemaphoreType.DMA((chunks,)),
            pltpu.SemaphoreType.DMA((31,)),
            pltpu.SemaphoreType.DMA((31,)),
            pltpu.SemaphoreType.DMA((2 + heads,)),
            pltpu.SemaphoreType.DMA((10,)),
        ],
        compiler_params=pltpu.CompilerParams(
            collective_id=0, has_side_effects=True, vmem_limit_bytes=63 * 2**20
        ),
    )(rates, marks, tokens, cotangent, *shards)


def split_heads(weight, halves):
    return weight.reshape(weight.shape[0], CORES, -1, LANES)


def pack(parts):
    joined = jnp.concatenate([split_heads(part, CORES) for part in parts], axis=-1)
    return joined.transpose(2, 1, 0, 3)


def unpack(packed):
    blocks, cores, rows, width = packed.shape
    parts = packed.reshape(blocks, cores, rows, width // LANES, LANES).transpose(3, 2, 1, 0, 4)
    return [parts[index].reshape(rows, -1) for index in range(width // LANES)]


def local(
    mids,
    tokens,
    segment_ids,
    decay_rates,
    gain_attn,
    w_query,
    w_key,
    w_value,
    w_gate,
    w_out,
    gain_ffn,
    w_left,
    w_right,
    w_down,
    cotangent,
):
    f32, bf16 = jnp.float32, jnp.bfloat16
    batches, local_rows, model_width = tokens.shape
    core = lax.rem(lax.axis_index("dp"), CORES)
    heads = decay_rates.shape[0] // CORES
    rates = lax.dynamic_slice_in_dim(decay_rates, core * heads, heads)
    own = lambda values: values.reshape(batches * local_rows, model_width)
    marks = (segment_ids.reshape(-1)[:, None] == jnp.arange(LANES)[None, :]).astype(bf16)
    gain_columns = jnp.pad(
        jnp.stack([gain_attn, gain_ffn], axis=1), ((0, 0), (0, LANES - 2))
    )
    shards = (
        jnp.stack([gain_columns] * CORES)[None],
        pack([w_query, w_key, w_value, w_gate, w_out.T]),
        pack([w_left, w_right, w_down.T]),
    )
    (
        _,
        full_a,
        _,
        normed,
        normed_ffn,
        upstream,
        act,
        partial,
        result,
        saved,
        values,
        marks,
        gains,
        inverse,
        middle,
    ) = forward(mids, rates, marks, own(tokens), own(cotangent), shards)
    full_a = full_a.reshape(heads, model_width, -1)
    of, oqkv, ogo, ogain, grad_tokens, result = backward(
        mids,
        (rates, marks, gains, inverse, own(tokens), middle, own(cotangent)),
        (normed_ffn, upstream, normed, act, partial, result, saved, values, full_a),
    )
    result = result.reshape(tokens.shape)
    grad_tokens = grad_tokens.reshape(tokens.shape)
    grad_gains = lax.psum(jnp.sum(ogain[0], axis=0)[:, :2], "tensor").T
    oa = jnp.concatenate([oqkv, ogo], axis=-1)
    grad_query, grad_key, grad_value, grad_gate_proj, grad_out = unpack(oa)
    grad_w_left, grad_w_right, grad_down = unpack(of)
    return (
        result,
        grad_tokens,
        grad_gains[0],
        grad_query,
        grad_key,
        grad_value,
        grad_gate_proj,
        grad_out.T,
        grad_gains[1],
        grad_w_left,
        grad_w_right,
        grad_down.T,
    )


def solution(mesh):
    return jax.shard_map(
        functools.partial(local, mesh.shape["dp"] // (LAYERS * CORES)),
        mesh=mesh,
        in_specs=(
            P(None, ("dp", "tensor"), None),
            P(None, "dp"),
            P("tensor"),
            P("dp"),
            P("dp", "tensor"),
            P("dp", "tensor"),
            P("dp", "tensor"),
            P("dp", "tensor"),
            P("tensor", "dp"),
            P("dp"),
            P("dp", "tensor"),
            P("dp", "tensor"),
            P("tensor", "dp"),
            P(None, ("dp", "tensor"), None),
        ),
        out_specs=(
            P(None, ("dp", "tensor"), None),
            P(None, ("dp", "tensor"), None),
            P("dp"),
            P("dp", "tensor"),
            P("dp", "tensor"),
            P("dp", "tensor"),
            P("dp", "tensor"),
            P("tensor", "dp"),
            P("dp"),
            P("dp", "tensor"),
            P("dp", "tensor"),
            P("tensor", "dp"),
        ),
        check_vma=False,
    )
```

```python
import functools

import jax
import jax.numpy as jnp
from jax import lax
from jax.experimental import pallas as pl
from jax.experimental.pallas import tpu as pltpu
from jax.sharding import PartitionSpec as P

EPSILON = 1e-06
LAYERS = 4
CORES = 2
LANES = 128
AHEAD = 1
BEFORE = 3
LEAD = 2
BEHIND = 2
SUMS = 3
FETCH = 2
MESH = pl.DeviceIdType.MESH


class Place:
    def __init__(self, mids):
        place = lax.axis_index("dp")
        self.mids = mids
        self.t = lax.axis_index("tensor")
        self.k = lax.rem(place, CORES)
        self.m = lax.rem(lax.div(place, CORES), mids)
        self.z = lax.div(place, CORES * mids)

    def device(self, z, m, k):
        return ((z * self.mids + m) * CORES + k, self.t)

    def layer(self, step):
        return lax.rem(self.z + step, LAYERS)

    def mid(self, step):
        return lax.rem(self.m + step, self.mids)

    def row(self, core, batch, half, part):
        return pl.multiple_of(((core * 2 + batch) * 2 + half) * part, part)

    def weight_peers(self):
        peers = [self.device(self.z, self.m, 1 - self.k)]
        for step in range(1, LAYERS):
            for core in range(CORES):
                peers.append(self.device(self.layer(step), self.m, core))
        for step in range(1, self.mids):
            for core in range(CORES):
                peers.append(self.device(self.z, self.mid(step), core))
        return peers


def greet(peers):
    barrier = pltpu.get_barrier_semaphore()
    for peer in peers:
        pl.semaphore_signal(barrier, inc=1, device_id=peer, device_id_type=MESH)
    pl.semaphore_wait(barrier, len(peers))


def remote(source, target, send, receive, peer):
    return pltpu.make_async_remote_copy(
        src_ref=source,
        dst_ref=target,
        send_sem=send,
        recv_sem=receive,
        device_id=peer,
        device_id_type=MESH,
    )


def apart(one, layer):
    near = jnp.logical_and(one - layer <= 2, layer - one <= 2)
    return jnp.logical_and(one != layer, near)


def relayed(here, layer):
    first, last = layer == 0, layer == LAYERS - 1
    if not (first or last):
        return None, None
    return (here == LAYERS - 2, LAYERS - 1) if first else (here == 1, 0)


class Gather:
    def __init__(self, place, source, target, sems):
        self.place, self.source, self.target = place, source, target
        self.send, self.receive, self.local = sems
        here = place
        self.own = target.at[here.z, here.m, here.k]
        self.keep = pltpu.make_async_copy(source.at[here.k], self.own, self.local)
        self.beside = remote(
            source.at[1 - here.k],
            self.own,
            self.send.at[0],
            self.receive.at[0],
            here.device(here.z, here.m, 1 - here.k),
        )
        self.sides = 1 + LAYERS * CORES
        self.crosses = self.sides + (here.mids - 1) * CORES

    @staticmethod
    def semaphores(mids):
        return 1 + LAYERS * CORES + (mids - 1) * (CORES + LAYERS)

    def hop(self, layer, core, origin):
        here = self.place
        arrival = 1 + (here.z * CORES + here.k if origin is None else origin * CORES + core)
        return remote(
            self.source.at[core],
            self.own,
            self.send.at[1 + layer * CORES + core],
            self.receive.at[arrival],
            here.device(layer, here.m, core),
        )

    def pass_on(self, layer, core, goal):
        here = self.place
        block = self.target.at[layer, here.m, core]
        return remote(
            block,
            block,
            self.send.at[1 + here.z * CORES + core],
            self.receive.at[1 + layer * CORES + core],
            here.device(goal, here.m, here.k),
        )

    def side(self, step, core, wait):
        here = self.place
        at = self.sides + (step - 1) * CORES
        return remote(
            self.source.at[core],
            self.own,
            self.send.at[at + core],
            self.receive.at[at + (core if wait else here.k)],
            here.device(here.z, here.mid(step), core),
        )

    def crossing(self, step, layer):
        here = self.place
        at = self.crosses + (step - 1) * LAYERS + layer
        block = self.target.at[layer, here.m]
        return remote(
            block,
            block,
            self.send.at[at],
            self.receive.at[at],
            here.device(here.z, here.mid(step), here.k),
        )

    def start(self):
        here = self.place
        self.keep.start()
        self.beside.start()
        for step in range(1, here.mids):
            for core in range(CORES):
                self.side(step, core, False).start()
        for layer in range(LAYERS):

            @pl.when(apart(here.z, layer))
            def _():
                for core in range(CORES):
                    self.hop(layer, core, None).start()

    def relay(self):
        for layer in (0, LAYERS - 1):
            mine, goal = relayed(self.place.z, layer)

            @pl.when(mine)
            def _():
                for core in range(CORES):
                    self.hop(layer, core, layer).wait_recv()
                    self.pass_on(layer, core, goal).start()

    def cross(self):
        here = self.place
        for layer in range(LAYERS):
            awaited = here.z != layer
            mine, _ = relayed(here.z, layer)
            if mine is not None:
                awaited = jnp.logical_and(awaited, jnp.logical_not(mine))

            @pl.when(awaited)
            def _():
                for core in range(CORES):
                    self.hop(layer, core, layer).wait_recv()

            @pl.when(here.z != layer)
            def _():
                for step in range(1, here.mids):
                    self.crossing(step, layer).start()

    def arrive(self):
        here = self.place
        self.keep.wait()
        self.beside.wait_recv()
        for step in range(1, here.mids):
            for core in range(CORES):
                self.side(step, core, True).wait_recv()
        for layer in range(LAYERS):

            @pl.when(here.z != layer)
            def _():
                for step in range(1, here.mids):
                    self.crossing(step, layer).wait_recv()

    def finish(self):
        here = self.place
        self.beside.wait_send()
        for step in range(1, here.mids):
            for core in range(CORES):
                self.side(step, core, False).wait_send()
        for layer in range(LAYERS):

            @pl.when(apart(here.z, layer))
            def _():
                for core in range(CORES):
                    self.hop(layer, core, None).wait_send()

            mine, goal = relayed(here.z, layer)
            if mine is not None:

                @pl.when(mine)
                def _():
                    for core in range(CORES):
                        self.pass_on(layer, core, goal).wait_send()

            @pl.when(here.z != layer)
            def _():
                for step in range(1, here.mids):
                    self.crossing(step, layer).wait_send()


class Reduce:
    def __init__(self, place, source, crossed, landed, output, slots, sems):
        self.place, self.source, self.crossed, self.landed = place, source, crossed, landed
        self.output = output
        self.own_slot, self.cross_slot, self.sum_slot, self.land_slot, self.out_slot = slots
        send, receive, local = sems
        here = place
        self.crossings = [
            remote(
                source.at[:, here.mid(step)],
                crossed.at[step - 1],
                send.at[step - 1],
                receive.at[step - 1],
                here.device(here.z, here.mid(step), here.k),
            )
            for step in range(1, here.mids)
        ]
        base = here.mids - 1
        sibling = 1 - here.k
        self.hops = [
            remote(
                self.sum_slot.at[here.z, sibling],
                landed.at[here.k, 0],
                send.at[base],
                receive.at[base],
                here.device(here.z, here.m, sibling),
            )
        ]
        self.arrivals = self.hops[:]
        for step in range(1, LAYERS):
            for core in range(CORES):
                slot = base + 1 + (step - 1) * CORES
                hop = functools.partial(
                    remote,
                    self.sum_slot.at[here.layer(step), core],
                    landed.at[here.k, step],
                    send.at[slot + core],
                    peer=here.device(here.layer(step), here.m, core),
                )
                self.hops.append(hop(receive.at[slot + here.k]))
                self.arrivals.append(hop(receive.at[slot + core]))
        self.keep = pltpu.make_async_copy(
            self.sum_slot.at[here.z, here.k], landed.at[here.k, 0], local.at[0]
        )
        self.load_own = pltpu.make_async_copy(source.at[:, here.m], self.own_slot, local.at[1])
        self.load_cross = pltpu.make_async_copy(crossed, self.cross_slot, local.at[2])
        self.load_land = pltpu.make_async_copy(landed, self.land_slot, local.at[3])
        self.store = pltpu.make_async_copy(self.out_slot, output, local.at[4])

    def start(self):
        for crossing in self.crossings:
            crossing.start()

    def load(self):
        self.load_own.start()
        for crossing in self.crossings:
            crossing.wait_recv()
        self.load_cross.start()

    def add(self):
        self.load_own.wait()
        self.load_cross.wait()

        @pl.loop(0, LAYERS * CORES)
        def _(at):
            layer, core = lax.div(at, CORES), lax.rem(at, CORES)
            total = self.own_slot[layer, core].astype(jnp.float32)
            for step in range(1, self.place.mids):
                total += self.cross_slot[step - 1, layer, core].astype(jnp.float32)
            self.sum_slot[layer, core] = total.astype(jnp.bfloat16)

        self.keep.start()
        for hop in self.hops:
            hop.start()

    def release(self):
        for hop in self.hops:
            hop.wait_send()

    def fetch(self):
        self.keep.wait()
        for hop in self.arrivals:
            hop.wait_recv()
        self.load_land.start()

    def total(self):
        self.load_land.wait()

        @pl.loop(0, CORES)
        def _(core):
            total = self.land_slot[core, 0].astype(jnp.float32)
            for step in range(1, LAYERS):
                total += self.land_slot[core, step].astype(jnp.float32)
            self.out_slot[core] = total

        self.store.start()

    def finish(self):
        for crossing in self.crossings:
            crossing.wait_send()


def dots(left, right, left_axis, right_axis):
    return lax.dot_general(
        left, right, (((left_axis,), (right_axis,)), ((), ())), preferred_element_type=jnp.float32
    )


class Reducer:
    def __init__(self, chunks):
        self.chunks = chunks
        self.ahead = BEHIND
        self.produced = self.started = self.ticks = 0

    def launch(self):
        while self.started < min(self.produced, self.ticks + self.ahead + 1):
            self.chunks[self.started].start()
            self.started += 1

    def produce(self):
        self.produced += 1
        self.launch()

    def tick(self):
        at, chunks = self.ticks, self.chunks
        count, landed = len(chunks), at - FETCH
        if at < count:
            assert at < self.started
            chunks[at].load()
        self.ticks += 1
        self.launch()
        if 0 <= landed:
            chunks[landed].fetch()
        if at < count:
            if at >= SUMS:
                chunks[at - SUMS].release()
            chunks[at].add()
        if 0 <= landed:
            if landed >= 2:
                chunks[landed - 2].store.wait()
            chunks[landed].total()

    def drain(self):
        count = len(self.chunks)
        self.ahead = AHEAD
        while self.ticks < count + FETCH:
            self.tick()
        for chunk in self.chunks[-2:]:
            chunk.store.wait()
        for chunk in self.chunks[-SUMS:]:
            chunk.release()
        for chunk in self.chunks:
            chunk.finish()


class Spread:
    def __init__(self, here, buffer, part, send, receive):
        sibling = here.device(here.z, here.m, 1 - here.k)
        other = (here.device(here.z, here.m, here.k)[0], 1 - here.t)
        self.across, self.beside, self.onward = [], [], []
        for batch in range(2):
            own = buffer.at[pl.ds(here.row(here.k, batch, here.t, part), part)]
            theirs = buffer.at[pl.ds(here.row(here.k, batch, 1 - here.t, part), part)]
            self.across.append(remote(own, own, send.at[batch], receive.at[batch], other))
            self.beside.append(remote(own, own, send.at[2 + batch], receive.at[2 + batch], sibling))
            self.onward.append(
                remote(theirs, theirs, send.at[4 + batch], receive.at[4 + batch], sibling)
            )

    def start(self, batch):
        self.across[batch].start()
        self.beside[batch].start()

    def forward(self):
        for batch in range(2):
            self.across[batch].wait_recv()
            self.onward[batch].start()

    def arrive(self):
        for copy in self.beside + self.onward:
            copy.wait_recv()

    def finish(self):
        for copy in self.across + self.beside + self.onward:
            copy.wait_send()


def backward_kernel(mids, *refs):
    f32, bf16 = jnp.float32, jnp.bfloat16
    (
        rates,
        onehot,
        gains,
        inverse,
        tokens,
        middle,
        cotangent,
        normed_ffn_hbm,
        upstream_hbm,
        normed_hbm,
        act_hbm,
        partial_hbm,
        result_hbm,
        saved_hbm,
        values_hbm,
        weights_hbm,
        weights_go_hbm,
        out_f,
        out_qkv,
        out_go,
        out_gain,
        grad_tokens,
        result,
        p_f,
        p_qkv,
        p_go,
        p_gain,
        *rest,
    ) = refs
    crossed, landed, rest = rest[:4], rest[4:8], rest[8:]
    (
        normed,
        upstream,
        grad_out,
        act,
        stage,
        own_slot,
        cross_slot,
        sum_slot,
        land_slot,
        out_slot,
        saved,
        values,
        weights,
        projected,
        branch,
        total,
        part,
        part_in,
        across,
        across_in,
        kept,
        grad_middle,
        dot_sum,
        table,
        same,
        columns,
        send,
        receive,
        local,
        row_send,
        row_receive,
        load_sem,
        stage_sem,
        free,
    ) = rest
    rows, width = normed.shape
    half = rows // CORES
    part_rows = half // 4
    length = 2 * part_rows
    heads, units = saved_hbm.shape[0], act_hbm.shape[0]
    here = Place(mids)
    sibling = here.device(here.z, here.m, 1 - here.k)
    other = (here.device(here.z, here.m, here.k)[0], 1 - here.t)
    greet(here.weight_peers() + [other])

    chunks = []
    lists = [(p_f, index, 0, out_f, act.shape[-1]) for index in range(units)]
    for index in range(heads):
        lists.append((p_qkv, index, 1, out_qkv, 3 * LANES))
        lists.append((p_go, index, 2, out_go, 2 * LANES))
    lists.append((p_gain, 0, 3, out_gain, LANES))
    for at, (source, index, kind, output, wide) in enumerate(lists):
        slots = [
            slot.at[(at % slot.shape[0],) + (slice(None),) * (len(slot.shape) - 2) + (pl.ds(0, wide),)]
            for slot in (own_slot, cross_slot, sum_slot, land_slot, out_slot)
        ]
        chunks.append(
            Reduce(
                here,
                source.at[index],
                crossed[kind].at[index],
                landed[kind].at[index],
                output.at[index],
                slots,
                (send.at[at], receive.at[at], local.at[at]),
            )
        )
    reducer = Reducer(chunks)

    def load(source, target, at):
        return pltpu.make_async_copy(source, target, load_sem.at[at])

    loads = {
        "normed_ffn": load(normed_ffn_hbm, normed, 0),
        "upstream": load(upstream_hbm, upstream, 1),
        "part": load(partial_hbm.at[pl.ds(here.k * half, half)], part, 2),
        "normed": load(normed_hbm, normed, 3),
    }
    acts = [load(act_hbm.at[at], act.at[at % 2], 4 + at % 2) for at in range(units)]
    head_loads = [
        (
            load(saved_hbm.at[at], saved.at[at % 2], 6 + at % 2),
            load(values_hbm.at[at], values.at[at % 2], 8 + at % 2),
            load(weights_hbm.at[at], weights.at[at % 2, :, pl.ds(0, 3 * LANES)], 10 + at % 2),
            load(
                weights_go_hbm.at[at],
                weights.at[at % 2, :, pl.ds(3 * LANES, 2 * LANES)],
                13 + at % 2,
            ),
        )
        for at in range(heads)
    ]
    loads["normed_ffn"].start()
    acts[0].start()
    loads["upstream"].start()
    loads["part"].start()

    def swap_beside(source, at):
        return remote(source, part_in, row_send.at[12 + at], row_receive.at[12 + at], sibling)

    def swap_across(batch, at):
        block = pl.ds(batch * part_rows, part_rows)
        return remote(
            across.at[block],
            across_in.at[block],
            row_send.at[15 + 2 * at + batch],
            row_receive.at[15 + 2 * at + batch],
            other,
        )

    beside = swap_beside(partial_hbm.at[pl.ds((1 - here.k) * half, half)], 0)
    beside.start()

    down = lax.broadcasted_iota(jnp.int32, (length, length), 0)
    right = lax.broadcasted_iota(jnp.int32, (length, length), 1)
    offset = (down - right).astype(f32)
    for head in range(heads):
        decay = jnp.exp(-rates[head] * jnp.maximum(offset, 0.0))
        table[head] = jnp.where(down >= right, decay, 0.0)
    for sequence in range(rows // length):
        marks = onehot[pl.ds(sequence * length, length), :]
        same[sequence] = dots(marks, marks, 1, 1)

    per_block = 2 * LANES
    group = per_block // (CORES * p_f.shape[4])
    turns = mids // group

    def store_block(slot, at, first, value):
        layer, chip = lax.div(at, turns), lax.rem(at, turns) * group
        shaped = value.astype(bf16).reshape(group, CORES, p_f.shape[4], value.shape[-1])
        stage[slot, layer, pl.ds(chip, group), :, :, pl.ds(first, value.shape[-1])] = shaped

    def stage_out(slot, target):
        wide = target.shape[-1]
        return pltpu.make_async_copy(
            stage.at[slot, :, :, :, :, pl.ds(0, wide)], target, stage_sem.at[slot]
        )

    pending = [None, None]

    def flush(slot):
        if pending[slot] is not None:
            pending[slot].wait()
            pending[slot] = None
            reducer.produce()

    def unit_chunk(at):
        slot = at % 2
        if at + 1 < units:
            acts[at + 1].start()
        acts[at].wait()
        flush(slot)

        @pl.loop(0, width // per_block)
        def _(block):
            where = pl.ds(pl.multiple_of(block * per_block, per_block), per_block)
            store_block(slot, block, 0, dots(normed[:, where], act[slot, :, : 2 * LANES], 0, 0))
            store_block(
                slot, block, 2 * LANES, dots(upstream[:, where], act[slot, :, 2 * LANES :], 0, 0)
            )

        flush(1 - slot)
        pending[slot] = stage_out(slot, p_f.at[at])
        pending[slot].start()

    step_rows = 16

    def row_loop(count):
        return pl.loop(0, count // step_rows)

    def at_rows(base, index):
        return pl.ds(pl.multiple_of(base + index * step_rows, step_rows), step_rows)

    def reduce_beside(own):
        def leave(batch):
            @row_loop(part_rows)
            def _(index):
                base = batch * length + (1 - here.t) * part_rows
                value = own(base, index) + part_in[at_rows(base, index), :].astype(f32)
                across[at_rows(batch * part_rows, index), :] = value.astype(bf16)

        def keep(batch):
            @row_loop(part_rows)
            def _(index):
                base = batch * length + here.t * part_rows
                value = own(base, index) + part_in[at_rows(base, index), :].astype(f32)
                kept[at_rows(batch * part_rows, index), :] = value

        return leave, keep

    loads["normed_ffn"].wait()
    loads["upstream"].wait()
    unit_chunk(0)
    unit_chunk(1)
    loads["part"].wait()
    beside.wait_recv()
    leave, keep = reduce_beside(lambda base, index: part[at_rows(base, index), :].astype(f32))
    crossings = [swap_across(batch, 0) for batch in range(2)]
    for batch in range(2):
        leave(batch)
        crossings[batch].start()
    for batch in range(2):
        keep(batch)
    for at in range(2, 6):
        unit_chunk(at)
        if at % 2 == 1:
            reducer.tick()
    columns[...] = jnp.zeros_like(columns)
    rows_go = Spread(here, grad_out, part_rows, row_send.at[pl.ds(0, 6)], row_receive.at[pl.ds(0, 6)])
    rows_dot = Spread(here, dot_sum, part_rows, row_send.at[pl.ds(6, 6)], row_receive.at[pl.ds(6, 6)])

    for batch in range(2):
        crossings[batch].wait_recv()
        base = here.row(here.k, batch, here.t, part_rows)

        @row_loop(part_rows)
        def _(index):
            here_rows = at_rows(batch * part_rows, index)
            grad = kept[here_rows, :] + across_in[here_rows, :].astype(f32)
            mid = middle[here_rows, :]
            scale = lax.rsqrt(jnp.mean(mid * mid, axis=-1, keepdims=True) + EPSILON)
            unit = mid * scale
            weighted = grad * unit
            columns[1] += weighted[:8] + weighted[8:]
            scaled = grad * gains[1:2, :]
            slope = cotangent[here_rows, :].astype(f32) + scale * (
                scaled - unit * jnp.mean(scaled * unit, axis=-1, keepdims=True)
            )
            grad_middle[here_rows, :] = slope
            rounded = slope.astype(bf16)
            grad_out[at_rows(base, index), :] = rounded
            attended = mid - tokens[here_rows, :].astype(f32)
            inner = jnp.mean(rounded.astype(f32) * attended, axis=-1, keepdims=True)
            dot_sum[at_rows(base, index), :] = jnp.broadcast_to(inner, (step_rows, LANES))

        rows_go.start(batch)
        rows_dot.start(batch)
    for at in range(6, 9):
        unit_chunk(at)
        if at == 7:
            reducer.tick()
    rows_go.forward()
    rows_dot.forward()
    for at in range(9, units):
        unit_chunk(at)
    for copy in head_loads[0]:
        copy.start()
    loads["normed"].start()
    reducer.tick()
    rows_go.arrive()
    rows_dot.arrive()
    loads["normed"].wait()
    beside.wait_send()
    beside = swap_beside(result_hbm.at[pl.ds((1 - here.k) * half, half)], 1)
    beside.start()
    load_part = load(result_hbm.at[pl.ds(here.k * half, half)], part, 2)
    load_part.start()

    for head in range(heads):
        slot = head % 2
        if head + 1 < heads:
            for copy in head_loads[head + 1]:
                copy.start()
        for copy in head_loads[head]:
            copy.wait()

        @pl.loop(0, rows // length)
        def _(sequence):
            where = pl.ds(pl.multiple_of(sequence * length, length), length)
            query_pre = saved[slot, where, 0:LANES]
            key_pre = saved[slot, where, LANES : 2 * LANES]
            gate = saved[slot, where, 2 * LANES : 3 * LANES]
            scale = inverse[where, :]
            unit = saved[slot, where, 3 * LANES : 4 * LANES] * scale
            grad_branch = dots(grad_out[where, :], weights[slot, :, 4 * LANES :], 1, 0)
            grad_unit = grad_branch * gate
            branch[where, :] = (unit * gate).astype(bf16)
            projected[where, 3 * LANES :] = (grad_branch * unit).astype(bf16)
            grad_mixed = (scale * (grad_unit - unit * dot_sum[where, :])).astype(bf16)
            query_gate = 1.0 / (1.0 + jnp.exp(-query_pre))
            key_gate = 1.0 / (1.0 + jnp.exp(-key_pre))
            queries = (query_pre * query_gate).astype(bf16)
            keys = (key_pre * key_gate).astype(bf16)
            masked = table[head] * same[sequence]
            mixing = (dots(queries, keys, 1, 1) * masked).astype(bf16)
            grad_scores = (
                dots(grad_mixed, values[slot, where, :], 1, 1) * masked
            ).astype(bf16)
            grad_queries = dots(grad_scores, keys, 1, 0)
            grad_keys = dots(grad_scores, queries, 0, 0)
            projected[where, 0:LANES] = (
                grad_queries * (query_gate * (1.0 + query_pre * (1.0 - query_gate)))
            ).astype(bf16)
            projected[where, LANES : 2 * LANES] = (
                grad_keys * (key_gate * (1.0 + key_pre * (1.0 - key_gate)))
            ).astype(bf16)
            projected[where, 2 * LANES : 3 * LANES] = dots(mixing, grad_mixed, 0, 0).astype(bf16)
            product = dots(projected[where, :], weights[slot, :, : 4 * LANES], 1, 1)
            if head == 0:
                total[where, :] = product
            else:
                total[where, :] += product

        flush(0)
        flush(1)
        reducer.tick()

        @pl.loop(0, width // per_block)
        def _(block):
            where = pl.ds(pl.multiple_of(block * per_block, per_block), per_block)
            product = dots(normed[:, where], projected[...], 0, 0)
            store_block(0, block, 0, product[:, : 3 * LANES])
            store_block(1, block, 0, product[:, 3 * LANES :])
            store_block(1, block, LANES, dots(grad_out[:, where], branch[...], 0, 0))

        pending[0] = stage_out(0, p_qkv.at[head])
        pending[1] = stage_out(1, p_go.at[head])
        pending[0].start()
        pending[1].start()
        if head == heads - 1:
            beside.wait_send()

            @row_loop(half)
            def _(index):
                part[at_rows(0, index), :] = total[
                    at_rows((1 - here.k) * half, index), :
                ].astype(bf16)

            pl.semaphore_wait(free.at[0], 1)
            beside = swap_beside(part, 2)
            beside.start()
        flush(0)
        flush(1)
        if head == 0:
            load_part.wait()
            beside.wait_recv()
            leave, keep = reduce_beside(
                lambda base, index: part[at_rows(base, index), :].astype(f32)
            )
            for crossing in crossings:
                crossing.wait_send()
            crossings = [swap_across(batch, 1) for batch in range(2)]
            for batch in range(2):
                leave(batch)
                crossings[batch].start()
            for batch in range(2):
                keep(batch)
            pl.semaphore_signal(free.at[0], inc=1, device_id=sibling, device_id_type=MESH)
        if head == 2:
            for crossing in crossings:
                crossing.wait_recv()
                crossing.wait_send()

            @row_loop(2 * part_rows)
            def _(index):
                here_rows = at_rows(0, index)
                value = kept[here_rows, :] + across_in[here_rows, :].astype(f32)
                across[here_rows, :] = (middle[here_rows, :] + value).astype(bf16)

            store_result = load(across, result, 12)
            store_result.start()
            pl.semaphore_signal(free.at[1], inc=1, device_id=other, device_id_type=MESH)
        reducer.tick()

    beside.wait_recv()
    leave, keep = reduce_beside(
        lambda base, index: total[at_rows(here.k * half + base, index), :]
    )
    crossings = [swap_across(batch, 2) for batch in range(2)]
    store_result.wait()
    pl.semaphore_wait(free.at[1], 1)
    for batch in range(2):
        leave(batch)
        crossings[batch].start()
    for batch in range(2):
        keep(batch)
    reducer.tick()
    for batch in range(2):
        crossings[batch].wait_recv()

        @row_loop(part_rows)
        def _(index):
            here_rows = at_rows(batch * part_rows, index)
            grad = kept[here_rows, :] + across_in[here_rows, :].astype(f32)
            value = tokens[here_rows, :].astype(f32)
            scale = lax.rsqrt(jnp.mean(value * value, axis=-1, keepdims=True) + EPSILON)
            unit = value * scale
            weighted = grad * unit
            columns[0] += weighted[:8] + weighted[8:]
            scaled = grad * gains[0:1, :]
            grad_tokens[here_rows, :] = grad_middle[here_rows, :] + scale * (
                scaled - unit * jnp.mean(scaled * unit, axis=-1, keepdims=True)
            )

    lane = lax.broadcasted_iota(jnp.int32, (8, LANES), 1)

    @pl.loop(0, width // per_block)
    def _(block):
        where = pl.ds(pl.multiple_of(block * per_block, per_block), per_block)
        first = jnp.where(lane == 0, 1.0, 0.0).astype(bf16)
        second = jnp.where(lane == 1, 1.0, 0.0).astype(bf16)
        value = dots(columns[0, :, where].astype(bf16), first, 0, 0)
        value += dots(columns[1, :, where].astype(bf16), second, 0, 0)
        store_block(0, block, 0, value)

    pending[0] = stage_out(0, p_gain.at[0])
    pending[0].start()
    flush(0)
    reducer.drain()
    beside.wait_send()
    for crossing in crossings:
        crossing.wait_send()
    rows_go.finish()
    rows_dot.finish()


def backward(mids, small, large):
    f32, bf16 = jnp.float32, jnp.bfloat16
    shape = jax.ShapeDtypeStruct
    rates, onehot, gains, inverse, tokens, middle, cotangent = small
    normed_ffn, upstream, normed, act, partial, result, saved, values, weights, weights_go = large
    rows, width = normed.shape
    heads, units = saved.shape[0], act.shape[0]
    block_rows = width // (LAYERS * mids * CORES)
    widths = ((units, 3 * LANES), (heads, 3 * LANES), (heads, 2 * LANES), (1, LANES))
    chunks = sum(count for count, _ in widths)
    hops = mids + (LAYERS - 1) * CORES
    anywhere = pl.BlockSpec(memory_space=pl.ANY)
    vmem = pl.BlockSpec(memory_space=pltpu.VMEM)
    smem = pl.BlockSpec(memory_space=pltpu.SMEM)
    widest = 3 * LANES
    half, own = rows // CORES, rows // (2 * CORES)
    length = own
    outs = [shape((count, CORES, block_rows, wide), f32) for count, wide in widths]
    sums = [shape((count, LAYERS, mids, CORES, block_rows, wide), bf16) for count, wide in widths]
    cross = [
        shape((count, mids - 1, LAYERS, CORES, block_rows, wide), bf16) for count, wide in widths
    ]
    land = [shape((count, CORES, LAYERS, block_rows, wide), bf16) for count, wide in widths]
    return pl.pallas_call(
        functools.partial(backward_kernel, mids),
        name="backward",
        out_shape=(*outs, shape((own, width), f32), shape((own, width), bf16), *sums, *cross, *land),
        in_specs=[smem] + [vmem] * 6 + [anywhere] * 10,
        out_specs=(anywhere,) * 4 + (vmem,) + (anywhere,) * 13,
        scratch_shapes=[
            pltpu.VMEM((rows, width), bf16),
            pltpu.VMEM((rows, width), bf16),
            pltpu.VMEM((rows, width), bf16),
            pltpu.VMEM((2, rows, widest), bf16),
            pltpu.VMEM((2, LAYERS, mids, CORES, block_rows, widest), bf16),
            pltpu.VMEM((1, LAYERS, CORES, block_rows, widest), bf16),
            pltpu.VMEM((1, mids - 1, LAYERS, CORES, block_rows, widest), bf16),
            pltpu.VMEM((SUMS, LAYERS, CORES, block_rows, widest), bf16),
            pltpu.VMEM((1, CORES, LAYERS, block_rows, widest), bf16),
            pltpu.VMEM((2, CORES, block_rows, widest), f32),
            pltpu.VMEM((2, rows, 4 * LANES), f32),
            pltpu.VMEM((2, rows, LANES), bf16),
            pltpu.VMEM((2, width, 5 * LANES), bf16),
            pltpu.VMEM((rows, 4 * LANES), bf16),
            pltpu.VMEM((rows, LANES), bf16),
            pltpu.VMEM((rows, width), f32),
            pltpu.VMEM((half, width), bf16),
            pltpu.VMEM((half, width), bf16),
            pltpu.VMEM((own, width), bf16),
            pltpu.VMEM((own, width), bf16),
            pltpu.VMEM((own, width), f32),
            pltpu.VMEM((own, width), f32),
            pltpu.VMEM((rows, LANES), f32),
            pltpu.VMEM((heads, length, length), f32),
            pltpu.VMEM((rows // length, length, length), f32),
            pltpu.VMEM((2, 8, width), f32),
            pltpu.SemaphoreType.DMA((chunks, hops)),
            pltpu.SemaphoreType.DMA((chunks, hops)),
            pltpu.SemaphoreType.DMA((chunks, 5)),
            pltpu.SemaphoreType.DMA((21,)),
            pltpu.SemaphoreType.DMA((21,)),
            pltpu.SemaphoreType.DMA((15,)),
            pltpu.SemaphoreType.DMA((2,)),
            pltpu.SemaphoreType.REGULAR((2,)),
        ],
        compiler_params=pltpu.CompilerParams(
            collective_id=1, has_side_effects=True, vmem_limit_bytes=63 * 2**20
        ),
    )(*small, *large)[:6]


class Gatherer:
    def __init__(self, chunks):
        self.chunks = chunks
        self.started = self.crossed = self.passed = 0

    def relay(self, at):
        if at < len(self.chunks) and self.passed == at:
            self.chunks[at].relay()
            self.passed += 1

    def launch(self):
        while self.started < min(len(self.chunks), self.crossed + BEFORE + 1):
            self.chunks[self.started].start()
            self.started += 1

    def cross(self, count=1):
        for _ in range(count):
            if self.crossed < len(self.chunks):
                self.relay(self.crossed)
                self.chunks[self.crossed].cross()
                self.crossed += 1
                self.launch()
                self.relay(self.crossed)

    def arrive(self, at):
        self.cross(at + 1 - self.crossed)
        self.chunks[at].arrive()


def forward_kernel(mids, *refs):
    f32, bf16 = jnp.float32, jnp.bfloat16
    (
        rates,
        own_marks,
        tokens,
        cotangent,
        shard_g,
        shard_go,
        shard_qkv,
        shard_f,
        full_g,
        full_go,
        full_qkv,
        full_f,
        normed_hbm,
        normed_ffn_hbm,
        upstream_hbm,
        act_hbm,
        partial_hbm,
        result_hbm,
        saved_hbm,
        values_hbm,
        marks,
        gains,
        inverse,
        middle,
        normed,
        normed_ffn,
        upstream,
        total,
        grad_total,
        weights,
        out_weights,
        saved,
        values,
        act,
        branch,
        part,
        part_in,
        across,
        across_in,
        kept,
        squares,
        squares_in,
        squares_across,
        squares_across_in,
        table,
        same,
        gain_columns,
        send,
        receive,
        local,
        row_send,
        row_receive,
        load_sem,
        store_sem,
    ) = refs
    rows, width = normed.shape
    half = rows // CORES
    part_rows = half // 4
    length = 2 * part_rows
    heads, units = full_qkv.shape[0], full_f.shape[0]
    here = Place(mids)
    sibling = here.device(here.z, here.m, 1 - here.k)
    other = (here.device(here.z, here.m, here.k)[0], 1 - here.t)
    greet(here.weight_peers() + [other])

    chunks = []
    pairs = [(shard_g, full_g, 0)]
    for index in range(heads):
        pairs += [(shard_go, full_go, index), (shard_qkv, full_qkv, index)]
    pairs += [(shard_f, full_f, index) for index in range(units)]
    for at, (source, target, index) in enumerate(pairs):
        chunks.append(
            Gather(
                here,
                source.at[index],
                target.at[index],
                (send.at[at], receive.at[at], local.at[at]),
            )
        )
    gatherer = Gatherer(chunks)
    gatherer.launch()

    step_rows = 16

    def row_loop(count):
        return pl.loop(0, count // step_rows)

    def at_rows(base, index):
        return pl.ds(pl.multiple_of(base + index * step_rows, step_rows), step_rows)

    def spread(buffer, at):
        window = pl.ds(6 * at, 6)
        return Spread(here, buffer, part_rows, row_send.at[window], row_receive.at[window])

    rows_normed, rows_up = spread(normed, 0), spread(upstream, 1)
    rows_ffn, rows_inverse = spread(normed_ffn, 2), spread(inverse, 3)
    lone = lambda source, target, at, peer: remote(
        source, target, row_send.at[24 + at], row_receive.at[24 + at], peer
    )

    own_half = pl.ds(pl.multiple_of(here.k * half, half), half)
    far_half = pl.ds(pl.multiple_of((1 - here.k) * half, half), half)
    marks[own_half, :] = own_marks[...]
    marks_copy = lone(own_marks, marks.at[own_half], 0, sibling)
    marks_copy.start()

    gatherer.arrive(0)
    load_gain = pltpu.make_async_copy(full_g.at[0], gain_columns, load_sem.at[0])
    load_gain.start()
    load_gain.wait()
    down = lax.broadcasted_iota(jnp.int32, (8, LANES), 0)
    right = lax.broadcasted_iota(jnp.int32, (8, LANES), 1)
    pick = jnp.where(down == right, 1.0, 0.0).astype(bf16)
    gains[...] = dots(pick, gain_columns[...].reshape(width, LANES), 1, 1)

    for batch in range(2):
        base = here.row(here.k, batch, here.t, part_rows)

        @row_loop(part_rows)
        def _(index):
            here_rows = at_rows(batch * part_rows, index)
            value = tokens[here_rows, :].astype(f32)
            scale = lax.rsqrt(jnp.mean(value * value, axis=-1, keepdims=True) + EPSILON)
            normed[at_rows(base, index), :] = (value * scale * gains[0:1, :]).astype(bf16)

        rows_normed.start(batch)
    for batch in range(2):
        base = here.row(here.k, batch, here.t, part_rows)
        upstream[pl.ds(base, part_rows), :] = cotangent[pl.ds(batch * part_rows, part_rows), :]
        rows_up.start(batch)

    down = lax.broadcasted_iota(jnp.int32, (length, length), 0)
    right = lax.broadcasted_iota(jnp.int32, (length, length), 1)
    offset = (down - right).astype(f32)
    for head in range(heads):
        decay = jnp.exp(-rates[head] * jnp.maximum(offset, 0.0))
        table[head] = jnp.where(down >= right, decay, 0.0)
    marks_copy.wait_recv()
    for sequence in range(rows // length):
        mark = marks[pl.ds(sequence * length, length), :]
        same[sequence] = dots(mark, mark, 1, 1)
    squares[...] = jnp.zeros_like(squares)

    def weight(slot, first, last):
        return weights[slot, :, :, :, :, first * LANES : last * LANES].reshape(
            width, (last - first) * LANES
        )

    def store(source, target, at):
        copy = pltpu.make_async_copy(source, target, store_sem.at[at])
        copy.start()
        return copy

    stores = []
    gatherer.cross()
    rows_normed.forward()
    rows_normed.arrive()
    stores.append(store(normed, normed_hbm, 0))
    gatherer.cross()
    rows_up.forward()

    pending = [[], []]
    for head in range(heads):
        slot = head % 2
        gatherer.cross(3 + 2 * head + LEAD - gatherer.crossed)
        gatherer.arrive(1 + 2 * head)
        load_out = pltpu.make_async_copy(
            full_go.at[head, :, :, :, :, pl.ds(LANES, LANES)],
            out_weights.at[:, :, :, :, pl.ds(head * LANES, LANES)],
            load_sem.at[4 + head],
        )
        load_gate = pltpu.make_async_copy(
            full_go.at[head, :, :, :, :, pl.ds(0, LANES)],
            weights.at[slot, :, :, :, :, pl.ds(3 * LANES, LANES)],
            load_sem.at[2 + slot],
        )
        load_gate.start()
        gatherer.cross(3 + 2 * head + LEAD - gatherer.crossed)
        gatherer.arrive(2 + 2 * head)
        load = pltpu.make_async_copy(
            full_qkv.at[head],
            weights.at[slot, :, :, :, :, pl.ds(0, 3 * LANES)],
            load_sem.at[slot],
        )
        load.start()
        load_out.start()
        for copy in pending[slot]:
            copy.wait()
        load_gate.wait()
        load.wait()

        @pl.loop(0, rows // length)
        def _(sequence):
            where = pl.ds(pl.multiple_of(sequence * length, length), length)
            product = dots(normed[where, :], weight(slot, 0, 4), 1, 0)
            query_pre, key_pre = product[:, :LANES], product[:, LANES : 2 * LANES]
            value = product[:, 2 * LANES : 3 * LANES].astype(bf16)
            gate = product[:, 3 * LANES :]
            queries = (query_pre / (1.0 + jnp.exp(-query_pre))).astype(bf16)
            keys = (key_pre / (1.0 + jnp.exp(-key_pre))).astype(bf16)
            masked = table[head] * same[sequence]
            mixing = (dots(queries, keys, 1, 1) * masked).astype(bf16)
            mixed = dots(mixing, value, 1, 0)
            saved[slot, where, : 2 * LANES] = product[:, : 2 * LANES]
            saved[slot, where, 2 * LANES : 3 * LANES] = gate
            saved[slot, where, 3 * LANES :] = mixed
            values[slot, where, :] = value
            branch[where, head * LANES : (head + 1) * LANES] = (mixed * gate).astype(bf16)
            squares[where, :] += jnp.broadcast_to(
                jnp.sum(mixed * mixed, axis=-1, keepdims=True), (length, LANES)
            )

        pending[slot] = [
            store(saved.at[slot], saved_hbm.at[head], 4 + slot),
            store(values.at[slot], values_hbm.at[head], 6 + slot),
        ]
        load_out.wait()
    stores += pending[0] + pending[1]

    @pl.loop(0, half // length)
    def _(block):
        base = (1 - here.k) * half + block * length
        where = pl.ds(pl.multiple_of(base, length), length)
        to = pl.ds(pl.multiple_of(block * length, length), length)
        part[to, :] = dots(branch[where, :], out_weights[...].reshape(width, -1), 1, 1).astype(bf16)

    beside = lone(part, part_in, 1, sibling)
    beside.start()
    beside_squares = lone(squares.at[far_half], squares_in, 2, sibling)
    beside_squares.start()

    @pl.loop(0, half // length)
    def _(block):
        base = here.k * half + block * length
        where = pl.ds(pl.multiple_of(base, length), length)
        total[where, :] = dots(branch[where, :], out_weights[...].reshape(width, -1), 1, 1)

    beside.wait_recv()
    beside_squares.wait_recv()
    crossings = []
    for batch in range(2):
        block = pl.ds(batch * part_rows, part_rows)
        crossings.append(
            (
                lone(across.at[block], across_in.at[block], 3 + batch, other),
                lone(squares_across.at[block], squares_across_in.at[block], 5 + batch, other),
            )
        )

        @row_loop(part_rows)
        def _(index):
            base = batch * length + (1 - here.t) * part_rows
            value = total[at_rows(here.k * half + base, index), :]
            value += part_in[at_rows(base, index), :].astype(f32)
            to = at_rows(batch * part_rows, index)
            across[to, :] = value.astype(bf16)
            squares_across[to, :] = (
                squares[at_rows(here.k * half + base, index), :]
                + squares_in[at_rows(base, index), :]
            )

        for copy in crossings[batch]:
            copy.start()
    for batch in range(2):

        @row_loop(part_rows)
        def _(index):
            base = batch * length + here.t * part_rows
            value = total[at_rows(here.k * half + base, index), :]
            to = at_rows(batch * part_rows, index)
            kept[to, :] = value + part_in[at_rows(base, index), :].astype(f32)

    gatherer.cross()
    rows_up.arrive()
    stores.append(store(upstream, upstream_hbm, 1))
    for batch in range(2):
        for copy in crossings[batch]:
            copy.wait_recv()
        base = here.row(here.k, batch, here.t, part_rows)

        @row_loop(part_rows)
        def _(index):
            here_rows = at_rows(batch * part_rows, index)
            from_rows = batch * length + here.t * part_rows
            square = (
                squares[at_rows(here.k * half + from_rows, index), :]
                + squares_in[at_rows(from_rows, index), :]
                + squares_across_in[here_rows, :]
            )
            scale = lax.rsqrt(square / width + EPSILON)
            inverse[at_rows(base, index), :] = scale
            attended = (kept[here_rows, :] + across_in[here_rows, :].astype(f32)) * scale[:, :1]
            mid = tokens[here_rows, :].astype(f32) + attended
            middle[here_rows, :] = mid
            scale = lax.rsqrt(jnp.mean(mid * mid, axis=-1, keepdims=True) + EPSILON)
            normed_ffn[at_rows(base, index), :] = (mid * scale * gains[1:2, :]).astype(bf16)

        rows_ffn.start(batch)
        rows_inverse.start(batch)
    gatherer.cross()
    rows_ffn.forward()
    rows_inverse.forward()
    gatherer.cross()
    rows_ffn.arrive()
    rows_inverse.arrive()
    stores.append(store(normed_ffn, normed_ffn_hbm, 2))

    pending = [None, None]
    for at in range(units):
        slot = at % 2
        gatherer.cross(2 + 2 * heads + at + 1 - gatherer.crossed)
        gatherer.arrive(1 + 2 * heads + at)
        load = pltpu.make_async_copy(
            full_f.at[at], weights.at[slot, :, :, :, :, pl.ds(0, 3 * LANES)], load_sem.at[slot]
        )
        load.start()
        if pending[slot] is not None:
            pending[slot].wait()
        gatherer.cross()
        if at == units - 1:
            for copy in stores:
                copy.wait()
            rows_normed.finish()
            rows_ffn.finish()
        load.wait()

        @pl.loop(0, rows // length)
        def _(block):
            where = pl.ds(pl.multiple_of(block * length, length), length)
            product = dots(normed_ffn[where, :], weight(slot, 0, 2), 1, 0)
            left, right = product[:, :LANES], product[:, LANES:]
            grad_joined = dots(upstream[where, :], weight(slot, 2, 3), 1, 0)
            act[slot, where, :LANES] = (grad_joined * right).astype(bf16)
            act[slot, where, LANES : 2 * LANES] = (grad_joined * left).astype(bf16)
            act[slot, where, 2 * LANES :] = (left * right).astype(bf16)
            out = dots(act[slot, where, 2 * LANES :], weight(slot, 2, 3), 1, 1)
            grad = dots(act[slot, where, : 2 * LANES], weight(slot, 0, 2), 1, 1)
            if at == 0:
                total[where, :] = out
                grad_total[where, :] = grad
            elif at == units - 1:
                normed[where, :] = (total[where, :] + out).astype(bf16)
                normed_ffn[where, :] = (grad_total[where, :] + grad).astype(bf16)
            else:
                total[where, :] += out
                grad_total[where, :] += grad

        pending[slot] = store(act.at[slot], act_hbm.at[at], 8 + slot)

    grads = store(normed_ffn, partial_hbm, 0)
    outs = store(normed, result_hbm, 1)
    for copy in pending + [grads, outs]:
        copy.wait()
    for chunk in chunks:
        chunk.finish()
    rows_up.finish()
    rows_inverse.finish()
    marks_copy.wait_send()
    beside.wait_send()
    beside_squares.wait_send()
    for pair in crossings:
        for copy in pair:
            copy.wait_send()


def forward(mids, rates, marks, tokens, cotangent, shards):
    f32, bf16 = jnp.float32, jnp.bfloat16
    shape = jax.ShapeDtypeStruct
    own, width = tokens.shape
    rows, half = 4 * own, 2 * own
    length = own
    heads, units = shards[1].shape[0], shards[3].shape[0]
    block_rows = shards[0].shape[2]
    full = [shape((w.shape[0], LAYERS, mids) + w.shape[1:], bf16) for w in shards]
    chunks = 1 + 2 * heads + units
    hops = Gather.semaphores(mids)
    anywhere = pl.BlockSpec(memory_space=pl.ANY)
    vmem = pl.BlockSpec(memory_space=pltpu.VMEM)
    smem = pl.BlockSpec(memory_space=pltpu.SMEM)
    block = (LAYERS, mids, CORES, block_rows)
    return pl.pallas_call(
        functools.partial(forward_kernel, mids),
        name="forward",
        out_shape=(
            *full,
            *[shape((rows, width), bf16)] * 3,
            shape((units, rows, 3 * LANES), bf16),
            *[shape((rows, width), bf16)] * 2,
            shape((heads, rows, 4 * LANES), f32),
            shape((heads, rows, LANES), bf16),
            shape((rows, LANES), bf16),
            shape((8, width), f32),
            shape((rows, LANES), f32),
            shape((own, width), f32),
        ),
        in_specs=[smem] + [vmem] * 3 + [anywhere] * 4,
        out_specs=(anywhere,) * 12 + (vmem,) * 4,
        scratch_shapes=[
            pltpu.VMEM((rows, width), bf16),
            pltpu.VMEM((rows, width), bf16),
            pltpu.VMEM((rows, width), bf16),
            pltpu.VMEM((rows, width), f32),
            pltpu.VMEM((rows, width), f32),
            pltpu.VMEM((2, *block, 4 * LANES), bf16),
            pltpu.VMEM((*block, heads * LANES), bf16),
            pltpu.VMEM((2, rows, 4 * LANES), f32),
            pltpu.VMEM((2, rows, LANES), bf16),
            pltpu.VMEM((2, rows, 3 * LANES), bf16),
            pltpu.VMEM((rows, heads * LANES), bf16),
            pltpu.VMEM((half, width), bf16),
            pltpu.VMEM((half, width), bf16),
            pltpu.VMEM((own, width), bf16),
            pltpu.VMEM((own, width), bf16),
            pltpu.VMEM((own, width), f32),
            pltpu.VMEM((rows, LANES), f32),
            pltpu.VMEM((half, LANES), f32),
            pltpu.VMEM((own, LANES), f32),
            pltpu.VMEM((own, LANES), f32),
            pltpu.VMEM((heads, length, length), f32),
            pltpu.VMEM((rows // length, length, length), f32),
            pltpu.VMEM((*block, LANES), bf16),
            pltpu.SemaphoreType.DMA((chunks, hops)),
            pltpu.SemaphoreType.DMA((chunks, hops)),
            pltpu.SemaphoreType.DMA((chunks,)),
            pltpu.SemaphoreType.DMA((31,)),
            pltpu.SemaphoreType.DMA((31,)),
            pltpu.SemaphoreType.DMA((4 + heads,)),
            pltpu.SemaphoreType.DMA((10,)),
        ],
        compiler_params=pltpu.CompilerParams(
            collective_id=0, has_side_effects=True, vmem_limit_bytes=63 * 2**20
        ),
    )(rates, marks, tokens, cotangent, *shards)


def split_heads(weight, halves):
    return weight.reshape(weight.shape[0], CORES, -1, LANES)


def pack(parts):
    joined = jnp.concatenate([split_heads(part, CORES) for part in parts], axis=-1)
    return joined.transpose(2, 1, 0, 3)


def unpack(packed):
    blocks, cores, rows, width = packed.shape
    parts = packed.reshape(blocks, cores, rows, width // LANES, LANES).transpose(3, 2, 1, 0, 4)
    return [parts[index].reshape(rows, -1) for index in range(width // LANES)]


def local(
    mids,
    tokens,
    segment_ids,
    decay_rates,
    gain_attn,
    w_query,
    w_key,
    w_value,
    w_gate,
    w_out,
    gain_ffn,
    w_left,
    w_right,
    w_down,
    cotangent,
):
    f32, bf16 = jnp.float32, jnp.bfloat16
    batches, local_rows, model_width = tokens.shape
    core = lax.rem(lax.axis_index("dp"), CORES)
    heads = decay_rates.shape[0] // CORES
    rates = lax.dynamic_slice_in_dim(decay_rates, core * heads, heads)
    own = lambda values: values.reshape(batches * local_rows, model_width)
    marks = (segment_ids.reshape(-1)[:, None] == jnp.arange(LANES)[None, :]).astype(bf16)
    gain_columns = jnp.pad(
        jnp.stack([gain_attn, gain_ffn], axis=1), ((0, 0), (0, LANES - 2))
    )
    shards = (
        jnp.stack([gain_columns] * CORES)[None],
        pack([w_gate, w_out.T]),
        pack([w_query, w_key, w_value]),
        pack([w_left, w_right, w_down.T]),
    )
    (
        _,
        full_go,
        full_qkv,
        _,
        normed,
        normed_ffn,
        upstream,
        act,
        partial,
        result,
        saved,
        values,
        marks,
        gains,
        inverse,
        middle,
    ) = forward(mids, rates, marks, own(tokens), own(cotangent), shards)
    full_go = full_go.reshape(heads, model_width, -1)
    full_qkv = full_qkv.reshape(heads, model_width, -1)
    of, oqkv, ogo, ogain, grad_tokens, result = backward(
        mids,
        (rates, marks, gains, inverse, own(tokens), middle, own(cotangent)),
        (normed_ffn, upstream, normed, act, partial, result, saved, values, full_qkv, full_go),
    )
    result = result.reshape(tokens.shape)
    grad_tokens = grad_tokens.reshape(tokens.shape)
    grad_gains = lax.psum(jnp.sum(ogain[0], axis=0)[:, :2], "tensor").T
    oa = jnp.concatenate([oqkv, ogo], axis=-1)
    grad_query, grad_key, grad_value, grad_gate_proj, grad_out = unpack(oa)
    grad_w_left, grad_w_right, grad_down = unpack(of)
    return (
        result,
        grad_tokens,
        grad_gains[0],
        grad_query,
        grad_key,
        grad_value,
        grad_gate_proj,
        grad_out.T,
        grad_gains[1],
        grad_w_left,
        grad_w_right,
        grad_down.T,
    )


def solution(mesh):
    return jax.shard_map(
        functools.partial(local, mesh.shape["dp"] // (LAYERS * CORES)),
        mesh=mesh,
        in_specs=(
            P(None, ("dp", "tensor"), None),
            P(None, "dp"),
            P("tensor"),
            P("dp"),
            P("dp", "tensor"),
            P("dp", "tensor"),
            P("dp", "tensor"),
            P("dp", "tensor"),
            P("tensor", "dp"),
            P("dp"),
            P("dp", "tensor"),
            P("dp", "tensor"),
            P("tensor", "dp"),
            P(None, ("dp", "tensor"), None),
        ),
        out_specs=(
            P(None, ("dp", "tensor"), None),
            P(None, ("dp", "tensor"), None),
            P("dp"),
            P("dp", "tensor"),
            P("dp", "tensor"),
            P("dp", "tensor"),
            P("dp", "tensor"),
            P("tensor", "dp"),
            P("dp"),
            P("dp", "tensor"),
            P("dp", "tensor"),
            P("tensor", "dp"),
        ),
        check_vma=False,
    )
```

```python
import functools

import jax
import jax.numpy as jnp
from jax import lax
from jax.experimental import pallas as pl
from jax.experimental.pallas import tpu as pltpu
from jax.sharding import PartitionSpec as P

EPSILON = 1e-06
LAYERS = 4
CORES = 2
LANES = 128
AHEAD = 1
BEFORE = 4
LEAD = 3
SIDEWAYS = (9, 13)
BEHIND = 2
SUMS = 4
FETCH = 3
MESH = pl.DeviceIdType.MESH


class Place:
    def __init__(self, mids):
        place = lax.axis_index("dp")
        self.mids = mids
        self.t = lax.axis_index("tensor")
        self.k = lax.rem(place, CORES)
        self.m = lax.rem(lax.div(place, CORES), mids)
        self.z = lax.div(place, CORES * mids)

    def device(self, z, m, k):
        return ((z * self.mids + m) * CORES + k, self.t)

    def layer(self, step):
        return lax.rem(self.z + step, LAYERS)

    def mid(self, step):
        return lax.rem(self.m + step, self.mids)

    def row(self, core, batch, half, part):
        return pl.multiple_of(((core * 2 + batch) * 2 + half) * part, part)

    def weight_peers(self):
        peers = [self.device(self.z, self.m, 1 - self.k)]
        for step in range(1, LAYERS):
            for core in range(CORES):
                peers.append(self.device(self.layer(step), self.m, core))
        for step in range(1, self.mids):
            for core in range(CORES):
                peers.append(self.device(self.z, self.mid(step), core))
        return peers


def greet(peers):
    barrier = pltpu.get_barrier_semaphore()
    for peer in peers:
        pl.semaphore_signal(barrier, inc=1, device_id=peer, device_id_type=MESH)
    pl.semaphore_wait(barrier, len(peers))


def remote(source, target, send, receive, peer):
    return pltpu.make_async_remote_copy(
        src_ref=source,
        dst_ref=target,
        send_sem=send,
        recv_sem=receive,
        device_id=peer,
        device_id_type=MESH,
    )


def apart(one, layer):
    near = jnp.logical_and(one - layer <= 2, layer - one <= 2)
    return jnp.logical_and(one != layer, near)


def relayed(here, layer):
    first, last = layer == 0, layer == LAYERS - 1
    if not (first or last):
        return None, None
    return (here == LAYERS - 2, LAYERS - 1) if first else (here == 1, 0)


class Gather:
    def __init__(self, place, source, target, sems, sideways):
        self.place, self.source, self.target = place, source, target
        self.send, self.receive, self.local = sems
        self.sideways = sideways
        here = place
        self.own = target.at[here.z, here.m, here.k]
        self.keep = pltpu.make_async_copy(source.at[here.k], self.own, self.local)
        self.beside = remote(
            source.at[1 - here.k],
            self.own,
            self.send.at[0],
            self.receive.at[0],
            here.device(here.z, here.m, 1 - here.k),
        )
        self.sides = 1 + LAYERS * CORES
        self.crosses = self.sides + (here.mids - 1) * CORES

    @staticmethod
    def semaphores(mids):
        return 1 + LAYERS * CORES + (mids - 1) * (CORES + LAYERS)

    def hop(self, layer, core, origin):
        here = self.place
        arrival = 1 + (here.z * CORES + here.k if origin is None else origin * CORES + core)
        return remote(
            self.source.at[core],
            self.own,
            self.send.at[1 + layer * CORES + core],
            self.receive.at[arrival],
            here.device(layer, here.m, core),
        )

    def pass_on(self, layer, core, goal):
        here = self.place
        block = self.target.at[layer, here.m, core]
        return remote(
            block,
            block,
            self.send.at[1 + here.z * CORES + core],
            self.receive.at[1 + layer * CORES + core],
            here.device(goal, here.m, here.k),
        )

    def side(self, step, core, wait):
        here = self.place
        at = self.sides + (step - 1) * CORES
        return remote(
            self.source.at[core],
            self.own,
            self.send.at[at + core],
            self.receive.at[at + (core if wait else here.k)],
            here.device(here.z, here.mid(step), core),
        )

    def crossing(self, step, layer):
        here = self.place
        at = self.crosses + (step - 1) * LAYERS + layer
        block = self.target.at[layer, here.m]
        return remote(
            block,
            block,
            self.send.at[at],
            self.receive.at[at],
            here.device(here.z, here.mid(step), here.k),
        )

    def start(self):
        here = self.place
        self.keep.start()
        self.beside.start()
        for step in range(1, here.mids):
            for core in range(CORES):
                self.side(step, core, False).start()
        for layer in range(LAYERS):

            @pl.when(apart(here.z, layer))
            def _():
                for core in range(CORES):
                    self.hop(layer, core, None).start()

    def relay(self):
        for layer in (0, LAYERS - 1):
            mine, goal = relayed(self.place.z, layer)

            @pl.when(mine)
            def _():
                for core in range(CORES):
                    self.hop(layer, core, layer).wait_recv()
                    self.pass_on(layer, core, goal).start()

    def climb(self, step, layer):
        here = self.place
        at = self.crosses + (step - 1) * LAYERS
        block = self.target.at[here.z, here.mid(step)]
        return remote(
            block,
            block,
            self.send.at[at + layer],
            self.receive.at[at + here.z],
            here.device(layer, here.m, here.k),
        )

    def climbed(self, step, layer, goal):
        here = self.place
        at = self.crosses + (step - 1) * LAYERS
        block = self.target.at[layer, here.mid(step)]
        return remote(
            block,
            block,
            self.send.at[at + here.z],
            self.receive.at[at + layer],
            here.device(goal, here.m, here.k),
        )

    def wait_layers(self, then):
        here = self.place
        for layer in range(LAYERS):
            awaited = here.z != layer
            mine, _ = relayed(here.z, layer)
            if mine is not None:
                awaited = jnp.logical_and(awaited, jnp.logical_not(mine))

            @pl.when(awaited)
            def _():
                for core in range(CORES):
                    self.hop(layer, core, layer).wait_recv()

            then(layer)

    def cross(self):
        here = self.place
        if self.sideways:
            for step in range(1, here.mids):
                for core in range(CORES):
                    self.side(step, core, True).wait_recv()
            for layer in range(LAYERS):

                @pl.when(apart(here.z, layer))
                def _():
                    for step in range(1, here.mids):
                        self.climb(step, layer).start()

            return

        def send_on(layer):
            @pl.when(here.z != layer)
            def _():
                for step in range(1, here.mids):
                    self.crossing(step, layer).start()

        self.wait_layers(send_on)

    def relay_on(self):
        if self.sideways:
            here = self.place
            for layer in (0, LAYERS - 1):
                mine, goal = relayed(here.z, layer)

                @pl.when(mine)
                def _():
                    for step in range(1, here.mids):
                        self.climbed(step, layer, goal).wait_recv()
                        self.climbed(step, layer, goal).start()

    def arrive(self):
        here = self.place
        self.keep.wait()
        self.beside.wait_recv()
        if self.sideways:
            self.wait_layers(lambda layer: None)
            for layer in range(LAYERS):
                awaited = here.z != layer
                mine, _ = relayed(here.z, layer)
                if mine is not None:
                    awaited = jnp.logical_and(awaited, jnp.logical_not(mine))

                @pl.when(awaited)
                def _():
                    for step in range(1, here.mids):
                        self.climbed(step, layer, layer).wait_recv()

            return
        for step in range(1, here.mids):
            for core in range(CORES):
                self.side(step, core, True).wait_recv()
        for layer in range(LAYERS):

            @pl.when(here.z != layer)
            def _():
                for step in range(1, here.mids):
                    self.crossing(step, layer).wait_recv()

    def finish(self):
        here = self.place
        self.beside.wait_send()
        for step in range(1, here.mids):
            for core in range(CORES):
                self.side(step, core, False).wait_send()
        for layer in range(LAYERS):

            @pl.when(apart(here.z, layer))
            def _():
                for core in range(CORES):
                    self.hop(layer, core, None).wait_send()
                if self.sideways:
                    for step in range(1, here.mids):
                        self.climb(step, layer).wait_send()

            mine, goal = relayed(here.z, layer)
            if mine is not None:

                @pl.when(mine)
                def _():
                    for core in range(CORES):
                        self.pass_on(layer, core, goal).wait_send()
                    if self.sideways:
                        for step in range(1, here.mids):
                            self.climbed(step, layer, goal).wait_send()

            if not self.sideways:

                @pl.when(here.z != layer)
                def _():
                    for step in range(1, here.mids):
                        self.crossing(step, layer).wait_send()


class Reduce:
    def __init__(self, place, source, crossed, landed, passed, stores, slots, sems):
        self.place, self.source, self.crossed, self.landed = place, source, crossed, landed
        self.passed = passed
        (
            self.own_slot,
            self.cross_slot,
            self.sum_slot,
            self.land_slot,
            self.out_slot,
            self.turn_slot,
            self.pass_slot,
        ) = slots
        self.send, self.receive, local = sems
        here = place
        self.crossings = [
            remote(
                source.at[:, here.mid(step)],
                crossed.at[step - 1],
                self.send.at[step - 1],
                self.receive.at[step - 1],
                here.device(here.z, here.mid(step), here.k),
            )
            for step in range(1, here.mids)
        ]
        self.base = here.mids
        self.beside = remote(
            self.sum_slot.at[here.z, 1 - here.k],
            landed.at[here.k, here.z],
            self.send.at[here.mids - 1],
            self.receive.at[here.mids - 1],
            here.device(here.z, here.m, 1 - here.k),
        )
        self.keep = pltpu.make_async_copy(
            self.sum_slot.at[here.z, here.k], landed.at[here.k, here.z], local.at[0]
        )
        self.load_own = pltpu.make_async_copy(source.at[:, here.m], self.own_slot, local.at[1])
        self.load_cross = pltpu.make_async_copy(crossed, self.cross_slot, local.at[2])
        self.load_land = pltpu.make_async_copy(landed, self.land_slot, local.at[3])
        self.load_pass = pltpu.make_async_copy(passed, self.pass_slot, local.at[4])
        self.turned = self.turn_slot is not None
        self.stores = [
            pltpu.make_async_copy(piece(self.out_slot, self.turn_slot), target, local.at[5 + at])
            for at, (piece, target) in enumerate(stores)
        ]

    @staticmethod
    def semaphores(mids):
        return mids + LAYERS * CORES + 1

    def hop(self, layer, core, origin):
        here = self.place
        arrival = here.z * CORES + here.k if origin is None else origin * CORES + core
        return remote(
            self.sum_slot.at[layer, core],
            self.landed.at[here.k, here.z],
            self.send.at[self.base + layer * CORES + core],
            self.receive.at[self.base + arrival],
            here.device(layer, here.m, core),
        )

    def far(self, layer, goal):
        here = self.place
        at = self.base + LAYERS * CORES
        return remote(
            self.sum_slot.at[layer],
            self.passed,
            self.send.at[at],
            self.receive.at[at],
            here.device(goal, here.m, here.k),
        )

    def ends(self):
        return (
            (self.place.z == 0, LAYERS - 1, LAYERS - 2),
            (self.place.z == LAYERS - 1, 0, 1),
        )

    def start(self):
        for crossing in self.crossings:
            crossing.start()

    def load(self):
        self.load_own.start()
        for crossing in self.crossings:
            crossing.wait_recv()
        self.load_cross.start()

    def add(self):
        here = self.place
        self.load_own.wait()
        self.load_cross.wait()

        @pl.loop(0, LAYERS * CORES)
        def _(at):
            layer, core = lax.div(at, CORES), lax.rem(at, CORES)
            total = self.own_slot[layer, core].astype(jnp.float32)
            for step in range(1, here.mids):
                total += self.cross_slot[step - 1, layer, core].astype(jnp.float32)
            self.sum_slot[layer, core] = total.astype(jnp.bfloat16)

        for end, layer, goal in self.ends():

            @pl.when(end)
            def _():
                self.far(layer, goal).start()

        self.keep.start()
        self.beside.start()
        for layer in range(LAYERS):
            now = apart(here.z, layer)
            if layer in (0, LAYERS - 1):
                now = jnp.logical_and(now, here.z != (1 if layer == 0 else LAYERS - 2))

            @pl.when(now)
            def _():
                for core in range(CORES):
                    self.hop(layer, core, None).start()

    def relay(self):
        for _, layer, goal in self.ends():

            @pl.when(self.place.z == goal)
            def _():
                self.far(layer, goal).wait_recv()
                self.load_pass.start()
                self.load_pass.wait()

                @pl.loop(0, CORES)
                def _(core):
                    total = self.sum_slot[layer, core].astype(jnp.float32)
                    total += self.pass_slot[core].astype(jnp.float32)
                    self.sum_slot[layer, core] = total.astype(jnp.bfloat16)

                for core in range(CORES):
                    self.hop(layer, core, None).start()

    def release(self):
        self.beside.wait_send()
        for layer in range(LAYERS):

            @pl.when(apart(self.place.z, layer))
            def _():
                for core in range(CORES):
                    self.hop(layer, core, None).wait_send()

        for end, layer, goal in self.ends():

            @pl.when(end)
            def _():
                self.far(layer, goal).wait_send()

    def fetch(self):
        self.keep.wait()
        self.beside.wait_recv()
        for layer in range(LAYERS):

            @pl.when(apart(self.place.z, layer))
            def _():
                for core in range(CORES):
                    self.hop(layer, core, layer).wait_recv()

        self.load_land.start()

    def total(self):
        self.load_land.wait()
        here = self.place
        present = [
            jnp.logical_or(here.z == layer, apart(here.z, layer)) for layer in range(LAYERS)
        ]

        @pl.loop(0, CORES)
        def _(core):
            total = None
            for layer in range(LAYERS):
                value = self.land_slot[core, layer].astype(jnp.float32)
                if layer in (0, LAYERS - 1):
                    value = jnp.where(present[layer], value, 0.0)
                total = value if total is None else total + value
            self.out_slot[core] = total
            if self.turned:
                self.turn_slot[core] = total[:, -LANES:].T

        for store in self.stores:
            store.start()

    def stored(self):
        for store in self.stores:
            store.wait()

    def finish(self):
        for crossing in self.crossings:
            crossing.wait_send()


def dots(left, right, left_axis, right_axis):
    return lax.dot_general(
        left, right, (((left_axis,), (right_axis,)), ((), ())), preferred_element_type=jnp.float32
    )


class Reducer:
    def __init__(self, chunks):
        self.chunks = chunks
        self.ahead = BEHIND
        self.produced = self.started = self.ticks = 0

    def launch(self):
        while self.started < min(self.produced, self.ticks + self.ahead + 1):
            self.chunks[self.started].start()
            self.started += 1

    def produce(self):
        self.produced += 1
        self.launch()

    def tick(self):
        at, chunks = self.ticks, self.chunks
        count, passed, landed = len(chunks), at - 1, at - FETCH
        if at < count:
            assert at < self.started
            chunks[at].load()
        self.ticks += 1
        self.launch()
        if 0 <= passed < count:
            chunks[passed].relay()
        if 0 <= landed:
            chunks[landed].fetch()
        if at < count:
            if at >= SUMS:
                chunks[at - SUMS].release()
            chunks[at].add()
        if 0 <= landed:
            if landed >= 2:
                chunks[landed - 2].stored()
            chunks[landed].total()

    def drain(self):
        count = len(self.chunks)
        self.ahead = AHEAD
        while self.ticks < count + FETCH:
            self.tick()
        for chunk in self.chunks[-2:]:
            chunk.stored()
        for chunk in self.chunks[-SUMS:]:
            chunk.release()
        for chunk in self.chunks:
            chunk.finish()


class Spread:
    def __init__(self, here, buffer, part, send, receive):
        sibling = here.device(here.z, here.m, 1 - here.k)
        other = (here.device(here.z, here.m, here.k)[0], 1 - here.t)
        self.across, self.beside, self.onward = [], [], []
        for batch in range(2):
            own = buffer.at[pl.ds(here.row(here.k, batch, here.t, part), part)]
            theirs = buffer.at[pl.ds(here.row(here.k, batch, 1 - here.t, part), part)]
            self.across.append(remote(own, own, send.at[batch], receive.at[batch], other))
            self.beside.append(remote(own, own, send.at[2 + batch], receive.at[2 + batch], sibling))
            self.onward.append(
                remote(theirs, theirs, send.at[4 + batch], receive.at[4 + batch], sibling)
            )

    def start(self, batch):
        self.across[batch].start()
        self.beside[batch].start()

    def forward(self):
        for batch in range(2):
            self.across[batch].wait_recv()
            self.onward[batch].start()

    def arrive(self):
        for copy in self.beside + self.onward:
            copy.wait_recv()

    def finish(self):
        for copy in self.across + self.beside + self.onward:
            copy.wait_send()


def backward_kernel(mids, *refs):
    f32, bf16 = jnp.float32, jnp.bfloat16
    (
        rates,
        onehot,
        gains,
        inverse,
        tokens,
        middle,
        cotangent,
        normed_ffn_hbm,
        upstream_hbm,
        normed_hbm,
        act_hbm,
        partial_hbm,
        result_hbm,
        saved_hbm,
        values_hbm,
        weights_hbm,
        weights_go_hbm,
        out_query,
        out_key,
        out_value,
        out_gate,
        out_out,
        out_left,
        out_right,
        out_down,
        out_gain,
        grad_tokens,
        result,
        p_f,
        p_qkv,
        p_go,
        p_gain,
        *rest,
    ) = refs
    crossed, landed, passed, rest = rest[:4], rest[4:8], rest[8:12], rest[12:]
    (
        normed,
        upstream,
        grad_out,
        act,
        stage,
        own_slot,
        cross_slot,
        sum_slot,
        land_slot,
        out_slot,
        turn_slot,
        pass_slot,
        gain_slot,
        saved,
        values,
        weights,
        projected,
        branch,
        total,
        part,
        part_in,
        across,
        across_in,
        kept,
        grad_middle,
        dot_sum,
        table,
        same,
        columns,
        send,
        receive,
        local,
        row_send,
        row_receive,
        load_sem,
        stage_sem,
        free,
    ) = rest
    rows, width = normed.shape
    half = rows // CORES
    part_rows = half // 4
    length = 2 * part_rows
    heads, units = saved_hbm.shape[0], act_hbm.shape[0]
    here = Place(mids)
    sibling = here.device(here.z, here.m, 1 - here.k)
    other = (here.device(here.z, here.m, here.k)[0], 1 - here.t)
    greet(here.weight_peers() + [other])

    chunks = []
    lists = []

    def columns_of(target, index, count, place):
        for core in range(CORES):
            where = pl.ds((core * count + index) * LANES, LANES)
            yield (
                lambda out, turn, core=core: out.at[core, :, pl.ds(place * LANES, LANES)],
                target.at[:, where],
            )

    def rows_of(target, index, count):
        for core in range(CORES):
            where = pl.ds((core * count + index) * LANES, LANES)
            yield (lambda out, turn, core=core: turn.at[core], target.at[where])

    for index in range(units):
        stores = [
            *columns_of(out_left, index, units, 0),
            *columns_of(out_right, index, units, 1),
            *rows_of(out_down, index, units),
        ]
        lists.append((p_f, index, 0, stores, True))
    for index in range(heads):
        stores = []
        for place, target in enumerate((out_query, out_key, out_value)):
            stores += columns_of(target, index, heads, place)
        lists.append((p_qkv, index, 1, stores, False))
        stores = [*columns_of(out_gate, index, heads, 0), *rows_of(out_out, index, heads)]
        lists.append((p_go, index, 2, stores, True))
    lists.append((p_gain, 0, 3, [], False))
    for at, (source, index, kind, stores, turned) in enumerate(lists):
        wide = source.shape[-1]
        slots = [
            slot.at[(at % slot.shape[0],) + (slice(None),) * (len(slot.shape) - 2) + (pl.ds(0, wide),)]
            for slot in (own_slot, cross_slot, sum_slot, land_slot, out_slot)
        ]
        slots.append(turn_slot.at[at % 2] if turned else None)
        slots.append(pass_slot.at[:, :, pl.ds(0, wide)])
        chunks.append(
            Reduce(
                here,
                source.at[index],
                crossed[kind].at[index],
                landed[kind].at[index],
                passed[kind].at[index],
                stores,
                slots,
                (send.at[at], receive.at[at], local.at[at]),
            )
        )
    reducer = Reducer(chunks)

    def load(source, target, at):
        return pltpu.make_async_copy(source, target, load_sem.at[at])

    loads = {
        "normed_ffn": load(normed_ffn_hbm, normed, 0),
        "upstream": load(upstream_hbm, upstream, 1),
        "part": load(partial_hbm.at[pl.ds(here.k * half, half)], part, 2),
        "normed": load(normed_hbm, normed, 3),
    }
    acts = [load(act_hbm.at[at], act.at[at % 2], 4 + at % 2) for at in range(units)]
    head_loads = [
        (
            load(saved_hbm.at[at], saved.at[at % 2], 6 + at % 2),
            load(values_hbm.at[at], values.at[at % 2], 8 + at % 2),
            load(weights_hbm.at[at], weights.at[at % 2, :, pl.ds(0, 3 * LANES)], 10 + at % 2),
            load(
                weights_go_hbm.at[at],
                weights.at[at % 2, :, pl.ds(3 * LANES, 2 * LANES)],
                13 + at % 2,
            ),
        )
        for at in range(heads)
    ]
    loads["normed_ffn"].start()
    acts[0].start()
    loads["upstream"].start()
    loads["part"].start()

    def swap_beside(source, at):
        return remote(source, part_in, row_send.at[12 + at], row_receive.at[12 + at], sibling)

    def swap_across(batch, at):
        block = pl.ds(batch * part_rows, part_rows)
        return remote(
            across.at[block],
            across_in.at[block],
            row_send.at[15 + 2 * at + batch],
            row_receive.at[15 + 2 * at + batch],
            other,
        )

    beside = swap_beside(partial_hbm.at[pl.ds((1 - here.k) * half, half)], 0)
    beside.start()

    down = lax.broadcasted_iota(jnp.int32, (length, length), 0)
    right = lax.broadcasted_iota(jnp.int32, (length, length), 1)
    offset = (down - right).astype(f32)
    for head in range(heads):
        decay = jnp.exp(-rates[head] * jnp.maximum(offset, 0.0))
        table[head] = jnp.where(down >= right, decay, 0.0)
    for sequence in range(rows // length):
        marks = onehot[pl.ds(sequence * length, length), :]
        same[sequence] = dots(marks, marks, 1, 1)

    per_block = 2 * LANES
    group = per_block // (CORES * p_f.shape[4])
    turns = mids // group

    def store_block(slot, at, first, value):
        layer, chip = lax.div(at, turns), lax.rem(at, turns) * group
        shaped = value.astype(bf16).reshape(group, CORES, p_f.shape[4], value.shape[-1])
        stage[slot, layer, pl.ds(chip, group), :, :, pl.ds(first, value.shape[-1])] = shaped

    def stage_out(slot, target):
        wide = target.shape[-1]
        return pltpu.make_async_copy(
            stage.at[slot, :, :, :, :, pl.ds(0, wide)], target, stage_sem.at[slot]
        )

    pending = [None, None]

    def flush(slot):
        if pending[slot] is not None:
            pending[slot].wait()
            pending[slot] = None
            reducer.produce()

    def unit_chunk(at):
        slot = at % 2
        if at + 1 < units:
            acts[at + 1].start()
        acts[at].wait()
        flush(slot)

        @pl.loop(0, width // per_block)
        def _(block):
            where = pl.ds(pl.multiple_of(block * per_block, per_block), per_block)
            store_block(slot, block, 0, dots(normed[:, where], act[slot, :, : 2 * LANES], 0, 0))
            store_block(
                slot, block, 2 * LANES, dots(upstream[:, where], act[slot, :, 2 * LANES :], 0, 0)
            )

        flush(1 - slot)
        pending[slot] = stage_out(slot, p_f.at[at])
        pending[slot].start()

    step_rows = 16

    def row_loop(count):
        return pl.loop(0, count // step_rows)

    def at_rows(base, index):
        return pl.ds(pl.multiple_of(base + index * step_rows, step_rows), step_rows)

    def reduce_beside(own):
        def leave(batch):
            @row_loop(part_rows)
            def _(index):
                base = batch * length + (1 - here.t) * part_rows
                value = own(base, index) + part_in[at_rows(base, index), :].astype(f32)
                across[at_rows(batch * part_rows, index), :] = value.astype(bf16)

        def keep(batch):
            @row_loop(part_rows)
            def _(index):
                base = batch * length + here.t * part_rows
                value = own(base, index) + part_in[at_rows(base, index), :].astype(f32)
                kept[at_rows(batch * part_rows, index), :] = value

        return leave, keep

    loads["normed_ffn"].wait()
    loads["upstream"].wait()
    unit_chunk(0)
    unit_chunk(1)
    loads["part"].wait()
    beside.wait_recv()
    leave, keep = reduce_beside(lambda base, index: part[at_rows(base, index), :].astype(f32))
    crossings = [swap_across(batch, 0) for batch in range(2)]
    for batch in range(2):
        leave(batch)
        crossings[batch].start()
    for batch in range(2):
        keep(batch)
    for at in range(2, 6):
        unit_chunk(at)
        if at % 2 == 1:
            reducer.tick()
    columns[...] = jnp.zeros_like(columns)
    rows_go = Spread(here, grad_out, part_rows, row_send.at[pl.ds(0, 6)], row_receive.at[pl.ds(0, 6)])
    rows_dot = Spread(here, dot_sum, part_rows, row_send.at[pl.ds(6, 6)], row_receive.at[pl.ds(6, 6)])

    for batch in range(2):
        crossings[batch].wait_recv()
        base = here.row(here.k, batch, here.t, part_rows)

        @row_loop(part_rows)
        def _(index):
            here_rows = at_rows(batch * part_rows, index)
            grad = kept[here_rows, :] + across_in[here_rows, :].astype(f32)
            mid = middle[here_rows, :]
            scale = lax.rsqrt(jnp.mean(mid * mid, axis=-1, keepdims=True) + EPSILON)
            unit = mid * scale
            weighted = grad * unit
            columns[1] += weighted[:8] + weighted[8:]
            scaled = grad * gains[1:2, :]
            slope = cotangent[here_rows, :].astype(f32) + scale * (
                scaled - unit * jnp.mean(scaled * unit, axis=-1, keepdims=True)
            )
            grad_middle[here_rows, :] = slope
            rounded = slope.astype(bf16)
            grad_out[at_rows(base, index), :] = rounded
            attended = mid - tokens[here_rows, :].astype(f32)
            inner = jnp.mean(rounded.astype(f32) * attended, axis=-1, keepdims=True)
            dot_sum[at_rows(base, index), :] = jnp.broadcast_to(inner, (step_rows, LANES))

        rows_go.start(batch)
        rows_dot.start(batch)
    for at in range(6, 9):
        unit_chunk(at)
        if at == 7:
            reducer.tick()
    rows_go.forward()
    rows_dot.forward()
    for at in range(9, units):
        unit_chunk(at)
    for copy in head_loads[0]:
        copy.start()
    loads["normed"].start()
    reducer.tick()
    rows_go.arrive()
    rows_dot.arrive()
    loads["normed"].wait()
    beside.wait_send()
    beside = swap_beside(result_hbm.at[pl.ds((1 - here.k) * half, half)], 1)
    beside.start()
    load_part = load(result_hbm.at[pl.ds(here.k * half, half)], part, 2)
    load_part.start()

    for head in range(heads):
        slot = head % 2
        if head + 1 < heads:
            for copy in head_loads[head + 1]:
                copy.start()
        for copy in head_loads[head]:
            copy.wait()

        @pl.loop(0, rows // length)
        def _(sequence):
            where = pl.ds(pl.multiple_of(sequence * length, length), length)
            query_pre = saved[slot, where, 0:LANES]
            key_pre = saved[slot, where, LANES : 2 * LANES]
            gate = saved[slot, where, 2 * LANES : 3 * LANES]
            scale = inverse[where, :]
            unit = saved[slot, where, 3 * LANES : 4 * LANES] * scale
            grad_branch = dots(grad_out[where, :], weights[slot, :, 4 * LANES :], 1, 0)
            grad_unit = grad_branch * gate
            branch[where, :] = (unit * gate).astype(bf16)
            projected[where, 3 * LANES :] = (grad_branch * unit).astype(bf16)
            grad_mixed = (scale * (grad_unit - unit * dot_sum[where, :])).astype(bf16)
            query_gate = 1.0 / (1.0 + jnp.exp(-query_pre))
            key_gate = 1.0 / (1.0 + jnp.exp(-key_pre))
            queries = (query_pre * query_gate).astype(bf16)
            keys = (key_pre * key_gate).astype(bf16)
            masked = table[head] * same[sequence]
            mixing = (dots(queries, keys, 1, 1) * masked).astype(bf16)
            grad_scores = (
                dots(grad_mixed, values[slot, where, :], 1, 1) * masked
            ).astype(bf16)
            grad_queries = dots(grad_scores, keys, 1, 0)
            grad_keys = dots(grad_scores, queries, 0, 0)
            projected[where, 0:LANES] = (
                grad_queries * (query_gate * (1.0 + query_pre * (1.0 - query_gate)))
            ).astype(bf16)
            projected[where, LANES : 2 * LANES] = (
                grad_keys * (key_gate * (1.0 + key_pre * (1.0 - key_gate)))
            ).astype(bf16)
            projected[where, 2 * LANES : 3 * LANES] = dots(mixing, grad_mixed, 0, 0).astype(bf16)
            product = dots(projected[where, :], weights[slot, :, : 4 * LANES], 1, 1)
            if head == 0:
                total[where, :] = product
            else:
                total[where, :] += product

        flush(0)
        flush(1)
        reducer.tick()

        @pl.loop(0, width // per_block)
        def _(block):
            where = pl.ds(pl.multiple_of(block * per_block, per_block), per_block)
            product = dots(normed[:, where], projected[...], 0, 0)
            store_block(0, block, 0, product[:, : 3 * LANES])
            store_block(1, block, 0, product[:, 3 * LANES :])
            store_block(1, block, LANES, dots(grad_out[:, where], branch[...], 0, 0))

        pending[0] = stage_out(0, p_qkv.at[head])
        pending[1] = stage_out(1, p_go.at[head])
        pending[0].start()
        pending[1].start()
        if head == heads - 1:
            beside.wait_send()

            @row_loop(half)
            def _(index):
                part[at_rows(0, index), :] = total[
                    at_rows((1 - here.k) * half, index), :
                ].astype(bf16)

            pl.semaphore_wait(free.at[0], 1)
            beside = swap_beside(part, 2)
            beside.start()
        flush(0)
        flush(1)
        if head == 0:
            load_part.wait()
            beside.wait_recv()
            leave, keep = reduce_beside(
                lambda base, index: part[at_rows(base, index), :].astype(f32)
            )
            for crossing in crossings:
                crossing.wait_send()
            crossings = [swap_across(batch, 1) for batch in range(2)]
            for batch in range(2):
                leave(batch)
                crossings[batch].start()
            for batch in range(2):
                keep(batch)
            pl.semaphore_signal(free.at[0], inc=1, device_id=sibling, device_id_type=MESH)
        if head == 2:
            for crossing in crossings:
                crossing.wait_recv()
                crossing.wait_send()

            @row_loop(2 * part_rows)
            def _(index):
                here_rows = at_rows(0, index)
                value = kept[here_rows, :] + across_in[here_rows, :].astype(f32)
                across[here_rows, :] = (middle[here_rows, :] + value).astype(bf16)

            store_result = load(across, result, 12)
            store_result.start()
            pl.semaphore_signal(free.at[1], inc=1, device_id=other, device_id_type=MESH)
        reducer.tick()

    beside.wait_recv()
    leave, keep = reduce_beside(
        lambda base, index: total[at_rows(here.k * half + base, index), :]
    )
    crossings = [swap_across(batch, 2) for batch in range(2)]
    store_result.wait()
    pl.semaphore_wait(free.at[1], 1)
    for batch in range(2):
        leave(batch)
        crossings[batch].start()
    for batch in range(2):
        keep(batch)
    reducer.tick()
    for batch in range(2):
        crossings[batch].wait_recv()

        @row_loop(part_rows)
        def _(index):
            here_rows = at_rows(batch * part_rows, index)
            grad = kept[here_rows, :] + across_in[here_rows, :].astype(f32)
            value = tokens[here_rows, :].astype(f32)
            scale = lax.rsqrt(jnp.mean(value * value, axis=-1, keepdims=True) + EPSILON)
            unit = value * scale
            weighted = grad * unit
            columns[0] += weighted[:8] + weighted[8:]
            scaled = grad * gains[0:1, :]
            grad_tokens[here_rows, :] = grad_middle[here_rows, :] + scale * (
                scaled - unit * jnp.mean(scaled * unit, axis=-1, keepdims=True)
            )

    lane = lax.broadcasted_iota(jnp.int32, (8, LANES), 1)

    @pl.loop(0, width // per_block)
    def _(block):
        where = pl.ds(pl.multiple_of(block * per_block, per_block), per_block)
        first = jnp.where(lane == 0, 1.0, 0.0).astype(bf16)
        second = jnp.where(lane == 1, 1.0, 0.0).astype(bf16)
        value = dots(columns[0, :, where].astype(bf16), first, 0, 0)
        value += dots(columns[1, :, where].astype(bf16), second, 0, 0)
        store_block(0, block, 0, value)

    pending[0] = stage_out(0, p_gain.at[0])
    pending[0].start()
    flush(0)
    reducer.drain()
    gain_sum = chunks[-1].out_slot[0] + chunks[-1].out_slot[1]
    gain_slot[0] = gain_sum
    gain_copy = remote(
        gain_slot.at[0], gain_slot.at[1], row_send.at[21], row_receive.at[21], other
    )
    gain_copy.start()
    gain_copy.wait_recv()
    out_gain[...] = (gain_sum + gain_slot[1]).T[:8]
    gain_copy.wait_send()
    beside.wait_send()
    for crossing in crossings:
        crossing.wait_send()
    rows_go.finish()
    rows_dot.finish()


def backward(mids, small, large):
    f32, bf16 = jnp.float32, jnp.bfloat16
    shape = jax.ShapeDtypeStruct
    rates, onehot, gains, inverse, tokens, middle, cotangent = small
    normed_ffn, upstream, normed, act, partial, result, saved, values, weights, weights_go = large
    rows, width = normed.shape
    heads, units = saved.shape[0], act.shape[0]
    block_rows = width // (LAYERS * mids * CORES)
    widths = ((units, 3 * LANES), (heads, 3 * LANES), (heads, 2 * LANES), (1, LANES))
    chunks = sum(count for count, _ in widths)
    hops = Reduce.semaphores(mids)
    anywhere = pl.BlockSpec(memory_space=pl.ANY)
    vmem = pl.BlockSpec(memory_space=pltpu.VMEM)
    smem = pl.BlockSpec(memory_space=pltpu.SMEM)
    widest = 3 * LANES
    half, own = rows // CORES, rows // (2 * CORES)
    length = own
    inner, outer = CORES * heads * LANES, CORES * units * LANES
    outs = [shape((block_rows, inner), f32)] * 4 + [shape((inner, block_rows), f32)]
    outs += [shape((block_rows, outer), f32)] * 2 + [shape((outer, block_rows), f32)]
    outs.append(shape((8, block_rows), f32))
    passed = [shape((count, CORES, block_rows, wide), bf16) for count, wide in widths]
    sums = [shape((count, LAYERS, mids, CORES, block_rows, wide), bf16) for count, wide in widths]
    cross = [
        shape((count, mids - 1, LAYERS, CORES, block_rows, wide), bf16) for count, wide in widths
    ]
    land = [shape((count, CORES, LAYERS, block_rows, wide), bf16) for count, wide in widths]
    return pl.pallas_call(
        functools.partial(backward_kernel, mids),
        name="backward",
        out_shape=(*outs, shape((own, width), f32), shape((own, width), bf16), *sums, *cross, *land, *passed),
        in_specs=[smem] + [vmem] * 6 + [anywhere] * 10,
        out_specs=(anywhere,) * 8 + (vmem,) * 2 + (anywhere,) * 17,
        scratch_shapes=[
            pltpu.VMEM((rows, width), bf16),
            pltpu.VMEM((rows, width), bf16),
            pltpu.VMEM((rows, width), bf16),
            pltpu.VMEM((2, rows, widest), bf16),
            pltpu.VMEM((2, LAYERS, mids, CORES, block_rows, widest), bf16),
            pltpu.VMEM((1, LAYERS, CORES, block_rows, widest), bf16),
            pltpu.VMEM((1, mids - 1, LAYERS, CORES, block_rows, widest), bf16),
            pltpu.VMEM((SUMS, LAYERS, CORES, block_rows, widest), bf16),
            pltpu.VMEM((1, CORES, LAYERS, block_rows, widest), bf16),
            pltpu.VMEM((2, CORES, block_rows, widest), f32),
            pltpu.VMEM((2, CORES, LANES, block_rows), f32),
            pltpu.VMEM((CORES, block_rows, widest), bf16),
            pltpu.VMEM((2, block_rows, LANES), f32),
            pltpu.VMEM((2, rows, 4 * LANES), f32),
            pltpu.VMEM((2, rows, LANES), bf16),
            pltpu.VMEM((2, width, 5 * LANES), bf16),
            pltpu.VMEM((rows, 4 * LANES), bf16),
            pltpu.VMEM((rows, LANES), bf16),
            pltpu.VMEM((rows, width), f32),
            pltpu.VMEM((half, width), bf16),
            pltpu.VMEM((half, width), bf16),
            pltpu.VMEM((own, width), bf16),
            pltpu.VMEM((own, width), bf16),
            pltpu.VMEM((own, width), f32),
            pltpu.VMEM((own, width), f32),
            pltpu.VMEM((rows, LANES), f32),
            pltpu.VMEM((heads, length, length), f32),
            pltpu.VMEM((rows // length, length, length), f32),
            pltpu.VMEM((2, 8, width), f32),
            pltpu.SemaphoreType.DMA((chunks, hops)),
            pltpu.SemaphoreType.DMA((chunks, hops)),
            pltpu.SemaphoreType.DMA((chunks, 11)),
            pltpu.SemaphoreType.DMA((22,)),
            pltpu.SemaphoreType.DMA((22,)),
            pltpu.SemaphoreType.DMA((15,)),
            pltpu.SemaphoreType.DMA((2,)),
            pltpu.SemaphoreType.REGULAR((2,)),
        ],
        compiler_params=pltpu.CompilerParams(
            collective_id=1, has_side_effects=True, vmem_limit_bytes=63 * 2**20
        ),
    )(*small, *large)[:11]


class Gatherer:
    def __init__(self, chunks):
        self.chunks = chunks
        self.started = self.crossed = self.passed = self.climbed = 0

    def relay_on(self, last):
        while self.climbed < last:
            self.chunks[self.climbed].relay_on()
            self.climbed += 1

    def relay(self, at):
        if at < len(self.chunks) and self.passed == at:
            self.chunks[at].relay()
            self.passed += 1

    def launch(self):
        while self.started < min(len(self.chunks), self.crossed + BEFORE + 1):
            self.chunks[self.started].start()
            self.started += 1

    def cross(self, count=1):
        for _ in range(count):
            if self.crossed < len(self.chunks):
                self.relay(self.crossed)
                self.chunks[self.crossed].cross()
                self.crossed += 1
                self.launch()
                self.relay(self.crossed)
                self.relay_on(self.crossed - 1)

    def arrive(self, at):
        self.cross(at + 1 - self.crossed)
        self.relay_on(at + 1)
        self.chunks[at].arrive()


def forward_kernel(mids, *refs):
    f32, bf16 = jnp.float32, jnp.bfloat16
    (
        rates,
        own_marks,
        tokens,
        cotangent,
        shard_g,
        shard_go,
        shard_qkv,
        shard_f,
        full_g,
        full_go,
        full_qkv,
        full_f,
        normed_hbm,
        normed_ffn_hbm,
        upstream_hbm,
        act_hbm,
        partial_hbm,
        result_hbm,
        saved_hbm,
        values_hbm,
        marks,
        gains,
        inverse,
        middle,
        normed,
        normed_ffn,
        upstream,
        total,
        grad_total,
        weights,
        out_weights,
        saved,
        values,
        act,
        branch,
        part,
        part_in,
        across,
        across_in,
        kept,
        squares,
        squares_in,
        squares_across,
        squares_across_in,
        table,
        same,
        gain_columns,
        send,
        receive,
        local,
        row_send,
        row_receive,
        load_sem,
        store_sem,
    ) = refs
    rows, width = normed.shape
    half = rows // CORES
    part_rows = half // 4
    length = 2 * part_rows
    heads, units = full_qkv.shape[0], full_f.shape[0]
    here = Place(mids)
    sibling = here.device(here.z, here.m, 1 - here.k)
    other = (here.device(here.z, here.m, here.k)[0], 1 - here.t)
    greet(here.weight_peers() + [other])

    chunks = []
    pairs = [(shard_g, full_g, 0)]
    for index in range(heads):
        pairs += [(shard_go, full_go, index), (shard_qkv, full_qkv, index)]
    pairs += [(shard_f, full_f, index) for index in range(units)]
    for at, (source, target, index) in enumerate(pairs):
        chunks.append(
            Gather(
                here,
                source.at[index],
                target.at[index],
                (send.at[at], receive.at[at], local.at[at]),
                at in SIDEWAYS,
            )
        )
    gatherer = Gatherer(chunks)
    gatherer.launch()

    step_rows = 16

    def row_loop(count):
        return pl.loop(0, count // step_rows)

    def at_rows(base, index):
        return pl.ds(pl.multiple_of(base + index * step_rows, step_rows), step_rows)

    def spread(buffer, at):
        window = pl.ds(6 * at, 6)
        return Spread(here, buffer, part_rows, row_send.at[window], row_receive.at[window])

    rows_normed, rows_up = spread(normed, 0), spread(upstream, 1)
    rows_ffn, rows_inverse = spread(normed_ffn, 2), spread(inverse, 3)
    lone = lambda source, target, at, peer: remote(
        source, target, row_send.at[24 + at], row_receive.at[24 + at], peer
    )

    own_half = pl.ds(pl.multiple_of(here.k * half, half), half)
    far_half = pl.ds(pl.multiple_of((1 - here.k) * half, half), half)
    marks[own_half, :] = own_marks[...]
    marks_copy = lone(own_marks, marks.at[own_half], 0, sibling)
    marks_copy.start()

    gatherer.arrive(0)
    load_gain = pltpu.make_async_copy(full_g.at[0], gain_columns, load_sem.at[0])
    load_gain.start()
    load_gain.wait()
    down = lax.broadcasted_iota(jnp.int32, (8, LANES), 0)
    right = lax.broadcasted_iota(jnp.int32, (8, LANES), 1)
    pick = jnp.where(down == right, 1.0, 0.0).astype(bf16)
    gains[...] = dots(pick, gain_columns[...].reshape(width, LANES), 1, 1)

    for batch in range(2):
        base = here.row(here.k, batch, here.t, part_rows)

        @row_loop(part_rows)
        def _(index):
            here_rows = at_rows(batch * part_rows, index)
            value = tokens[here_rows, :].astype(f32)
            scale = lax.rsqrt(jnp.mean(value * value, axis=-1, keepdims=True) + EPSILON)
            normed[at_rows(base, index), :] = (value * scale * gains[0:1, :]).astype(bf16)

        rows_normed.start(batch)
    for batch in range(2):
        base = here.row(here.k, batch, here.t, part_rows)
        upstream[pl.ds(base, part_rows), :] = cotangent[pl.ds(batch * part_rows, part_rows), :]
        rows_up.start(batch)

    down = lax.broadcasted_iota(jnp.int32, (length, length), 0)
    right = lax.broadcasted_iota(jnp.int32, (length, length), 1)
    offset = (down - right).astype(f32)
    for head in range(heads):
        decay = jnp.exp(-rates[head] * jnp.maximum(offset, 0.0))
        table[head] = jnp.where(down >= right, decay, 0.0)
    marks_copy.wait_recv()
    for sequence in range(rows // length):
        mark = marks[pl.ds(sequence * length, length), :]
        same[sequence] = dots(mark, mark, 1, 1)
    squares[...] = jnp.zeros_like(squares)

    def weight(slot, first, last):
        return weights[slot, :, :, :, :, first * LANES : last * LANES].reshape(
            width, (last - first) * LANES
        )

    def store(source, target, at):
        copy = pltpu.make_async_copy(source, target, store_sem.at[at])
        copy.start()
        return copy

    stores = []
    gatherer.cross()
    rows_normed.forward()
    rows_normed.arrive()
    stores.append(store(normed, normed_hbm, 0))
    gatherer.cross()
    rows_up.forward()

    pending = [[], []]
    for head in range(heads):
        slot = head % 2
        gatherer.cross(3 + 2 * head + LEAD - gatherer.crossed)
        gatherer.arrive(1 + 2 * head)
        load_out = pltpu.make_async_copy(
            full_go.at[head, :, :, :, :, pl.ds(LANES, LANES)],
            out_weights.at[:, :, :, :, pl.ds(head * LANES, LANES)],
            load_sem.at[4 + head],
        )
        load_gate = pltpu.make_async_copy(
            full_go.at[head, :, :, :, :, pl.ds(0, LANES)],
            weights.at[slot, :, :, :, :, pl.ds(3 * LANES, LANES)],
            load_sem.at[2 + slot],
        )
        load_gate.start()
        gatherer.cross(3 + 2 * head + LEAD - gatherer.crossed)
        gatherer.arrive(2 + 2 * head)
        load = pltpu.make_async_copy(
            full_qkv.at[head],
            weights.at[slot, :, :, :, :, pl.ds(0, 3 * LANES)],
            load_sem.at[slot],
        )
        load.start()
        load_out.start()
        for copy in pending[slot]:
            copy.wait()
        load_gate.wait()
        load.wait()

        @pl.loop(0, rows // length)
        def _(sequence):
            where = pl.ds(pl.multiple_of(sequence * length, length), length)
            product = dots(normed[where, :], weight(slot, 0, 4), 1, 0)
            query_pre, key_pre = product[:, :LANES], product[:, LANES : 2 * LANES]
            value = product[:, 2 * LANES : 3 * LANES].astype(bf16)
            gate = product[:, 3 * LANES :]
            queries = (query_pre / (1.0 + jnp.exp(-query_pre))).astype(bf16)
            keys = (key_pre / (1.0 + jnp.exp(-key_pre))).astype(bf16)
            masked = table[head] * same[sequence]
            mixing = (dots(queries, keys, 1, 1) * masked).astype(bf16)
            mixed = dots(mixing, value, 1, 0)
            saved[slot, where, : 2 * LANES] = product[:, : 2 * LANES]
            saved[slot, where, 2 * LANES : 3 * LANES] = gate
            saved[slot, where, 3 * LANES :] = mixed
            values[slot, where, :] = value
            branch[where, head * LANES : (head + 1) * LANES] = (mixed * gate).astype(bf16)
            squares[where, :] += jnp.broadcast_to(
                jnp.sum(mixed * mixed, axis=-1, keepdims=True), (length, LANES)
            )

        pending[slot] = [
            store(saved.at[slot], saved_hbm.at[head], 4 + slot),
            store(values.at[slot], values_hbm.at[head], 6 + slot),
        ]
        load_out.wait()
    stores += pending[0] + pending[1]

    @pl.loop(0, half // length)
    def _(block):
        base = (1 - here.k) * half + block * length
        where = pl.ds(pl.multiple_of(base, length), length)
        to = pl.ds(pl.multiple_of(block * length, length), length)
        part[to, :] = dots(branch[where, :], out_weights[...].reshape(width, -1), 1, 1).astype(bf16)

    beside = lone(part, part_in, 1, sibling)
    beside.start()
    beside_squares = lone(squares.at[far_half], squares_in, 2, sibling)
    beside_squares.start()

    @pl.loop(0, half // length)
    def _(block):
        base = here.k * half + block * length
        where = pl.ds(pl.multiple_of(base, length), length)
        total[where, :] = dots(branch[where, :], out_weights[...].reshape(width, -1), 1, 1)

    beside.wait_recv()
    beside_squares.wait_recv()
    crossings = []
    for batch in range(2):
        block = pl.ds(batch * part_rows, part_rows)
        crossings.append(
            (
                lone(across.at[block], across_in.at[block], 3 + batch, other),
                lone(squares_across.at[block], squares_across_in.at[block], 5 + batch, other),
            )
        )

        @row_loop(part_rows)
        def _(index):
            base = batch * length + (1 - here.t) * part_rows
            value = total[at_rows(here.k * half + base, index), :]
            value += part_in[at_rows(base, index), :].astype(f32)
            to = at_rows(batch * part_rows, index)
            across[to, :] = value.astype(bf16)
            squares_across[to, :] = (
                squares[at_rows(here.k * half + base, index), :]
                + squares_in[at_rows(base, index), :]
            )

        for copy in crossings[batch]:
            copy.start()
    for batch in range(2):

        @row_loop(part_rows)
        def _(index):
            base = batch * length + here.t * part_rows
            value = total[at_rows(here.k * half + base, index), :]
            to = at_rows(batch * part_rows, index)
            kept[to, :] = value + part_in[at_rows(base, index), :].astype(f32)

    gatherer.cross()
    rows_up.arrive()
    stores.append(store(upstream, upstream_hbm, 1))
    for batch in range(2):
        for copy in crossings[batch]:
            copy.wait_recv()
        base = here.row(here.k, batch, here.t, part_rows)

        @row_loop(part_rows)
        def _(index):
            here_rows = at_rows(batch * part_rows, index)
            from_rows = batch * length + here.t * part_rows
            square = (
                squares[at_rows(here.k * half + from_rows, index), :]
                + squares_in[at_rows(from_rows, index), :]
                + squares_across_in[here_rows, :]
            )
            scale = lax.rsqrt(square / width + EPSILON)
            inverse[at_rows(base, index), :] = scale
            attended = (kept[here_rows, :] + across_in[here_rows, :].astype(f32)) * scale[:, :1]
            mid = tokens[here_rows, :].astype(f32) + attended
            middle[here_rows, :] = mid
            scale = lax.rsqrt(jnp.mean(mid * mid, axis=-1, keepdims=True) + EPSILON)
            normed_ffn[at_rows(base, index), :] = (mid * scale * gains[1:2, :]).astype(bf16)

        rows_ffn.start(batch)
        rows_inverse.start(batch)
    gatherer.cross()
    rows_ffn.forward()
    rows_inverse.forward()
    gatherer.cross()
    rows_ffn.arrive()
    rows_inverse.arrive()
    stores.append(store(normed_ffn, normed_ffn_hbm, 2))

    pending = [None, None]
    for at in range(units):
        slot = at % 2
        gatherer.cross(2 + 2 * heads + at + 1 - gatherer.crossed)
        gatherer.arrive(1 + 2 * heads + at)
        load = pltpu.make_async_copy(
            full_f.at[at], weights.at[slot, :, :, :, :, pl.ds(0, 3 * LANES)], load_sem.at[slot]
        )
        load.start()
        if pending[slot] is not None:
            pending[slot].wait()
        gatherer.cross()
        if at == units - 1:
            for copy in stores:
                copy.wait()
            rows_normed.finish()
            rows_ffn.finish()
        load.wait()

        @pl.loop(0, rows // length)
        def _(block):
            where = pl.ds(pl.multiple_of(block * length, length), length)
            product = dots(normed_ffn[where, :], weight(slot, 0, 2), 1, 0)
            left, right = product[:, :LANES], product[:, LANES:]
            grad_joined = dots(upstream[where, :], weight(slot, 2, 3), 1, 0)
            act[slot, where, :LANES] = (grad_joined * right).astype(bf16)
            act[slot, where, LANES : 2 * LANES] = (grad_joined * left).astype(bf16)
            act[slot, where, 2 * LANES :] = (left * right).astype(bf16)
            out = dots(act[slot, where, 2 * LANES :], weight(slot, 2, 3), 1, 1)
            grad = dots(act[slot, where, : 2 * LANES], weight(slot, 0, 2), 1, 1)
            if at == 0:
                total[where, :] = out
                grad_total[where, :] = grad
            elif at == units - 1:
                normed[where, :] = (total[where, :] + out).astype(bf16)
                normed_ffn[where, :] = (grad_total[where, :] + grad).astype(bf16)
            else:
                total[where, :] += out
                grad_total[where, :] += grad

        pending[slot] = store(act.at[slot], act_hbm.at[at], 8 + slot)

    grads = store(normed_ffn, partial_hbm, 0)
    outs = store(normed, result_hbm, 1)
    for copy in pending + [grads, outs]:
        copy.wait()
    for chunk in chunks:
        chunk.finish()
    rows_up.finish()
    rows_inverse.finish()
    marks_copy.wait_send()
    beside.wait_send()
    beside_squares.wait_send()
    for pair in crossings:
        for copy in pair:
            copy.wait_send()


def forward(mids, rates, marks, tokens, cotangent, shards):
    f32, bf16 = jnp.float32, jnp.bfloat16
    shape = jax.ShapeDtypeStruct
    own, width = tokens.shape
    rows, half = 4 * own, 2 * own
    length = own
    heads, units = shards[1].shape[0], shards[3].shape[0]
    block_rows = shards[0].shape[2]
    full = [shape((w.shape[0], LAYERS, mids) + w.shape[1:], bf16) for w in shards]
    chunks = 1 + 2 * heads + units
    hops = Gather.semaphores(mids)
    anywhere = pl.BlockSpec(memory_space=pl.ANY)
    vmem = pl.BlockSpec(memory_space=pltpu.VMEM)
    smem = pl.BlockSpec(memory_space=pltpu.SMEM)
    block = (LAYERS, mids, CORES, block_rows)
    return pl.pallas_call(
        functools.partial(forward_kernel, mids),
        name="forward",
        out_shape=(
            *full,
            *[shape((rows, width), bf16)] * 3,
            shape((units, rows, 3 * LANES), bf16),
            *[shape((rows, width), bf16)] * 2,
            shape((heads, rows, 4 * LANES), f32),
            shape((heads, rows, LANES), bf16),
            shape((rows, LANES), bf16),
            shape((8, width), f32),
            shape((rows, LANES), f32),
            shape((own, width), f32),
        ),
        in_specs=[smem] + [vmem] * 3 + [anywhere] * 4,
        out_specs=(anywhere,) * 12 + (vmem,) * 4,
        scratch_shapes=[
            pltpu.VMEM((rows, width), bf16),
            pltpu.VMEM((rows, width), bf16),
            pltpu.VMEM((rows, width), bf16),
            pltpu.VMEM((rows, width), f32),
            pltpu.VMEM((rows, width), f32),
            pltpu.VMEM((2, *block, 4 * LANES), bf16),
            pltpu.VMEM((*block, heads * LANES), bf16),
            pltpu.VMEM((2, rows, 4 * LANES), f32),
            pltpu.VMEM((2, rows, LANES), bf16),
            pltpu.VMEM((2, rows, 3 * LANES), bf16),
            pltpu.VMEM((rows, heads * LANES), bf16),
            pltpu.VMEM((half, width), bf16),
            pltpu.VMEM((half, width), bf16),
            pltpu.VMEM((own, width), bf16),
            pltpu.VMEM((own, width), bf16),
            pltpu.VMEM((own, width), f32),
            pltpu.VMEM((rows, LANES), f32),
            pltpu.VMEM((half, LANES), f32),
            pltpu.VMEM((own, LANES), f32),
            pltpu.VMEM((own, LANES), f32),
            pltpu.VMEM((heads, length, length), f32),
            pltpu.VMEM((rows // length, length, length), f32),
            pltpu.VMEM((*block, LANES), bf16),
            pltpu.SemaphoreType.DMA((chunks, hops)),
            pltpu.SemaphoreType.DMA((chunks, hops)),
            pltpu.SemaphoreType.DMA((chunks,)),
            pltpu.SemaphoreType.DMA((31,)),
            pltpu.SemaphoreType.DMA((31,)),
            pltpu.SemaphoreType.DMA((4 + heads,)),
            pltpu.SemaphoreType.DMA((10,)),
        ],
        compiler_params=pltpu.CompilerParams(
            collective_id=0, has_side_effects=True, vmem_limit_bytes=63 * 2**20
        ),
    )(rates, marks, tokens, cotangent, *shards)


def split_heads(weight, halves):
    return weight.reshape(weight.shape[0], CORES, -1, LANES)


def pack(parts):
    joined = jnp.concatenate([split_heads(part, CORES) for part in parts], axis=-1)
    return joined.transpose(2, 1, 0, 3)


def local(
    mids,
    tokens,
    segment_ids,
    decay_rates,
    gain_attn,
    w_query,
    w_key,
    w_value,
    w_gate,
    w_out,
    gain_ffn,
    w_left,
    w_right,
    w_down,
    cotangent,
):
    f32, bf16 = jnp.float32, jnp.bfloat16
    batches, local_rows, model_width = tokens.shape
    core = lax.rem(lax.axis_index("dp"), CORES)
    heads = decay_rates.shape[0] // CORES
    rates = lax.dynamic_slice_in_dim(decay_rates, core * heads, heads)
    own = lambda values: values.reshape(batches * local_rows, model_width)
    marks = (segment_ids.reshape(-1)[:, None] == jnp.arange(LANES)[None, :]).astype(bf16)
    gain_columns = jnp.pad(
        jnp.stack([gain_attn, gain_ffn], axis=1), ((0, 0), (0, LANES - 2))
    )
    shards = (
        jnp.stack([gain_columns] * CORES)[None],
        pack([w_gate, w_out.T]),
        pack([w_query, w_key, w_value]),
        pack([w_left, w_right, w_down.T]),
    )
    (
        _,
        full_go,
        full_qkv,
        _,
        normed,
        normed_ffn,
        upstream,
        act,
        partial,
        result,
        saved,
        values,
        marks,
        gains,
        inverse,
        middle,
    ) = forward(mids, rates, marks, own(tokens), own(cotangent), shards)
    full_go = full_go.reshape(heads, model_width, -1)
    full_qkv = full_qkv.reshape(heads, model_width, -1)
    *grads, grad_gains, grad_tokens, result = backward(
        mids,
        (rates, marks, gains, inverse, own(tokens), middle, own(cotangent)),
        (normed_ffn, upstream, normed, act, partial, result, saved, values, full_qkv, full_go),
    )
    result = result.reshape(tokens.shape)
    return (
        result,
        grad_tokens.reshape(tokens.shape),
        grad_gains[0],
        *grads[:5],
        grad_gains[1],
        *grads[5:],
    )


def solution(mesh):
    return jax.shard_map(
        functools.partial(local, mesh.shape["dp"] // (LAYERS * CORES)),
        mesh=mesh,
        in_specs=(
            P(None, ("dp", "tensor"), None),
            P(None, "dp"),
            P("tensor"),
            P("dp"),
            P("dp", "tensor"),
            P("dp", "tensor"),
            P("dp", "tensor"),
            P("dp", "tensor"),
            P("tensor", "dp"),
            P("dp"),
            P("dp", "tensor"),
            P("dp", "tensor"),
            P("tensor", "dp"),
            P(None, ("dp", "tensor"), None),
        ),
        out_specs=(
            P(None, ("dp", "tensor"), None),
            P(None, ("dp", "tensor"), None),
            P("dp"),
            P("dp", "tensor"),
            P("dp", "tensor"),
            P("dp", "tensor"),
            P("dp", "tensor"),
            P("tensor", "dp"),
            P("dp"),
            P("dp", "tensor"),
            P("dp", "tensor"),
            P("tensor", "dp"),
        ),
        check_vma=False,
    )
```

```python
import functools

import jax
import jax.numpy as jnp
from jax import lax
from jax.experimental import pallas as pl
from jax.experimental.pallas import tpu as pltpu
from jax.sharding import PartitionSpec as P

EPSILON = 1e-06
LAYERS = 4
CORES = 2
LANES = 128
AHEAD = 1
BEFORE = 4
LEAD = 3
SIDEWAYS = (9, 13)
SLICE = 32
CLIMBS = {0: 4}
EARLY = 6
NEAR = 2
LAG = 2
BEHIND = 2
SUMS = 6
FETCH = 5
MESH = pl.DeviceIdType.MESH


class Place:
    def __init__(self, mids):
        place = lax.axis_index("dp")
        self.mids = mids
        self.t = lax.axis_index("tensor")
        self.k = lax.rem(place, CORES)
        self.m = lax.rem(lax.div(place, CORES), mids)
        self.z = lax.div(place, CORES * mids)

    def device(self, z, m, k):
        return ((z * self.mids + m) * CORES + k, self.t)

    def layer(self, step):
        return lax.rem(self.z + step, LAYERS)

    def mid(self, step):
        return lax.rem(self.m + step, self.mids)

    def row(self, core, batch, half, part):
        return pl.multiple_of(((core * 2 + batch) * 2 + half) * part, part)

    def weight_peers(self):
        peers = [self.device(self.z, self.m, 1 - self.k)]
        for step in range(1, LAYERS):
            for core in range(CORES):
                peers.append(self.device(self.layer(step), self.m, core))
        for step in range(1, self.mids):
            for core in range(CORES):
                peers.append(self.device(self.z, self.mid(step), core))
        return peers


def greet(peers):
    barrier = pltpu.get_barrier_semaphore()
    for peer in peers:
        pl.semaphore_signal(barrier, inc=1, device_id=peer, device_id_type=MESH)
    pl.semaphore_wait(barrier, len(peers))


def remote(source, target, send, receive, peer):
    return pltpu.make_async_remote_copy(
        src_ref=source,
        dst_ref=target,
        send_sem=send,
        recv_sem=receive,
        device_id=peer,
        device_id_type=MESH,
    )


def apart(one, layer):
    near = jnp.logical_and(one - layer <= 2, layer - one <= 2)
    return jnp.logical_and(one != layer, near)


def relayed(here, layer):
    first, last = layer == 0, layer == LAYERS - 1
    if not (first or last):
        return None, None
    return (here == LAYERS - 2, LAYERS - 1) if first else (here == 1, 0)


class Gather:
    def __init__(self, place, source, target, sems, sideways):
        self.place, self.source, self.target = place, source, target
        self.send, self.receive, self.local = sems
        self.sideways = sideways
        here = place
        self.own = target.at[here.z, here.m, here.k]
        self.keep = pltpu.make_async_copy(source.at[here.k], self.own, self.local)
        self.beside = remote(
            source.at[1 - here.k],
            self.own,
            self.send.at[0],
            self.receive.at[0],
            here.device(here.z, here.m, 1 - here.k),
        )
        self.sides = 1 + LAYERS * CORES
        self.crosses = self.sides + (here.mids - 1) * CORES

    @staticmethod
    def semaphores(mids):
        return 1 + LAYERS * CORES + (mids - 1) * (CORES + LAYERS)

    def hop(self, layer, core, origin):
        here = self.place
        arrival = 1 + (here.z * CORES + here.k if origin is None else origin * CORES + core)
        return remote(
            self.source.at[core],
            self.own,
            self.send.at[1 + layer * CORES + core],
            self.receive.at[arrival],
            here.device(layer, here.m, core),
        )

    def pass_on(self, layer, core, goal):
        here = self.place
        block = self.target.at[layer, here.m, core]
        return remote(
            block,
            block,
            self.send.at[1 + here.z * CORES + core],
            self.receive.at[1 + layer * CORES + core],
            here.device(goal, here.m, here.k),
        )

    def side(self, step, core, wait):
        here = self.place
        at = self.sides + (step - 1) * CORES
        return remote(
            self.source.at[core],
            self.own,
            self.send.at[at + core],
            self.receive.at[at + (core if wait else here.k)],
            here.device(here.z, here.mid(step), core),
        )

    def crossing(self, step, layer):
        here = self.place
        at = self.crosses + (step - 1) * LAYERS + layer
        block = self.target.at[layer, here.m]
        return remote(
            block,
            block,
            self.send.at[at],
            self.receive.at[at],
            here.device(here.z, here.mid(step), here.k),
        )

    def start(self):
        here = self.place
        self.keep.start()
        self.beside.start()
        for step in range(1, here.mids):
            for core in range(CORES):
                self.side(step, core, False).start()
        for layer in range(LAYERS):

            @pl.when(apart(here.z, layer))
            def _():
                for core in range(CORES):
                    self.hop(layer, core, None).start()

    def relay(self):
        for layer in (0, LAYERS - 1):
            mine, goal = relayed(self.place.z, layer)

            @pl.when(mine)
            def _():
                for core in range(CORES):
                    self.hop(layer, core, layer).wait_recv()
                    self.pass_on(layer, core, goal).start()

    def climb(self, step, layer):
        here = self.place
        at = self.crosses + (step - 1) * LAYERS
        block = self.target.at[here.z, here.mid(step)]
        return remote(
            block,
            block,
            self.send.at[at + layer],
            self.receive.at[at + here.z],
            here.device(layer, here.m, here.k),
        )

    def climbed(self, step, layer, goal):
        here = self.place
        at = self.crosses + (step - 1) * LAYERS
        block = self.target.at[layer, here.mid(step)]
        return remote(
            block,
            block,
            self.send.at[at + here.z],
            self.receive.at[at + layer],
            here.device(goal, here.m, here.k),
        )

    def wait_layers(self, then):
        here = self.place
        for layer in range(LAYERS):
            awaited = here.z != layer
            mine, _ = relayed(here.z, layer)
            if mine is not None:
                awaited = jnp.logical_and(awaited, jnp.logical_not(mine))

            @pl.when(awaited)
            def _():
                for core in range(CORES):
                    self.hop(layer, core, layer).wait_recv()

            then(layer)

    def cross(self):
        here = self.place
        if self.sideways:
            for step in range(1, here.mids):
                for core in range(CORES):
                    self.side(step, core, True).wait_recv()
            for layer in range(LAYERS):

                @pl.when(apart(here.z, layer))
                def _():
                    for step in range(1, here.mids):
                        self.climb(step, layer).start()

            return

        def send_on(layer):
            @pl.when(here.z != layer)
            def _():
                for step in range(1, here.mids):
                    self.crossing(step, layer).start()

        self.wait_layers(send_on)

    def relay_on(self):
        if self.sideways:
            here = self.place
            for layer in (0, LAYERS - 1):
                mine, goal = relayed(here.z, layer)

                @pl.when(mine)
                def _():
                    for step in range(1, here.mids):
                        self.climbed(step, layer, goal).wait_recv()
                        self.climbed(step, layer, goal).start()

    def arrive(self):
        here = self.place
        self.keep.wait()
        self.beside.wait_recv()
        if self.sideways:
            self.wait_layers(lambda layer: None)
            for layer in range(LAYERS):
                awaited = here.z != layer
                mine, _ = relayed(here.z, layer)
                if mine is not None:
                    awaited = jnp.logical_and(awaited, jnp.logical_not(mine))

                @pl.when(awaited)
                def _():
                    for step in range(1, here.mids):
                        self.climbed(step, layer, layer).wait_recv()

            return
        for step in range(1, here.mids):
            for core in range(CORES):
                self.side(step, core, True).wait_recv()
        for layer in range(LAYERS):

            @pl.when(here.z != layer)
            def _():
                for step in range(1, here.mids):
                    self.crossing(step, layer).wait_recv()

    def finish(self):
        here = self.place
        self.beside.wait_send()
        for step in range(1, here.mids):
            for core in range(CORES):
                self.side(step, core, False).wait_send()
        for layer in range(LAYERS):

            @pl.when(apart(here.z, layer))
            def _():
                for core in range(CORES):
                    self.hop(layer, core, None).wait_send()
                if self.sideways:
                    for step in range(1, here.mids):
                        self.climb(step, layer).wait_send()

            mine, goal = relayed(here.z, layer)
            if mine is not None:

                @pl.when(mine)
                def _():
                    for core in range(CORES):
                        self.pass_on(layer, core, goal).wait_send()
                    if self.sideways:
                        for step in range(1, here.mids):
                            self.climbed(step, layer, goal).wait_send()

            if not self.sideways:

                @pl.when(here.z != layer)
                def _():
                    for step in range(1, here.mids):
                        self.crossing(step, layer).wait_send()


class Reduce:
    sideways = False

    def __init__(self, place, source, crossed, landed, passed, stores, slots, sems):
        self.place, self.source, self.crossed, self.landed = place, source, crossed, landed
        self.passed = passed
        (
            self.own_slot,
            self.cross_slot,
            self.sum_slot,
            self.land_slot,
            self.out_slot,
            self.turn_slot,
            self.pass_slot,
        ) = slots
        self.send, self.receive, local = sems
        here = place
        self.crossings = [
            remote(
                source.at[:, here.mid(step)],
                crossed.at[step - 1],
                self.send.at[step - 1],
                self.receive.at[step - 1],
                here.device(here.z, here.mid(step), here.k),
            )
            for step in range(1, here.mids)
        ]
        self.base = here.mids
        self.beside = remote(
            self.sum_slot.at[here.z, 1 - here.k],
            landed.at[here.k, here.z],
            self.send.at[here.mids - 1],
            self.receive.at[here.mids - 1],
            here.device(here.z, here.m, 1 - here.k),
        )
        self.keep = pltpu.make_async_copy(
            self.sum_slot.at[here.z, here.k], landed.at[here.k, here.z], local.at[0]
        )
        self.load_own = pltpu.make_async_copy(source.at[:, here.m], self.own_slot, local.at[1])
        self.load_cross = pltpu.make_async_copy(crossed, self.cross_slot, local.at[2])
        self.load_land = pltpu.make_async_copy(landed, self.land_slot, local.at[3])
        self.load_pass = pltpu.make_async_copy(passed, self.pass_slot, local.at[4])
        self.turned = self.turn_slot is not None
        self.stores = [
            pltpu.make_async_copy(piece(self.out_slot, self.turn_slot), target, local.at[5 + at])
            for at, (piece, target) in enumerate(stores)
        ]

    @staticmethod
    def semaphores(mids):
        return max(mids + LAYERS * CORES + 1, LAYERS + 2 + (mids - 1) * CORES)

    def hop(self, layer, core, origin):
        here = self.place
        arrival = here.z * CORES + here.k if origin is None else origin * CORES + core
        return remote(
            self.sum_slot.at[layer, core],
            self.landed.at[here.k, here.z],
            self.send.at[self.base + layer * CORES + core],
            self.receive.at[self.base + arrival],
            here.device(layer, here.m, core),
        )

    def far(self, layer, goal):
        here = self.place
        at = self.base + LAYERS * CORES
        return remote(
            self.sum_slot.at[layer],
            self.passed,
            self.send.at[at],
            self.receive.at[at],
            here.device(goal, here.m, here.k),
        )

    def ends(self):
        return (
            (self.place.z == 0, LAYERS - 1, LAYERS - 2),
            (self.place.z == LAYERS - 1, 0, 1),
        )

    def start(self):
        for crossing in self.crossings:
            crossing.start()

    def load(self):
        self.load_own.start()
        for crossing in self.crossings:
            crossing.wait_recv()
        self.load_cross.start()

    def add(self):
        here = self.place
        self.load_own.wait()
        self.load_cross.wait()

        @pl.loop(0, LAYERS * CORES)
        def _(at):
            layer, core = lax.div(at, CORES), lax.rem(at, CORES)

            @pl.loop(0, self.own_slot.shape[2] // SLICE)
            def _(index):
                where = pl.ds(pl.multiple_of(index * SLICE, SLICE), SLICE)
                total = self.own_slot[layer, core, where].astype(jnp.float32)
                for step in range(1, here.mids):
                    total += self.cross_slot[step - 1, layer, core, where].astype(jnp.float32)
                self.sum_slot[layer, core, where] = total.astype(jnp.bfloat16)

        for end, layer, goal in self.ends():

            @pl.when(end)
            def _():
                self.far(layer, goal).start()

        self.keep.start()
        self.beside.start()
        for layer in range(LAYERS):
            now = apart(here.z, layer)
            if layer in (0, LAYERS - 1):
                now = jnp.logical_and(now, here.z != (1 if layer == 0 else LAYERS - 2))

            @pl.when(now)
            def _():
                for core in range(CORES):
                    self.hop(layer, core, None).start()

    def relay(self):
        for _, layer, goal in self.ends():

            @pl.when(self.place.z == goal)
            def _():
                self.far(layer, goal).wait_recv()
                self.load_pass.start()
                self.load_pass.wait()

                @pl.loop(0, CORES)
                def _(core):
                    total = self.sum_slot[layer, core].astype(jnp.float32)
                    total += self.pass_slot[core].astype(jnp.float32)
                    self.sum_slot[layer, core] = total.astype(jnp.bfloat16)

                for core in range(CORES):
                    self.hop(layer, core, None).start()

    def release(self):
        self.beside.wait_send()
        for layer in range(LAYERS):

            @pl.when(apart(self.place.z, layer))
            def _():
                for core in range(CORES):
                    self.hop(layer, core, None).wait_send()

        for end, layer, goal in self.ends():

            @pl.when(end)
            def _():
                self.far(layer, goal).wait_send()

    def fetch(self):
        self.keep.wait()
        self.beside.wait_recv()
        for layer in range(LAYERS):

            @pl.when(apart(self.place.z, layer))
            def _():
                for core in range(CORES):
                    self.hop(layer, core, layer).wait_recv()

        self.load_land.start()

    def total(self):
        self.load_land.wait()
        here = self.place
        present = [
            jnp.logical_or(here.z == layer, apart(here.z, layer)) for layer in range(LAYERS)
        ]

        @pl.loop(0, CORES)
        def _(core):
            total = None
            for layer in range(LAYERS):
                value = self.land_slot[core, layer].astype(jnp.float32)
                if layer in (0, LAYERS - 1):
                    value = jnp.where(present[layer], value, 0.0)
                total = value if total is None else total + value
            self.out_slot[core] = total
            if self.turned:
                self.turn_slot[core] = total[:, -LANES:].T

        for store in self.stores:
            store.start()

    def stored(self):
        for store in self.stores:
            store.wait()

    def finish(self):
        for crossing in self.crossings:
            crossing.wait_send()


class Climb(Reduce):
    sideways = True

    def __init__(self, place, source, climbed, landed, passed, stores, slots, sems):
        self.place, self.source, self.climbed_to, self.landed = place, source, climbed, landed
        self.passed = passed
        (
            self.own_slot,
            self.climb_slot,
            self.sum_slot,
            self.land_slot,
            self.out_slot,
            self.turn_slot,
            self.pass_slot,
            self.pass_sum,
        ) = slots
        self.send, self.receive, self.local = sems
        here = place
        self.turned = self.turn_slot is not None
        self.beside = remote(
            self.sum_slot.at[here.m, 1 - here.k],
            landed.at[here.k, 0],
            self.send.at[LAYERS + 1],
            self.receive.at[LAYERS + 1],
            here.device(here.z, here.m, 1 - here.k),
        )
        local = self.local
        self.keep = pltpu.make_async_copy(
            self.sum_slot.at[here.m, here.k], landed.at[here.k, 0], local.at[0]
        )
        self.load_own = pltpu.make_async_copy(source.at[here.z], self.own_slot, local.at[1])
        self.load_climbed = pltpu.make_async_copy(climbed, self.climb_slot, local.at[2])
        self.load_land = pltpu.make_async_copy(landed, self.land_slot, local.at[3])
        self.stores = [
            pltpu.make_async_copy(piece(self.out_slot, self.turn_slot), target, local.at[5 + at])
            for at, (piece, target) in enumerate(stores)
        ]

    def up(self, layer, block):
        here = self.place
        return remote(
            block,
            self.climbed_to.at[here.z],
            self.send.at[layer],
            self.receive.at[here.z],
            here.device(layer, here.m, here.k),
        )

    def come(self, layer):
        here = self.place
        block = self.climbed_to.at[layer]
        return remote(
            block,
            block,
            self.send.at[layer],
            self.receive.at[layer],
            here.device(layer, here.m, here.k),
        )

    def far(self, layer, goal):
        here = self.place
        return remote(
            self.source.at[layer],
            self.passed,
            self.send.at[LAYERS],
            self.receive.at[LAYERS],
            here.device(goal, here.m, here.k),
        )

    def across(self, step, core, wait):
        here = self.place
        at = LAYERS + 2 + (step - 1) * CORES
        return remote(
            self.sum_slot.at[here.mid(step), core],
            self.landed.at[here.k, step],
            self.send.at[at + core],
            self.receive.at[at + (core if wait else here.k)],
            here.device(here.z, here.mid(step), core),
        )

    def now(self, layer):
        now = apart(self.place.z, layer)
        if layer in (0, LAYERS - 1):
            now = jnp.logical_and(now, self.place.z != (1 if layer == 0 else LAYERS - 2))
        return now

    def start(self):
        for end, layer, goal in self.ends():

            @pl.when(end)
            def _():
                self.far(layer, goal).start()

        for layer in range(LAYERS):

            @pl.when(self.now(layer))
            def _():
                self.up(layer, self.source.at[layer]).start()

    def relay_up(self):
        here = self.place
        for _, layer, goal in self.ends():

            @pl.when(here.z == goal)
            def _():
                self.far(layer, goal).wait_recv()
                loads = (
                    pltpu.make_async_copy(self.passed, self.pass_slot, self.local.at[4]),
                    pltpu.make_async_copy(
                        self.source.at[layer], self.pass_sum, self.local.at[11]
                    ),
                )
                for copy in loads:
                    copy.start()
                for copy in loads:
                    copy.wait()

                @pl.loop(0, here.mids * CORES)
                def _(at):
                    mid, core = lax.div(at, CORES), lax.rem(at, CORES)
                    total = self.pass_sum[mid, core].astype(jnp.float32)
                    total += self.pass_slot[mid, core].astype(jnp.float32)
                    self.pass_sum[mid, core] = total.astype(jnp.bfloat16)

                self.up(layer, self.pass_sum).start()

    def load(self):
        self.load_own.start()
        for layer in range(LAYERS):

            @pl.when(apart(self.place.z, layer))
            def _():
                self.come(layer).wait_recv()

        self.load_climbed.start()

    def add(self):
        here = self.place
        self.load_own.wait()
        self.load_climbed.wait()
        present = [apart(here.z, layer) for layer in range(LAYERS)]

        @pl.loop(0, here.mids * CORES)
        def _(at):
            mid, core = lax.div(at, CORES), lax.rem(at, CORES)
            total = self.own_slot[mid, core].astype(jnp.float32)
            for layer in range(LAYERS):
                value = self.climb_slot[layer, mid, core].astype(jnp.float32)
                total += jnp.where(present[layer], value, 0.0)
            self.sum_slot[mid, core] = total.astype(jnp.bfloat16)

        for step in range(1, here.mids):
            for core in range(CORES):
                self.across(step, core, False).start()
        self.keep.start()
        self.beside.start()

    def relay(self):
        pass

    def release(self):
        here = self.place
        self.beside.wait_send()
        for step in range(1, here.mids):
            for core in range(CORES):
                self.across(step, core, False).wait_send()
        for layer in range(LAYERS):

            @pl.when(apart(here.z, layer))
            def _():
                self.up(layer, self.source.at[layer]).wait_send()

        for end, layer, goal in self.ends():

            @pl.when(end)
            def _():
                self.far(layer, goal).wait_send()

    def fetch(self):
        self.keep.wait()
        self.beside.wait_recv()
        for step in range(1, self.place.mids):
            for core in range(CORES):
                here = self.place
                at = LAYERS + 2 + (step - 1) * CORES + core
                block = self.landed.at[core, step]
                remote(
                    block,
                    block,
                    self.send.at[at],
                    self.receive.at[at],
                    here.device(here.z, here.mid(step), core),
                ).wait_recv()
        self.load_land.start()

    def total(self):
        self.load_land.wait()

        @pl.loop(0, CORES)
        def _(core):
            total = self.land_slot[core, 0].astype(jnp.float32)
            for step in range(1, self.place.mids):
                total += self.land_slot[core, step].astype(jnp.float32)
            self.out_slot[core] = total
            if self.turned:
                self.turn_slot[core] = total[:, -LANES:].T

        for store in self.stores:
            store.start()

    def finish(self):
        pass


def dots(left, right, left_axis, right_axis):
    return lax.dot_general(
        left, right, (((left_axis,), (right_axis,)), ((), ())), preferred_element_type=jnp.float32
    )


class Reducer:
    def __init__(self, chunks, keys):
        self.chunks, self.keys = chunks, keys
        self.ahead, self.fetch = BEHIND, FETCH
        self.ticks = self.landed = 0
        self.produced, self.started, self.relayed = set(), set(), set()

    def launch(self):
        blocked = False
        for at, chunk in enumerate(self.chunks):
            if at in self.started:
                continue
            ready = at in self.produced
            if chunk.sideways:
                ready = ready and at <= self.ticks + EARLY
            else:
                blocked = blocked or not ready or at > self.ticks + self.ahead
                ready = not blocked
            if ready:
                chunk.start()
                self.started.add(at)

    def relay_up(self, at):
        if at in self.started and self.chunks[at].sideways and at not in self.relayed:
            self.relayed.add(at)
            self.chunks[at].relay_up()

    def produce(self, key):
        self.produced.add(self.keys.index(key))
        self.launch()

    def tick(self):
        at, chunks = self.ticks, self.chunks
        count = len(chunks)
        if at < count:
            assert at in self.started
            self.relay_up(at)
            chunks[at].load()
        self.ticks += 1
        self.launch()
        for near in range(at + 1, min(at + 1 + NEAR, count)):
            self.relay_up(near)
        if 0 <= at - LAG < count:
            chunks[at - LAG].relay()
        if at < count:
            if at >= SUMS:
                chunks[at - SUMS].release()
            chunks[at].add()
        while self.landed <= min(at - self.fetch, count - 1):
            chunks[self.landed].fetch()
            if self.landed >= 2:
                chunks[self.landed - 2].stored()
            chunks[self.landed].total()
            self.landed += 1

    def drain(self):
        count = len(self.chunks)
        self.ahead, self.fetch = AHEAD, LAG + 1
        while self.landed < count:
            self.tick()
        for chunk in self.chunks[-2:]:
            chunk.stored()
        for chunk in self.chunks[-SUMS:]:
            chunk.release()
        for chunk in self.chunks:
            chunk.finish()


class Spread:
    def __init__(self, here, buffer, part, send, receive):
        sibling = here.device(here.z, here.m, 1 - here.k)
        other = (here.device(here.z, here.m, here.k)[0], 1 - here.t)
        self.across, self.beside, self.onward = [], [], []
        for batch in range(2):
            own = buffer.at[pl.ds(here.row(here.k, batch, here.t, part), part)]
            theirs = buffer.at[pl.ds(here.row(here.k, batch, 1 - here.t, part), part)]
            self.across.append(remote(own, own, send.at[batch], receive.at[batch], other))
            self.beside.append(remote(own, own, send.at[2 + batch], receive.at[2 + batch], sibling))
            self.onward.append(
                remote(theirs, theirs, send.at[4 + batch], receive.at[4 + batch], sibling)
            )

    def start(self, batch):
        self.across[batch].start()
        self.beside[batch].start()

    def forward(self):
        for batch in range(2):
            self.across[batch].wait_recv()
            self.onward[batch].start()

    def arrive(self):
        for copy in self.beside + self.onward:
            copy.wait_recv()

    def finish(self):
        for copy in self.across + self.beside + self.onward:
            copy.wait_send()


def backward_kernel(mids, *refs):
    f32, bf16 = jnp.float32, jnp.bfloat16
    (
        rates,
        onehot,
        gains,
        inverse,
        tokens,
        middle,
        cotangent,
        normed_ffn_hbm,
        upstream_hbm,
        normed_hbm,
        act_hbm,
        partial_hbm,
        result_hbm,
        saved_hbm,
        values_hbm,
        weights_hbm,
        weights_go_hbm,
        out_query,
        out_key,
        out_value,
        out_gate,
        out_out,
        out_left,
        out_right,
        out_down,
        out_gain,
        grad_tokens,
        result,
        p_f,
        p_qkv,
        p_go,
        p_gain,
        *rest,
    ) = refs
    crossed, landed, passed, side, rest = rest[:4], rest[4:8], rest[8:12], rest[12:15], rest[15:]
    (
        normed,
        upstream,
        grad_out,
        act,
        stage,
        own_slot,
        cross_slot,
        sum_slot,
        land_slot,
        out_slot,
        turn_slot,
        pass_slot,
        gain_slot,
        side_own,
        side_climb,
        side_sum,
        side_land,
        side_pass,
        side_pass_sum,
        saved,
        values,
        weights,
        projected,
        branch,
        total,
        part,
        part_in,
        across,
        across_in,
        kept,
        grad_middle,
        dot_sum,
        table,
        same,
        columns,
        send,
        receive,
        local,
        row_send,
        row_receive,
        load_sem,
        stage_sem,
        free,
    ) = rest
    rows, width = normed.shape
    half = rows // CORES
    part_rows = half // 4
    length = 2 * part_rows
    heads, units = saved_hbm.shape[0], act_hbm.shape[0]
    here = Place(mids)
    sibling = here.device(here.z, here.m, 1 - here.k)
    other = (here.device(here.z, here.m, here.k)[0], 1 - here.t)
    greet(here.weight_peers() + [other])

    chunks = []
    lists = []

    def columns_of(target, index, count, place):
        for core in range(CORES):
            where = pl.ds((core * count + index) * LANES, LANES)
            yield (
                lambda out, turn, core=core: out.at[core, :, pl.ds(place * LANES, LANES)],
                target.at[:, where],
            )

    def rows_of(target, index, count):
        for core in range(CORES):
            where = pl.ds((core * count + index) * LANES, LANES)
            yield (lambda out, turn, core=core: turn.at[core], target.at[where])

    order = [index for index in range(units) if index not in CLIMBS]
    for index, place in CLIMBS.items():
        order.insert(place, index)
    for index in order:
        stores = [
            *columns_of(out_left, index, units, 0),
            *columns_of(out_right, index, units, 1),
            *rows_of(out_down, index, units),
        ]
        lists.append((p_f, index, 0, stores, True))
    for index in range(heads):
        stores = []
        for place, target in enumerate((out_query, out_key, out_value)):
            stores += columns_of(target, index, heads, place)
        lists.append((p_qkv, index, 1, stores, False))
        stores = [*columns_of(out_gate, index, heads, 0), *rows_of(out_out, index, heads)]
        lists.append((p_go, index, 2, stores, True))
    lists.append((p_gain, 0, 3, [], False))
    for at, (source, index, kind, stores, turned) in enumerate(lists):
        wide = source.shape[-1]
        if kind == 0 and index in CLIMBS:
            nth = list(CLIMBS).index(index)
            chunks.append(
                Climb(
                    here,
                    source.at[index],
                    *[buffer.at[nth] for buffer in side],
                    stores,
                    (
                        side_own,
                        side_climb,
                        side_sum,
                        side_land,
                        out_slot.at[at % 2],
                        turn_slot.at[at % 2],
                        side_pass,
                        side_pass_sum,
                    ),
                    (send.at[at], receive.at[at], local.at[at]),
                )
            )
            continue
        slots = [
            slot.at[(at % slot.shape[0],) + (slice(None),) * (len(slot.shape) - 2) + (pl.ds(0, wide),)]
            for slot in (own_slot, cross_slot, sum_slot, land_slot, out_slot)
        ]
        slots.append(turn_slot.at[at % 2] if turned else None)
        slots.append(pass_slot.at[:, :, pl.ds(0, wide)])
        chunks.append(
            Reduce(
                here,
                source.at[index],
                crossed[kind].at[index],
                landed[kind].at[index],
                passed[kind].at[index],
                stores,
                slots,
                (send.at[at], receive.at[at], local.at[at]),
            )
        )
    reducer = Reducer(chunks, [(kind, index) for _, index, kind, _, _ in lists])

    def load(source, target, at):
        return pltpu.make_async_copy(source, target, load_sem.at[at])

    loads = {
        "normed_ffn": load(normed_ffn_hbm, normed, 0),
        "upstream": load(upstream_hbm, upstream, 1),
        "part": load(partial_hbm.at[pl.ds(here.k * half, half)], part, 2),
        "normed": load(normed_hbm, normed, 3),
    }
    acts = [load(act_hbm.at[at], act.at[at % 2], 4 + at % 2) for at in range(units)]
    head_loads = [
        (
            load(saved_hbm.at[at], saved.at[0], 6),
            load(values_hbm.at[at], values.at[0], 8),
            load(weights_hbm.at[at], weights.at[0, :, pl.ds(0, 3 * LANES)], 10),
            load(weights_go_hbm.at[at], weights.at[0, :, pl.ds(3 * LANES, 2 * LANES)], 13),
        )
        for at in range(heads)
    ]
    loads["normed_ffn"].start()
    acts[0].start()
    loads["upstream"].start()
    loads["part"].start()

    def swap_beside(source, at):
        return remote(source, part_in, row_send.at[12 + at], row_receive.at[12 + at], sibling)

    def swap_across(batch, at):
        block = pl.ds(batch * part_rows, part_rows)
        return remote(
            across.at[block],
            across_in.at[block],
            row_send.at[15 + 2 * at + batch],
            row_receive.at[15 + 2 * at + batch],
            other,
        )

    beside = swap_beside(partial_hbm.at[pl.ds((1 - here.k) * half, half)], 0)
    beside.start()

    per_block = 2 * LANES
    group = per_block // (CORES * p_f.shape[4])
    turns = mids // group

    def store_block(slot, at, first, value):
        layer, chip = lax.div(at, turns), lax.rem(at, turns) * group
        shaped = value.astype(bf16).reshape(group, CORES, p_f.shape[4], value.shape[-1])
        stage[slot, layer, pl.ds(chip, group), :, :, pl.ds(first, value.shape[-1])] = shaped

    def stage_out(slot, target):
        wide = target.shape[-1]
        return pltpu.make_async_copy(
            stage.at[slot, :, :, :, :, pl.ds(0, wide)], target, stage_sem.at[slot]
        )

    pending = [None, None]

    def send_stage(slot, target, kind, index):
        copy = stage_out(slot, target.at[index])
        copy.start()
        pending[slot] = (copy, (kind, index))

    def flush(slot):
        if pending[slot] is not None:
            copy, key = pending[slot]
            copy.wait()
            pending[slot] = None
            reducer.produce(key)

    def unit_chunk(at):
        slot = at % 2
        if at + 1 < units:
            acts[at + 1].start()
        acts[at].wait()
        flush(slot)

        @pl.loop(0, width // per_block)
        def _(block):
            where = pl.ds(pl.multiple_of(block * per_block, per_block), per_block)
            store_block(slot, block, 0, dots(normed[:, where], act[slot, :, : 2 * LANES], 0, 0))
            store_block(
                slot, block, 2 * LANES, dots(upstream[:, where], act[slot, :, 2 * LANES :], 0, 0)
            )

        flush(1 - slot)
        send_stage(slot, p_f, 0, at)
        if at < 2:
            flush(slot)

    step_rows = 16

    def row_loop(count):
        return pl.loop(0, count // step_rows)

    def at_rows(base, index):
        return pl.ds(pl.multiple_of(base + index * step_rows, step_rows), step_rows)

    def reduce_beside(own):
        def leave(batch):
            @row_loop(part_rows)
            def _(index):
                base = batch * length + (1 - here.t) * part_rows
                value = own(base, index) + part_in[at_rows(base, index), :].astype(f32)
                across[at_rows(batch * part_rows, index), :] = value.astype(bf16)

        def keep(batch):
            @row_loop(part_rows)
            def _(index):
                base = batch * length + here.t * part_rows
                value = own(base, index) + part_in[at_rows(base, index), :].astype(f32)
                kept[at_rows(batch * part_rows, index), :] = value

        return leave, keep

    loads["normed_ffn"].wait()
    loads["upstream"].wait()
    unit_chunk(0)
    unit_chunk(1)
    down = lax.broadcasted_iota(jnp.int32, (length, length), 0)
    right = lax.broadcasted_iota(jnp.int32, (length, length), 1)
    offset = (down - right).astype(f32)
    for head in range(heads):
        decay = jnp.exp(-rates[head] * jnp.maximum(offset, 0.0))
        table[head] = jnp.where(down >= right, decay, 0.0)
    for sequence in range(rows // length):
        marks = onehot[pl.ds(sequence * length, length), :]
        same[sequence] = dots(marks, marks, 1, 1)

    loads["part"].wait()
    beside.wait_recv()
    leave, keep = reduce_beside(lambda base, index: part[at_rows(base, index), :].astype(f32))
    crossings = [swap_across(batch, 0) for batch in range(2)]
    for batch in range(2):
        leave(batch)
        crossings[batch].start()
    for batch in range(2):
        keep(batch)
    for at in range(2, 6):
        unit_chunk(at)
        if at % 2 == 1:
            reducer.tick()
    columns[...] = jnp.zeros_like(columns)
    rows_go = Spread(here, grad_out, part_rows, row_send.at[pl.ds(0, 6)], row_receive.at[pl.ds(0, 6)])
    rows_dot = Spread(here, dot_sum, part_rows, row_send.at[pl.ds(6, 6)], row_receive.at[pl.ds(6, 6)])

    for batch in range(2):
        crossings[batch].wait_recv()
        base = here.row(here.k, batch, here.t, part_rows)

        @row_loop(part_rows)
        def _(index):
            here_rows = at_rows(batch * part_rows, index)
            grad = kept[here_rows, :] + across_in[here_rows, :].astype(f32)
            mid = middle[here_rows, :]
            scale = lax.rsqrt(jnp.mean(mid * mid, axis=-1, keepdims=True) + EPSILON)
            unit = mid * scale
            weighted = grad * unit
            columns[1] += weighted[:8] + weighted[8:]
            scaled = grad * gains[1:2, :]
            slope = cotangent[here_rows, :].astype(f32) + scale * (
                scaled - unit * jnp.mean(scaled * unit, axis=-1, keepdims=True)
            )
            grad_middle[here_rows, :] = slope
            rounded = slope.astype(bf16)
            grad_out[at_rows(base, index), :] = rounded
            attended = mid - tokens[here_rows, :].astype(f32)
            inner = jnp.mean(rounded.astype(f32) * attended, axis=-1, keepdims=True)
            dot_sum[at_rows(base, index), :] = jnp.broadcast_to(inner, (step_rows, LANES))

        rows_go.start(batch)
        rows_dot.start(batch)
    for at in range(6, 9):
        unit_chunk(at)
        if at == 7:
            reducer.tick()
    rows_go.forward()
    rows_dot.forward()
    for at in range(9, units):
        unit_chunk(at)
    for copy in head_loads[0]:
        copy.start()
    loads["normed"].start()
    reducer.tick()
    rows_go.arrive()
    rows_dot.arrive()
    loads["normed"].wait()
    beside.wait_send()
    beside = swap_beside(result_hbm.at[pl.ds((1 - here.k) * half, half)], 1)
    beside.start()
    load_part = load(result_hbm.at[pl.ds(here.k * half, half)], part, 2)
    load_part.start()

    for head in range(heads):
        for copy in head_loads[head]:
            copy.wait()

        @pl.loop(0, rows // length)
        def _(sequence):
            where = pl.ds(pl.multiple_of(sequence * length, length), length)
            query_pre = saved[0, where, 0:LANES]
            key_pre = saved[0, where, LANES : 2 * LANES]
            gate = saved[0, where, 2 * LANES : 3 * LANES]
            scale = inverse[where, :]
            unit = saved[0, where, 3 * LANES : 4 * LANES] * scale
            grad_branch = dots(grad_out[where, :], weights[0, :, 4 * LANES :], 1, 0)
            grad_unit = grad_branch * gate
            branch[where, :] = (unit * gate).astype(bf16)
            projected[where, 3 * LANES :] = (grad_branch * unit).astype(bf16)
            grad_mixed = (scale * (grad_unit - unit * dot_sum[where, :])).astype(bf16)
            query_gate = 1.0 / (1.0 + jnp.exp(-query_pre))
            key_gate = 1.0 / (1.0 + jnp.exp(-key_pre))
            queries = (query_pre * query_gate).astype(bf16)
            keys = (key_pre * key_gate).astype(bf16)
            masked = table[head] * same[sequence]
            mixing = (dots(queries, keys, 1, 1) * masked).astype(bf16)
            grad_scores = (
                dots(grad_mixed, values[0, where, :], 1, 1) * masked
            ).astype(bf16)
            grad_queries = dots(grad_scores, keys, 1, 0)
            grad_keys = dots(grad_scores, queries, 0, 0)
            projected[where, 0:LANES] = (
                grad_queries * (query_gate * (1.0 + query_pre * (1.0 - query_gate)))
            ).astype(bf16)
            projected[where, LANES : 2 * LANES] = (
                grad_keys * (key_gate * (1.0 + key_pre * (1.0 - key_gate)))
            ).astype(bf16)
            projected[where, 2 * LANES : 3 * LANES] = dots(mixing, grad_mixed, 0, 0).astype(bf16)
            product = dots(projected[where, :], weights[0, :, : 4 * LANES], 1, 1)
            if head == 0:
                total[where, :] = product
            else:
                total[where, :] += product

        if head + 1 < heads:
            for copy in head_loads[head + 1]:
                copy.start()
        flush(0)
        flush(1)
        reducer.tick()

        @pl.loop(0, width // per_block)
        def _(block):
            where = pl.ds(pl.multiple_of(block * per_block, per_block), per_block)
            product = dots(normed[:, where], projected[...], 0, 0)
            store_block(0, block, 0, product[:, : 3 * LANES])
            store_block(1, block, 0, product[:, 3 * LANES :])
            store_block(1, block, LANES, dots(grad_out[:, where], branch[...], 0, 0))

        send_stage(0, p_qkv, 1, head)
        send_stage(1, p_go, 2, head)
        if head == heads - 1:
            beside.wait_send()

            @row_loop(half)
            def _(index):
                part[at_rows(0, index), :] = total[
                    at_rows((1 - here.k) * half, index), :
                ].astype(bf16)

            pl.semaphore_wait(free.at[0], 1)
            beside = swap_beside(part, 2)
            beside.start()
        flush(0)
        flush(1)
        if head == 0:
            load_part.wait()
            beside.wait_recv()
            leave, keep = reduce_beside(
                lambda base, index: part[at_rows(base, index), :].astype(f32)
            )
            for crossing in crossings:
                crossing.wait_send()
            crossings = [swap_across(batch, 1) for batch in range(2)]
            for batch in range(2):
                leave(batch)
                crossings[batch].start()
            for batch in range(2):
                keep(batch)
            pl.semaphore_signal(free.at[0], inc=1, device_id=sibling, device_id_type=MESH)
        if head == 2:
            for crossing in crossings:
                crossing.wait_recv()
                crossing.wait_send()

            @row_loop(2 * part_rows)
            def _(index):
                here_rows = at_rows(0, index)
                value = kept[here_rows, :] + across_in[here_rows, :].astype(f32)
                across[here_rows, :] = (middle[here_rows, :] + value).astype(bf16)

            store_result = load(across, result, 12)
            store_result.start()
            pl.semaphore_signal(free.at[1], inc=1, device_id=other, device_id_type=MESH)
        reducer.tick()

    beside.wait_recv()
    leave, keep = reduce_beside(
        lambda base, index: total[at_rows(here.k * half + base, index), :]
    )
    crossings = [swap_across(batch, 2) for batch in range(2)]
    store_result.wait()
    pl.semaphore_wait(free.at[1], 1)
    for batch in range(2):
        leave(batch)
        crossings[batch].start()
    for batch in range(2):
        keep(batch)
    reducer.tick()
    for batch in range(2):
        crossings[batch].wait_recv()

        @row_loop(part_rows)
        def _(index):
            here_rows = at_rows(batch * part_rows, index)
            grad = kept[here_rows, :] + across_in[here_rows, :].astype(f32)
            value = tokens[here_rows, :].astype(f32)
            scale = lax.rsqrt(jnp.mean(value * value, axis=-1, keepdims=True) + EPSILON)
            unit = value * scale
            weighted = grad * unit
            columns[0] += weighted[:8] + weighted[8:]
            scaled = grad * gains[0:1, :]
            grad_tokens[here_rows, :] = grad_middle[here_rows, :] + scale * (
                scaled - unit * jnp.mean(scaled * unit, axis=-1, keepdims=True)
            )

    lane = lax.broadcasted_iota(jnp.int32, (8, LANES), 1)

    @pl.loop(0, width // per_block)
    def _(block):
        where = pl.ds(pl.multiple_of(block * per_block, per_block), per_block)
        first = jnp.where(lane == 0, 1.0, 0.0).astype(bf16)
        second = jnp.where(lane == 1, 1.0, 0.0).astype(bf16)
        value = dots(columns[0, :, where].astype(bf16), first, 0, 0)
        value += dots(columns[1, :, where].astype(bf16), second, 0, 0)
        store_block(0, block, 0, value)

    send_stage(0, p_gain, 3, 0)
    flush(0)
    reducer.drain()
    gain_sum = chunks[-1].out_slot[0] + chunks[-1].out_slot[1]
    gain_slot[0] = gain_sum
    gain_copy = remote(
        gain_slot.at[0], gain_slot.at[1], row_send.at[21], row_receive.at[21], other
    )
    gain_copy.start()
    gain_copy.wait_recv()
    out_gain[...] = (gain_sum + gain_slot[1]).T[:8]
    gain_copy.wait_send()
    beside.wait_send()
    for crossing in crossings:
        crossing.wait_send()
    rows_go.finish()
    rows_dot.finish()


def backward(mids, small, large):
    f32, bf16 = jnp.float32, jnp.bfloat16
    shape = jax.ShapeDtypeStruct
    rates, onehot, gains, inverse, tokens, middle, cotangent = small
    normed_ffn, upstream, normed, act, partial, result, saved, values, weights, weights_go = large
    rows, width = normed.shape
    heads, units = saved.shape[0], act.shape[0]
    block_rows = width // (LAYERS * mids * CORES)
    widths = ((units, 3 * LANES), (heads, 3 * LANES), (heads, 2 * LANES), (1, LANES))
    chunks = sum(count for count, _ in widths)
    hops = Reduce.semaphores(mids)
    anywhere = pl.BlockSpec(memory_space=pl.ANY)
    vmem = pl.BlockSpec(memory_space=pltpu.VMEM)
    smem = pl.BlockSpec(memory_space=pltpu.SMEM)
    widest = 3 * LANES
    half, own = rows // CORES, rows // (2 * CORES)
    length = own
    inner, outer = CORES * heads * LANES, CORES * units * LANES
    outs = [shape((block_rows, inner), f32)] * 4 + [shape((inner, block_rows), f32)]
    outs += [shape((block_rows, outer), f32)] * 2 + [shape((outer, block_rows), f32)]
    outs.append(shape((8, block_rows), f32))
    passed = [shape((count, CORES, block_rows, wide), bf16) for count, wide in widths]
    sums = [shape((count, LAYERS, mids, CORES, block_rows, wide), bf16) for count, wide in widths]
    cross = [
        shape((count, mids - 1, LAYERS, CORES, block_rows, wide), bf16) for count, wide in widths
    ]
    land = [shape((count, CORES, LAYERS, block_rows, wide), bf16) for count, wide in widths]
    few = max(len(CLIMBS), 1)
    side = [
        shape((few, LAYERS, mids, CORES, block_rows, widest), bf16),
        shape((few, CORES, mids, block_rows, widest), bf16),
        shape((few, mids, CORES, block_rows, widest), bf16),
    ]
    return pl.pallas_call(
        functools.partial(backward_kernel, mids),
        name="backward",
        out_shape=(*outs, shape((own, width), f32), shape((own, width), bf16), *sums, *cross, *land, *passed, *side),
        in_specs=[smem] + [vmem] * 6 + [anywhere] * 10,
        out_specs=(anywhere,) * 8 + (vmem,) * 2 + (anywhere,) * 20,
        scratch_shapes=[
            pltpu.VMEM((rows, width), bf16),
            pltpu.VMEM((rows, width), bf16),
            pltpu.VMEM((rows, width), bf16),
            pltpu.VMEM((2, rows, widest), bf16),
            pltpu.VMEM((2, LAYERS, mids, CORES, block_rows, widest), bf16),
            pltpu.VMEM((1, LAYERS, CORES, block_rows, widest), bf16),
            pltpu.VMEM((1, mids - 1, LAYERS, CORES, block_rows, widest), bf16),
            pltpu.VMEM((SUMS, LAYERS, CORES, block_rows, widest), bf16),
            pltpu.VMEM((1, CORES, LAYERS, block_rows, widest), bf16),
            pltpu.VMEM((2, CORES, block_rows, widest), f32),
            pltpu.VMEM((2, CORES, LANES, block_rows), f32),
            pltpu.VMEM((CORES, block_rows, widest), bf16),
            pltpu.VMEM((2, block_rows, LANES), f32),
            pltpu.VMEM((mids, CORES, block_rows, widest), bf16),
            pltpu.VMEM((LAYERS, mids, CORES, block_rows, widest), bf16),
            pltpu.VMEM((mids, CORES, block_rows, widest), bf16),
            pltpu.VMEM((CORES, mids, block_rows, widest), bf16),
            pltpu.VMEM((mids, CORES, block_rows, widest), bf16),
            pltpu.VMEM((mids, CORES, block_rows, widest), bf16),
            pltpu.VMEM((1, rows, 4 * LANES), f32),
            pltpu.VMEM((1, rows, LANES), bf16),
            pltpu.VMEM((1, width, 5 * LANES), bf16),
            pltpu.VMEM((rows, 4 * LANES), bf16),
            pltpu.VMEM((rows, LANES), bf16),
            pltpu.VMEM((rows, width), f32),
            pltpu.VMEM((half, width), bf16),
            pltpu.VMEM((half, width), bf16),
            pltpu.VMEM((own, width), bf16),
            pltpu.VMEM((own, width), bf16),
            pltpu.VMEM((own, width), f32),
            pltpu.VMEM((own, width), f32),
            pltpu.VMEM((rows, LANES), f32),
            pltpu.VMEM((heads, length, length), f32),
            pltpu.VMEM((rows // length, length, length), f32),
            pltpu.VMEM((2, 8, width), f32),
            pltpu.SemaphoreType.DMA((chunks, hops)),
            pltpu.SemaphoreType.DMA((chunks, hops)),
            pltpu.SemaphoreType.DMA((chunks, 12)),
            pltpu.SemaphoreType.DMA((22,)),
            pltpu.SemaphoreType.DMA((22,)),
            pltpu.SemaphoreType.DMA((15,)),
            pltpu.SemaphoreType.DMA((2,)),
            pltpu.SemaphoreType.REGULAR((2,)),
        ],
        compiler_params=pltpu.CompilerParams(
            collective_id=1, has_side_effects=True, vmem_limit_bytes=63 * 2**20
        ),
    )(*small, *large)[:11]


class Gatherer:
    def __init__(self, chunks):
        self.chunks = chunks
        self.started = self.crossed = self.passed = self.climbed = 0

    def relay_on(self, last):
        while self.climbed < last:
            self.chunks[self.climbed].relay_on()
            self.climbed += 1

    def relay(self, at):
        if at < len(self.chunks) and self.passed == at:
            self.chunks[at].relay()
            self.passed += 1

    def launch(self):
        while self.started < min(len(self.chunks), self.crossed + BEFORE + 1):
            self.chunks[self.started].start()
            self.started += 1

    def cross(self, count=1):
        for _ in range(count):
            if self.crossed < len(self.chunks):
                self.relay(self.crossed)
                self.chunks[self.crossed].cross()
                self.crossed += 1
                self.launch()
                self.relay(self.crossed)
                self.relay_on(self.crossed - 1)

    def arrive(self, at):
        self.cross(at + 1 - self.crossed)
        self.relay_on(at + 1)
        self.chunks[at].arrive()


def forward_kernel(mids, *refs):
    f32, bf16 = jnp.float32, jnp.bfloat16
    (
        rates,
        own_marks,
        tokens,
        cotangent,
        shard_g,
        shard_go,
        shard_qkv,
        shard_f,
        full_g,
        full_go,
        full_qkv,
        full_f,
        normed_hbm,
        normed_ffn_hbm,
        upstream_hbm,
        act_hbm,
        partial_hbm,
        result_hbm,
        saved_hbm,
        values_hbm,
        marks,
        gains,
        inverse,
        middle,
        normed,
        normed_ffn,
        upstream,
        total,
        grad_total,
        weights,
        out_weights,
        saved,
        values,
        act,
        branch,
        part,
        part_in,
        across,
        across_in,
        kept,
        squares,
        squares_in,
        squares_across,
        squares_across_in,
        table,
        same,
        gain_columns,
        send,
        receive,
        local,
        row_send,
        row_receive,
        load_sem,
        store_sem,
    ) = refs
    rows, width = normed.shape
    half = rows // CORES
    part_rows = half // 4
    length = 2 * part_rows
    heads, units = full_qkv.shape[0], full_f.shape[0]
    here = Place(mids)
    sibling = here.device(here.z, here.m, 1 - here.k)
    other = (here.device(here.z, here.m, here.k)[0], 1 - here.t)
    greet(here.weight_peers() + [other])

    chunks = []
    pairs = [(shard_g, full_g, 0)]
    for index in range(heads):
        pairs += [(shard_go, full_go, index), (shard_qkv, full_qkv, index)]
    pairs += [(shard_f, full_f, index) for index in range(units)]
    for at, (source, target, index) in enumerate(pairs):
        chunks.append(
            Gather(
                here,
                source.at[index],
                target.at[index],
                (send.at[at], receive.at[at], local.at[at]),
                at in SIDEWAYS,
            )
        )
    gatherer = Gatherer(chunks)
    gatherer.launch()

    step_rows = 16

    def row_loop(count):
        return pl.loop(0, count // step_rows)

    def at_rows(base, index):
        return pl.ds(pl.multiple_of(base + index * step_rows, step_rows), step_rows)

    def spread(buffer, at):
        window = pl.ds(6 * at, 6)
        return Spread(here, buffer, part_rows, row_send.at[window], row_receive.at[window])

    rows_normed, rows_up = spread(normed, 0), spread(upstream, 1)
    rows_ffn, rows_inverse = spread(normed_ffn, 2), spread(inverse, 3)
    lone = lambda source, target, at, peer: remote(
        source, target, row_send.at[24 + at], row_receive.at[24 + at], peer
    )

    own_half = pl.ds(pl.multiple_of(here.k * half, half), half)
    far_half = pl.ds(pl.multiple_of((1 - here.k) * half, half), half)
    marks[own_half, :] = own_marks[...]
    marks_copy = lone(own_marks, marks.at[own_half], 0, sibling)
    marks_copy.start()

    gatherer.arrive(0)
    load_gain = pltpu.make_async_copy(full_g.at[0], gain_columns, load_sem.at[0])
    load_gain.start()
    load_gain.wait()
    down = lax.broadcasted_iota(jnp.int32, (8, LANES), 0)
    right = lax.broadcasted_iota(jnp.int32, (8, LANES), 1)
    pick = jnp.where(down == right, 1.0, 0.0).astype(bf16)
    gains[...] = dots(pick, gain_columns[...].reshape(width, LANES), 1, 1)

    for batch in range(2):
        base = here.row(here.k, batch, here.t, part_rows)

        @row_loop(part_rows)
        def _(index):
            here_rows = at_rows(batch * part_rows, index)
            value = tokens[here_rows, :].astype(f32)
            scale = lax.rsqrt(jnp.mean(value * value, axis=-1, keepdims=True) + EPSILON)
            normed[at_rows(base, index), :] = (value * scale * gains[0:1, :]).astype(bf16)

        rows_normed.start(batch)
    for batch in range(2):
        base = here.row(here.k, batch, here.t, part_rows)
        upstream[pl.ds(base, part_rows), :] = cotangent[pl.ds(batch * part_rows, part_rows), :]
        rows_up.start(batch)

    down = lax.broadcasted_iota(jnp.int32, (length, length), 0)
    right = lax.broadcasted_iota(jnp.int32, (length, length), 1)
    offset = (down - right).astype(f32)
    for head in range(heads):
        decay = jnp.exp(-rates[head] * jnp.maximum(offset, 0.0))
        table[head] = jnp.where(down >= right, decay, 0.0)
    marks_copy.wait_recv()
    for sequence in range(rows // length):
        mark = marks[pl.ds(sequence * length, length), :]
        same[sequence] = dots(mark, mark, 1, 1)
    squares[...] = jnp.zeros_like(squares)

    def weight(slot, first, last):
        return weights[slot, :, :, :, :, first * LANES : last * LANES].reshape(
            width, (last - first) * LANES
        )

    def store(source, target, at):
        copy = pltpu.make_async_copy(source, target, store_sem.at[at])
        copy.start()
        return copy

    stores = []
    gatherer.cross()
    rows_normed.forward()
    rows_normed.arrive()
    stores.append(store(normed, normed_hbm, 0))
    gatherer.cross()
    rows_up.forward()

    pending = [[], []]
    for head in range(heads):
        slot = head % 2
        gatherer.cross(3 + 2 * head + LEAD - gatherer.crossed)
        gatherer.arrive(1 + 2 * head)
        load_out = pltpu.make_async_copy(
            full_go.at[head, :, :, :, :, pl.ds(LANES, LANES)],
            out_weights.at[:, :, :, :, pl.ds(head * LANES, LANES)],
            load_sem.at[4 + head],
        )
        load_gate = pltpu.make_async_copy(
            full_go.at[head, :, :, :, :, pl.ds(0, LANES)],
            weights.at[slot, :, :, :, :, pl.ds(3 * LANES, LANES)],
            load_sem.at[2 + slot],
        )
        load_gate.start()
        gatherer.cross(3 + 2 * head + LEAD - gatherer.crossed)
        gatherer.arrive(2 + 2 * head)
        load = pltpu.make_async_copy(
            full_qkv.at[head],
            weights.at[slot, :, :, :, :, pl.ds(0, 3 * LANES)],
            load_sem.at[slot],
        )
        load.start()
        load_out.start()
        for copy in pending[slot]:
            copy.wait()
        load_gate.wait()
        load.wait()

        @pl.loop(0, rows // length)
        def _(sequence):
            where = pl.ds(pl.multiple_of(sequence * length, length), length)
            product = dots(normed[where, :], weight(slot, 0, 4), 1, 0)
            query_pre, key_pre = product[:, :LANES], product[:, LANES : 2 * LANES]
            value = product[:, 2 * LANES : 3 * LANES].astype(bf16)
            gate = product[:, 3 * LANES :]
            queries = (query_pre / (1.0 + jnp.exp(-query_pre))).astype(bf16)
            keys = (key_pre / (1.0 + jnp.exp(-key_pre))).astype(bf16)
            masked = table[head] * same[sequence]
            mixing = (dots(queries, keys, 1, 1) * masked).astype(bf16)
            mixed = dots(mixing, value, 1, 0)
            saved[slot, where, : 2 * LANES] = product[:, : 2 * LANES]
            saved[slot, where, 2 * LANES : 3 * LANES] = gate
            saved[slot, where, 3 * LANES :] = mixed
            values[slot, where, :] = value
            branch[where, head * LANES : (head + 1) * LANES] = (mixed * gate).astype(bf16)
            squares[where, :] += jnp.broadcast_to(
                jnp.sum(mixed * mixed, axis=-1, keepdims=True), (length, LANES)
            )

        pending[slot] = [
            store(saved.at[slot], saved_hbm.at[head], 4 + slot),
            store(values.at[slot], values_hbm.at[head], 6 + slot),
        ]
        load_out.wait()
    stores += pending[0] + pending[1]

    @pl.loop(0, half // length)
    def _(block):
        base = (1 - here.k) * half + block * length
        where = pl.ds(pl.multiple_of(base, length), length)
        to = pl.ds(pl.multiple_of(block * length, length), length)
        part[to, :] = dots(branch[where, :], out_weights[...].reshape(width, -1), 1, 1).astype(bf16)

    beside = lone(part, part_in, 1, sibling)
    beside.start()
    beside_squares = lone(squares.at[far_half], squares_in, 2, sibling)
    beside_squares.start()

    @pl.loop(0, half // length)
    def _(block):
        base = here.k * half + block * length
        where = pl.ds(pl.multiple_of(base, length), length)
        total[where, :] = dots(branch[where, :], out_weights[...].reshape(width, -1), 1, 1)

    beside.wait_recv()
    beside_squares.wait_recv()
    crossings = []
    for batch in range(2):
        block = pl.ds(batch * part_rows, part_rows)
        crossings.append(
            (
                lone(across.at[block], across_in.at[block], 3 + batch, other),
                lone(squares_across.at[block], squares_across_in.at[block], 5 + batch, other),
            )
        )

        @row_loop(part_rows)
        def _(index):
            base = batch * length + (1 - here.t) * part_rows
            value = total[at_rows(here.k * half + base, index), :]
            value += part_in[at_rows(base, index), :].astype(f32)
            to = at_rows(batch * part_rows, index)
            across[to, :] = value.astype(bf16)
            squares_across[to, :] = (
                squares[at_rows(here.k * half + base, index), :]
                + squares_in[at_rows(base, index), :]
            )

        for copy in crossings[batch]:
            copy.start()
    for batch in range(2):

        @row_loop(part_rows)
        def _(index):
            base = batch * length + here.t * part_rows
            value = total[at_rows(here.k * half + base, index), :]
            to = at_rows(batch * part_rows, index)
            kept[to, :] = value + part_in[at_rows(base, index), :].astype(f32)

    gatherer.cross()
    rows_up.arrive()
    stores.append(store(upstream, upstream_hbm, 1))
    for batch in range(2):
        for copy in crossings[batch]:
            copy.wait_recv()
        base = here.row(here.k, batch, here.t, part_rows)

        @row_loop(part_rows)
        def _(index):
            here_rows = at_rows(batch * part_rows, index)
            from_rows = batch * length + here.t * part_rows
            square = (
                squares[at_rows(here.k * half + from_rows, index), :]
                + squares_in[at_rows(from_rows, index), :]
                + squares_across_in[here_rows, :]
            )
            scale = lax.rsqrt(square / width + EPSILON)
            inverse[at_rows(base, index), :] = scale
            attended = (kept[here_rows, :] + across_in[here_rows, :].astype(f32)) * scale[:, :1]
            mid = tokens[here_rows, :].astype(f32) + attended
            middle[here_rows, :] = mid
            scale = lax.rsqrt(jnp.mean(mid * mid, axis=-1, keepdims=True) + EPSILON)
            normed_ffn[at_rows(base, index), :] = (mid * scale * gains[1:2, :]).astype(bf16)

        rows_ffn.start(batch)
        rows_inverse.start(batch)
    gatherer.cross()
    rows_ffn.forward()
    rows_inverse.forward()
    gatherer.cross()
    rows_ffn.arrive()
    rows_inverse.arrive()
    stores.append(store(normed_ffn, normed_ffn_hbm, 2))

    pending = [None, None]
    for at in range(units):
        slot = at % 2
        gatherer.cross(2 + 2 * heads + at + 1 - gatherer.crossed)
        gatherer.arrive(1 + 2 * heads + at)
        load = pltpu.make_async_copy(
            full_f.at[at], weights.at[slot, :, :, :, :, pl.ds(0, 3 * LANES)], load_sem.at[slot]
        )
        load.start()
        if pending[slot] is not None:
            pending[slot].wait()
        gatherer.cross()
        if at == units - 1:
            for copy in stores:
                copy.wait()
            rows_normed.finish()
            rows_ffn.finish()
        load.wait()

        @pl.loop(0, rows // length)
        def _(block):
            where = pl.ds(pl.multiple_of(block * length, length), length)
            product = dots(normed_ffn[where, :], weight(slot, 0, 2), 1, 0)
            left, right = product[:, :LANES], product[:, LANES:]
            grad_joined = dots(upstream[where, :], weight(slot, 2, 3), 1, 0)
            act[slot, where, :LANES] = (grad_joined * right).astype(bf16)
            act[slot, where, LANES : 2 * LANES] = (grad_joined * left).astype(bf16)
            act[slot, where, 2 * LANES :] = (left * right).astype(bf16)
            out = dots(act[slot, where, 2 * LANES :], weight(slot, 2, 3), 1, 1)
            grad = dots(act[slot, where, : 2 * LANES], weight(slot, 0, 2), 1, 1)
            if at == 0:
                total[where, :] = out
                grad_total[where, :] = grad
            elif at == units - 1:
                normed[where, :] = (total[where, :] + out).astype(bf16)
                normed_ffn[where, :] = (grad_total[where, :] + grad).astype(bf16)
            else:
                total[where, :] += out
                grad_total[where, :] += grad

        pending[slot] = store(act.at[slot], act_hbm.at[at], 8 + slot)

    grads = store(normed_ffn, partial_hbm, 0)
    outs = store(normed, result_hbm, 1)
    for copy in pending + [grads, outs]:
        copy.wait()
    for chunk in chunks:
        chunk.finish()
    rows_up.finish()
    rows_inverse.finish()
    marks_copy.wait_send()
    beside.wait_send()
    beside_squares.wait_send()
    for pair in crossings:
        for copy in pair:
            copy.wait_send()


def forward(mids, rates, marks, tokens, cotangent, shards):
    f32, bf16 = jnp.float32, jnp.bfloat16
    shape = jax.ShapeDtypeStruct
    own, width = tokens.shape
    rows, half = 4 * own, 2 * own
    length = own
    heads, units = shards[1].shape[0], shards[3].shape[0]
    block_rows = shards[0].shape[2]
    full = [shape((w.shape[0], LAYERS, mids) + w.shape[1:], bf16) for w in shards]
    chunks = 1 + 2 * heads + units
    hops = Gather.semaphores(mids)
    anywhere = pl.BlockSpec(memory_space=pl.ANY)
    vmem = pl.BlockSpec(memory_space=pltpu.VMEM)
    smem = pl.BlockSpec(memory_space=pltpu.SMEM)
    block = (LAYERS, mids, CORES, block_rows)
    return pl.pallas_call(
        functools.partial(forward_kernel, mids),
        name="forward",
        out_shape=(
            *full,
            *[shape((rows, width), bf16)] * 3,
            shape((units, rows, 3 * LANES), bf16),
            *[shape((rows, width), bf16)] * 2,
            shape((heads, rows, 4 * LANES), f32),
            shape((heads, rows, LANES), bf16),
            shape((rows, LANES), bf16),
            shape((8, width), f32),
            shape((rows, LANES), f32),
            shape((own, width), f32),
        ),
        in_specs=[smem] + [vmem] * 3 + [anywhere] * 4,
        out_specs=(anywhere,) * 12 + (vmem,) * 4,
        scratch_shapes=[
            pltpu.VMEM((rows, width), bf16),
            pltpu.VMEM((rows, width), bf16),
            pltpu.VMEM((rows, width), bf16),
            pltpu.VMEM((rows, width), f32),
            pltpu.VMEM((rows, width), f32),
            pltpu.VMEM((2, *block, 4 * LANES), bf16),
            pltpu.VMEM((*block, heads * LANES), bf16),
            pltpu.VMEM((2, rows, 4 * LANES), f32),
            pltpu.VMEM((2, rows, LANES), bf16),
            pltpu.VMEM((2, rows, 3 * LANES), bf16),
            pltpu.VMEM((rows, heads * LANES), bf16),
            pltpu.VMEM((half, width), bf16),
            pltpu.VMEM((half, width), bf16),
            pltpu.VMEM((own, width), bf16),
            pltpu.VMEM((own, width), bf16),
            pltpu.VMEM((own, width), f32),
            pltpu.VMEM((rows, LANES), f32),
            pltpu.VMEM((half, LANES), f32),
            pltpu.VMEM((own, LANES), f32),
            pltpu.VMEM((own, LANES), f32),
            pltpu.VMEM((heads, length, length), f32),
            pltpu.VMEM((rows // length, length, length), f32),
            pltpu.VMEM((*block, LANES), bf16),
            pltpu.SemaphoreType.DMA((chunks, hops)),
            pltpu.SemaphoreType.DMA((chunks, hops)),
            pltpu.SemaphoreType.DMA((chunks,)),
            pltpu.SemaphoreType.DMA((31,)),
            pltpu.SemaphoreType.DMA((31,)),
            pltpu.SemaphoreType.DMA((4 + heads,)),
            pltpu.SemaphoreType.DMA((10,)),
        ],
        compiler_params=pltpu.CompilerParams(
            collective_id=0, has_side_effects=True, vmem_limit_bytes=63 * 2**20
        ),
    )(rates, marks, tokens, cotangent, *shards)


def split_heads(weight, halves):
    return weight.reshape(weight.shape[0], CORES, -1, LANES)


def pack(parts):
    joined = jnp.concatenate([split_heads(part, CORES) for part in parts], axis=-1)
    return joined.transpose(2, 1, 0, 3)


def local(
    mids,
    tokens,
    segment_ids,
    decay_rates,
    gain_attn,
    w_query,
    w_key,
    w_value,
    w_gate,
    w_out,
    gain_ffn,
    w_left,
    w_right,
    w_down,
    cotangent,
):
    f32, bf16 = jnp.float32, jnp.bfloat16
    batches, local_rows, model_width = tokens.shape
    core = lax.rem(lax.axis_index("dp"), CORES)
    heads = decay_rates.shape[0] // CORES
    rates = lax.dynamic_slice_in_dim(decay_rates, core * heads, heads)
    own = lambda values: values.reshape(batches * local_rows, model_width)
    marks = (segment_ids.reshape(-1)[:, None] == jnp.arange(LANES)[None, :]).astype(bf16)
    gain_columns = jnp.pad(
        jnp.stack([gain_attn, gain_ffn], axis=1), ((0, 0), (0, LANES - 2))
    )
    shards = (
        jnp.stack([gain_columns] * CORES)[None],
        pack([w_gate, w_out.T]),
        pack([w_query, w_key, w_value]),
        pack([w_left, w_right, w_down.T]),
    )
    (
        _,
        full_go,
        full_qkv,
        _,
        normed,
        normed_ffn,
        upstream,
        act,
        partial,
        result,
        saved,
        values,
        marks,
        gains,
        inverse,
        middle,
    ) = forward(mids, rates, marks, own(tokens), own(cotangent), shards)
    full_go = full_go.reshape(heads, model_width, -1)
    full_qkv = full_qkv.reshape(heads, model_width, -1)
    *grads, grad_gains, grad_tokens, result = backward(
        mids,
        (rates, marks, gains, inverse, own(tokens), middle, own(cotangent)),
        (normed_ffn, upstream, normed, act, partial, result, saved, values, full_qkv, full_go),
    )
    result = result.reshape(tokens.shape)
    return (
        result,
        grad_tokens.reshape(tokens.shape),
        grad_gains[0],
        *grads[:5],
        grad_gains[1],
        *grads[5:],
    )


def solution(mesh):
    return jax.shard_map(
        functools.partial(local, mesh.shape["dp"] // (LAYERS * CORES)),
        mesh=mesh,
        in_specs=(
            P(None, ("dp", "tensor"), None),
            P(None, "dp"),
            P("tensor"),
            P("dp"),
            P("dp", "tensor"),
            P("dp", "tensor"),
            P("dp", "tensor"),
            P("dp", "tensor"),
            P("tensor", "dp"),
            P("dp"),
            P("dp", "tensor"),
            P("dp", "tensor"),
            P("tensor", "dp"),
            P(None, ("dp", "tensor"), None),
        ),
        out_specs=(
            P(None, ("dp", "tensor"), None),
            P(None, ("dp", "tensor"), None),
            P("dp"),
            P("dp", "tensor"),
            P("dp", "tensor"),
            P("dp", "tensor"),
            P("dp", "tensor"),
            P("tensor", "dp"),
            P("dp"),
            P("dp", "tensor"),
            P("dp", "tensor"),
            P("tensor", "dp"),
        ),
        check_vma=False,
    )
```

```python
import functools

import jax
import jax.numpy as jnp
from jax import lax
from jax.experimental import pallas as pl
from jax.experimental.pallas import tpu as pltpu
from jax.sharding import PartitionSpec as P

EPSILON = 1e-06
LAYERS = 4
CORES = 2
LANES = 128
AHEAD = 1
BEFORE = 4
LEAD = 3
SIDEWAYS = (9, 13)
SLICE = 32
CLIMBS = {0: 4}
EARLY = 6
NEAR = 2
LAG = 2
BEHIND = 2
SUMS = 6
FETCH = 5
MESH = pl.DeviceIdType.MESH


class Place:
    def __init__(self, mids):
        place = lax.axis_index("dp")
        self.mids = mids
        self.t = lax.axis_index("tensor")
        self.k = lax.rem(place, CORES)
        self.m = lax.rem(lax.div(place, CORES), mids)
        self.z = lax.div(place, CORES * mids)

    def device(self, z, m, k):
        return ((z * self.mids + m) * CORES + k, self.t)

    def layer(self, step):
        return lax.rem(self.z + step, LAYERS)

    def mid(self, step):
        return lax.rem(self.m + step, self.mids)

    def row(self, core, batch, half, part):
        return pl.multiple_of(((core * 2 + batch) * 2 + half) * part, part)

    def weight_peers(self):
        peers = [self.device(self.z, self.m, 1 - self.k)]
        for step in range(1, LAYERS):
            for core in range(CORES):
                peers.append(self.device(self.layer(step), self.m, core))
        for step in range(1, self.mids):
            for core in range(CORES):
                peers.append(self.device(self.z, self.mid(step), core))
        return peers


def greet(peers):
    barrier = pltpu.get_barrier_semaphore()
    for peer in peers:
        pl.semaphore_signal(barrier, inc=1, device_id=peer, device_id_type=MESH)
    pl.semaphore_wait(barrier, len(peers))


def remote(source, target, send, receive, peer):
    return pltpu.make_async_remote_copy(
        src_ref=source,
        dst_ref=target,
        send_sem=send,
        recv_sem=receive,
        device_id=peer,
        device_id_type=MESH,
    )


def apart(one, layer):
    near = jnp.logical_and(one - layer <= 2, layer - one <= 2)
    return jnp.logical_and(one != layer, near)


def relayed(here, layer):
    first, last = layer == 0, layer == LAYERS - 1
    if not (first or last):
        return None, None
    return (here == LAYERS - 2, LAYERS - 1) if first else (here == 1, 0)


class Gather:
    def __init__(self, place, source, target, sems, sideways):
        self.place, self.source, self.target = place, source, target
        self.send, self.receive, self.local = sems
        self.sideways = sideways
        here = place
        self.own = target.at[here.z, here.m, here.k]
        self.keep = pltpu.make_async_copy(source.at[here.k], self.own, self.local)
        self.beside = remote(
            source.at[1 - here.k],
            self.own,
            self.send.at[0],
            self.receive.at[0],
            here.device(here.z, here.m, 1 - here.k),
        )
        self.sides = 1 + LAYERS * CORES
        self.crosses = self.sides + (here.mids - 1) * CORES

    @staticmethod
    def semaphores(mids):
        return 1 + LAYERS * CORES + (mids - 1) * (CORES + LAYERS)

    def hop(self, layer, core, origin):
        here = self.place
        arrival = 1 + (here.z * CORES + here.k if origin is None else origin * CORES + core)
        return remote(
            self.source.at[core],
            self.own,
            self.send.at[1 + layer * CORES + core],
            self.receive.at[arrival],
            here.device(layer, here.m, core),
        )

    def pass_on(self, layer, core, goal):
        here = self.place
        block = self.target.at[layer, here.m, core]
        return remote(
            block,
            block,
            self.send.at[1 + here.z * CORES + core],
            self.receive.at[1 + layer * CORES + core],
            here.device(goal, here.m, here.k),
        )

    def side(self, step, core, wait):
        here = self.place
        at = self.sides + (step - 1) * CORES
        return remote(
            self.source.at[core],
            self.own,
            self.send.at[at + core],
            self.receive.at[at + (core if wait else here.k)],
            here.device(here.z, here.mid(step), core),
        )

    def crossing(self, step, layer):
        here = self.place
        at = self.crosses + (step - 1) * LAYERS + layer
        block = self.target.at[layer, here.m]
        return remote(
            block,
            block,
            self.send.at[at],
            self.receive.at[at],
            here.device(here.z, here.mid(step), here.k),
        )

    def start(self):
        here = self.place
        self.keep.start()
        self.beside.start()
        for step in range(1, here.mids):
            for core in range(CORES):
                self.side(step, core, False).start()
        for layer in range(LAYERS):

            @pl.when(apart(here.z, layer))
            def _():
                for core in range(CORES):
                    self.hop(layer, core, None).start()

    def relay(self):
        for layer in (0, LAYERS - 1):
            mine, goal = relayed(self.place.z, layer)

            @pl.when(mine)
            def _():
                for core in range(CORES):
                    self.hop(layer, core, layer).wait_recv()
                    self.pass_on(layer, core, goal).start()

    def climb(self, step, layer):
        here = self.place
        at = self.crosses + (step - 1) * LAYERS
        block = self.target.at[here.z, here.mid(step)]
        return remote(
            block,
            block,
            self.send.at[at + layer],
            self.receive.at[at + here.z],
            here.device(layer, here.m, here.k),
        )

    def climbed(self, step, layer, goal):
        here = self.place
        at = self.crosses + (step - 1) * LAYERS
        block = self.target.at[layer, here.mid(step)]
        return remote(
            block,
            block,
            self.send.at[at + here.z],
            self.receive.at[at + layer],
            here.device(goal, here.m, here.k),
        )

    def wait_layers(self, then):
        here = self.place
        for layer in range(LAYERS):
            awaited = here.z != layer
            mine, _ = relayed(here.z, layer)
            if mine is not None:
                awaited = jnp.logical_and(awaited, jnp.logical_not(mine))

            @pl.when(awaited)
            def _():
                for core in range(CORES):
                    self.hop(layer, core, layer).wait_recv()

            then(layer)

    def cross(self):
        here = self.place
        if self.sideways:
            for step in range(1, here.mids):
                for core in range(CORES):
                    self.side(step, core, True).wait_recv()
            for layer in range(LAYERS):

                @pl.when(apart(here.z, layer))
                def _():
                    for step in range(1, here.mids):
                        self.climb(step, layer).start()

            return

        def send_on(layer):
            @pl.when(here.z != layer)
            def _():
                for step in range(1, here.mids):
                    self.crossing(step, layer).start()

        self.wait_layers(send_on)

    def relay_on(self):
        if self.sideways:
            here = self.place
            for layer in (0, LAYERS - 1):
                mine, goal = relayed(here.z, layer)

                @pl.when(mine)
                def _():
                    for step in range(1, here.mids):
                        self.climbed(step, layer, goal).wait_recv()
                        self.climbed(step, layer, goal).start()

    def arrive(self):
        here = self.place
        self.keep.wait()
        self.beside.wait_recv()
        if self.sideways:
            self.wait_layers(lambda layer: None)
            for layer in range(LAYERS):
                awaited = here.z != layer
                mine, _ = relayed(here.z, layer)
                if mine is not None:
                    awaited = jnp.logical_and(awaited, jnp.logical_not(mine))

                @pl.when(awaited)
                def _():
                    for step in range(1, here.mids):
                        self.climbed(step, layer, layer).wait_recv()

            return
        for step in range(1, here.mids):
            for core in range(CORES):
                self.side(step, core, True).wait_recv()
        for layer in range(LAYERS):

            @pl.when(here.z != layer)
            def _():
                for step in range(1, here.mids):
                    self.crossing(step, layer).wait_recv()

    def finish(self):
        here = self.place
        self.beside.wait_send()
        for step in range(1, here.mids):
            for core in range(CORES):
                self.side(step, core, False).wait_send()
        for layer in range(LAYERS):

            @pl.when(apart(here.z, layer))
            def _():
                for core in range(CORES):
                    self.hop(layer, core, None).wait_send()
                if self.sideways:
                    for step in range(1, here.mids):
                        self.climb(step, layer).wait_send()

            mine, goal = relayed(here.z, layer)
            if mine is not None:

                @pl.when(mine)
                def _():
                    for core in range(CORES):
                        self.pass_on(layer, core, goal).wait_send()
                    if self.sideways:
                        for step in range(1, here.mids):
                            self.climbed(step, layer, goal).wait_send()

            if not self.sideways:

                @pl.when(here.z != layer)
                def _():
                    for step in range(1, here.mids):
                        self.crossing(step, layer).wait_send()


class Reduce:
    sideways = False

    def __init__(self, place, source, crossed, landed, passed, stores, slots, sems):
        self.place, self.source, self.crossed, self.landed = place, source, crossed, landed
        self.passed = passed
        (
            self.own_slot,
            self.cross_slot,
            self.sum_slot,
            self.land_slot,
            self.out_slot,
            self.turn_slot,
            self.pass_slot,
        ) = slots
        self.send, self.receive, local = sems
        here = place
        self.crossings = [
            remote(
                source.at[:, here.mid(step)],
                crossed.at[step - 1],
                self.send.at[step - 1],
                self.receive.at[step - 1],
                here.device(here.z, here.mid(step), here.k),
            )
            for step in range(1, here.mids)
        ]
        self.base = here.mids
        self.beside = remote(
            self.sum_slot.at[here.z, 1 - here.k],
            landed.at[here.k, here.z],
            self.send.at[here.mids - 1],
            self.receive.at[here.mids - 1],
            here.device(here.z, here.m, 1 - here.k),
        )
        self.keep = pltpu.make_async_copy(
            self.sum_slot.at[here.z, here.k], landed.at[here.k, here.z], local.at[0]
        )
        self.load_own = pltpu.make_async_copy(source.at[:, here.m], self.own_slot, local.at[1])
        self.load_cross = pltpu.make_async_copy(crossed, self.cross_slot, local.at[2])
        self.load_land = pltpu.make_async_copy(landed, self.land_slot, local.at[3])
        self.load_pass = pltpu.make_async_copy(passed, self.pass_slot, local.at[4])
        self.turned = self.turn_slot is not None
        self.stores = [
            pltpu.make_async_copy(piece(self.out_slot, self.turn_slot), target, local.at[5 + at])
            for at, (piece, target) in enumerate(stores)
        ]

    @staticmethod
    def semaphores(mids):
        return max(mids + LAYERS * CORES + 1, LAYERS + 2 + (mids - 1) * CORES)

    def hop(self, layer, core, origin):
        here = self.place
        arrival = here.z * CORES + here.k if origin is None else origin * CORES + core
        return remote(
            self.sum_slot.at[layer, core],
            self.landed.at[here.k, here.z],
            self.send.at[self.base + layer * CORES + core],
            self.receive.at[self.base + arrival],
            here.device(layer, here.m, core),
        )

    def far(self, layer, goal):
        here = self.place
        at = self.base + LAYERS * CORES
        return remote(
            self.sum_slot.at[layer],
            self.passed,
            self.send.at[at],
            self.receive.at[at],
            here.device(goal, here.m, here.k),
        )

    def ends(self):
        return (
            (self.place.z == 0, LAYERS - 1, LAYERS - 2),
            (self.place.z == LAYERS - 1, 0, 1),
        )

    def start(self):
        for crossing in self.crossings:
            crossing.start()

    def load(self):
        self.load_own.start()
        for crossing in self.crossings:
            crossing.wait_recv()
        self.load_cross.start()

    def add(self):
        here = self.place
        self.load_own.wait()
        self.load_cross.wait()

        @pl.loop(0, LAYERS * CORES)
        def _(at):
            layer, core = lax.div(at, CORES), lax.rem(at, CORES)

            @pl.loop(0, self.own_slot.shape[2] // SLICE)
            def _(index):
                where = pl.ds(pl.multiple_of(index * SLICE, SLICE), SLICE)
                total = self.own_slot[layer, core, where].astype(jnp.float32)
                for step in range(1, here.mids):
                    total += self.cross_slot[step - 1, layer, core, where].astype(jnp.float32)
                self.sum_slot[layer, core, where] = total.astype(jnp.bfloat16)

        for end, layer, goal in self.ends():

            @pl.when(end)
            def _():
                self.far(layer, goal).start()

        self.keep.start()
        self.beside.start()
        for layer in range(LAYERS):
            now = apart(here.z, layer)
            if layer in (0, LAYERS - 1):
                now = jnp.logical_and(now, here.z != (1 if layer == 0 else LAYERS - 2))

            @pl.when(now)
            def _():
                for core in range(CORES):
                    self.hop(layer, core, None).start()

    def relay(self):
        for _, layer, goal in self.ends():

            @pl.when(self.place.z == goal)
            def _():
                self.far(layer, goal).wait_recv()
                self.load_pass.start()
                self.load_pass.wait()

                @pl.loop(0, CORES)
                def _(core):
                    total = self.sum_slot[layer, core].astype(jnp.float32)
                    total += self.pass_slot[core].astype(jnp.float32)
                    self.sum_slot[layer, core] = total.astype(jnp.bfloat16)

                for core in range(CORES):
                    self.hop(layer, core, None).start()

    def release(self):
        self.beside.wait_send()
        for layer in range(LAYERS):

            @pl.when(apart(self.place.z, layer))
            def _():
                for core in range(CORES):
                    self.hop(layer, core, None).wait_send()

        for end, layer, goal in self.ends():

            @pl.when(end)
            def _():
                self.far(layer, goal).wait_send()

    def fetch(self):
        self.keep.wait()
        self.beside.wait_recv()
        for layer in range(LAYERS):

            @pl.when(apart(self.place.z, layer))
            def _():
                for core in range(CORES):
                    self.hop(layer, core, layer).wait_recv()

        self.load_land.start()

    def total(self):
        self.load_land.wait()
        here = self.place
        present = [
            jnp.logical_or(here.z == layer, apart(here.z, layer)) for layer in range(LAYERS)
        ]

        @pl.loop(0, CORES)
        def _(core):
            total = None
            for layer in range(LAYERS):
                value = self.land_slot[core, layer].astype(jnp.float32)
                if layer in (0, LAYERS - 1):
                    value = jnp.where(present[layer], value, 0.0)
                total = value if total is None else total + value
            self.out_slot[core] = total
            if self.turned:
                self.turn_slot[core] = total[:, -LANES:].T

        for store in self.stores:
            store.start()

    def stored(self):
        for store in self.stores:
            store.wait()

    def finish(self):
        for crossing in self.crossings:
            crossing.wait_send()


class Climb(Reduce):
    sideways = True

    def __init__(self, place, source, climbed, landed, passed, stores, slots, sems):
        self.place, self.source, self.climbed_to, self.landed = place, source, climbed, landed
        self.passed = passed
        (
            self.own_slot,
            self.climb_slot,
            self.sum_slot,
            self.land_slot,
            self.out_slot,
            self.turn_slot,
            self.pass_slot,
            self.pass_sum,
        ) = slots
        self.send, self.receive, self.local = sems
        here = place
        self.turned = self.turn_slot is not None
        self.beside = remote(
            self.sum_slot.at[here.m, 1 - here.k],
            landed.at[here.k, 0],
            self.send.at[LAYERS + 1],
            self.receive.at[LAYERS + 1],
            here.device(here.z, here.m, 1 - here.k),
        )
        local = self.local
        self.keep = pltpu.make_async_copy(
            self.sum_slot.at[here.m, here.k], landed.at[here.k, 0], local.at[0]
        )
        self.load_own = pltpu.make_async_copy(source.at[here.z], self.own_slot, local.at[1])
        self.load_climbed = pltpu.make_async_copy(climbed, self.climb_slot, local.at[2])
        self.load_land = pltpu.make_async_copy(landed, self.land_slot, local.at[3])
        self.stores = [
            pltpu.make_async_copy(piece(self.out_slot, self.turn_slot), target, local.at[5 + at])
            for at, (piece, target) in enumerate(stores)
        ]

    def up(self, layer, block):
        here = self.place
        return remote(
            block,
            self.climbed_to.at[here.z],
            self.send.at[layer],
            self.receive.at[here.z],
            here.device(layer, here.m, here.k),
        )

    def come(self, layer):
        here = self.place
        block = self.climbed_to.at[layer]
        return remote(
            block,
            block,
            self.send.at[layer],
            self.receive.at[layer],
            here.device(layer, here.m, here.k),
        )

    def far(self, layer, goal):
        here = self.place
        return remote(
            self.source.at[layer],
            self.passed,
            self.send.at[LAYERS],
            self.receive.at[LAYERS],
            here.device(goal, here.m, here.k),
        )

    def across(self, step, core, wait):
        here = self.place
        at = LAYERS + 2 + (step - 1) * CORES
        return remote(
            self.sum_slot.at[here.mid(step), core],
            self.landed.at[here.k, step],
            self.send.at[at + core],
            self.receive.at[at + (core if wait else here.k)],
            here.device(here.z, here.mid(step), core),
        )

    def now(self, layer):
        now = apart(self.place.z, layer)
        if layer in (0, LAYERS - 1):
            now = jnp.logical_and(now, self.place.z != (1 if layer == 0 else LAYERS - 2))
        return now

    def start(self):
        for end, layer, goal in self.ends():

            @pl.when(end)
            def _():
                self.far(layer, goal).start()

        for layer in range(LAYERS):

            @pl.when(self.now(layer))
            def _():
                self.up(layer, self.source.at[layer]).start()

    def relay_up(self):
        here = self.place
        for _, layer, goal in self.ends():

            @pl.when(here.z == goal)
            def _():
                self.far(layer, goal).wait_recv()
                loads = (
                    pltpu.make_async_copy(self.passed, self.pass_slot, self.local.at[4]),
                    pltpu.make_async_copy(
                        self.source.at[layer], self.pass_sum, self.local.at[11]
                    ),
                )
                for copy in loads:
                    copy.start()
                for copy in loads:
                    copy.wait()

                @pl.loop(0, here.mids * CORES)
                def _(at):
                    mid, core = lax.div(at, CORES), lax.rem(at, CORES)
                    total = self.pass_sum[mid, core].astype(jnp.float32)
                    total += self.pass_slot[mid, core].astype(jnp.float32)
                    self.pass_sum[mid, core] = total.astype(jnp.bfloat16)

                self.up(layer, self.pass_sum).start()

    def load(self):
        self.load_own.start()
        for layer in range(LAYERS):

            @pl.when(apart(self.place.z, layer))
            def _():
                self.come(layer).wait_recv()

        self.load_climbed.start()

    def add(self):
        here = self.place
        self.load_own.wait()
        self.load_climbed.wait()
        present = [apart(here.z, layer) for layer in range(LAYERS)]

        @pl.loop(0, here.mids * CORES)
        def _(at):
            mid, core = lax.div(at, CORES), lax.rem(at, CORES)
            total = self.own_slot[mid, core].astype(jnp.float32)
            for layer in range(LAYERS):
                value = self.climb_slot[layer, mid, core].astype(jnp.float32)
                total += jnp.where(present[layer], value, 0.0)
            self.sum_slot[mid, core] = total.astype(jnp.bfloat16)

        for step in range(1, here.mids):
            for core in range(CORES):
                self.across(step, core, False).start()
        self.keep.start()
        self.beside.start()

    def relay(self):
        pass

    def release(self):
        here = self.place
        self.beside.wait_send()
        for step in range(1, here.mids):
            for core in range(CORES):
                self.across(step, core, False).wait_send()
        for layer in range(LAYERS):

            @pl.when(apart(here.z, layer))
            def _():
                self.up(layer, self.source.at[layer]).wait_send()

        for end, layer, goal in self.ends():

            @pl.when(end)
            def _():
                self.far(layer, goal).wait_send()

    def fetch(self):
        self.keep.wait()
        self.beside.wait_recv()
        for step in range(1, self.place.mids):
            for core in range(CORES):
                here = self.place
                at = LAYERS + 2 + (step - 1) * CORES + core
                block = self.landed.at[core, step]
                remote(
                    block,
                    block,
                    self.send.at[at],
                    self.receive.at[at],
                    here.device(here.z, here.mid(step), core),
                ).wait_recv()
        self.load_land.start()

    def total(self):
        self.load_land.wait()

        @pl.loop(0, CORES)
        def _(core):
            total = self.land_slot[core, 0].astype(jnp.float32)
            for step in range(1, self.place.mids):
                total += self.land_slot[core, step].astype(jnp.float32)
            self.out_slot[core] = total
            if self.turned:
                self.turn_slot[core] = total[:, -LANES:].T

        for store in self.stores:
            store.start()

    def finish(self):
        pass


def dots(left, right, left_axis, right_axis):
    return lax.dot_general(
        left, right, (((left_axis,), (right_axis,)), ((), ())), preferred_element_type=jnp.float32
    )


class Reducer:
    def __init__(self, chunks, keys):
        self.chunks, self.keys = chunks, keys
        self.ahead, self.fetch = BEHIND, FETCH
        self.ticks = self.landed = 0
        self.produced, self.started, self.relayed = set(), set(), set()

    def launch(self):
        blocked = False
        for at, chunk in enumerate(self.chunks):
            if at in self.started:
                continue
            ready = at in self.produced
            if chunk.sideways:
                ready = ready and at <= self.ticks + EARLY
            else:
                blocked = blocked or not ready or at > self.ticks + self.ahead
                ready = not blocked
            if ready:
                chunk.start()
                self.started.add(at)

    def relay_up(self, at):
        if at in self.started and self.chunks[at].sideways and at not in self.relayed:
            self.relayed.add(at)
            self.chunks[at].relay_up()

    def produce(self, key):
        self.produced.add(self.keys.index(key))
        self.launch()

    def tick(self):
        at, chunks = self.ticks, self.chunks
        count = len(chunks)
        if at < count:
            assert at in self.started
            self.relay_up(at)
            chunks[at].load()
        self.ticks += 1
        self.launch()
        for near in range(at + 1, min(at + 1 + NEAR, count)):
            self.relay_up(near)
        if 0 <= at - LAG < count:
            chunks[at - LAG].relay()
        if at < count:
            if at >= SUMS:
                chunks[at - SUMS].release()
            chunks[at].add()
        while self.landed <= min(at - self.fetch, count - 1):
            chunks[self.landed].fetch()
            if self.landed >= 2:
                chunks[self.landed - 2].stored()
            chunks[self.landed].total()
            self.landed += 1

    def drain(self):
        count = len(self.chunks)
        self.ahead, self.fetch = AHEAD, LAG + 1
        while self.landed < count:
            self.tick()
        for chunk in self.chunks[-2:]:
            chunk.stored()
        for chunk in self.chunks[-SUMS:]:
            chunk.release()
        for chunk in self.chunks:
            chunk.finish()


class Spread:
    def __init__(self, here, buffer, part, send, receive):
        sibling = here.device(here.z, here.m, 1 - here.k)
        other = (here.device(here.z, here.m, here.k)[0], 1 - here.t)
        self.across, self.beside, self.onward = [], [], []
        for batch in range(2):
            own = buffer.at[pl.ds(here.row(here.k, batch, here.t, part), part)]
            theirs = buffer.at[pl.ds(here.row(here.k, batch, 1 - here.t, part), part)]
            self.across.append(remote(own, own, send.at[batch], receive.at[batch], other))
            self.beside.append(remote(own, own, send.at[2 + batch], receive.at[2 + batch], sibling))
            self.onward.append(
                remote(theirs, theirs, send.at[4 + batch], receive.at[4 + batch], sibling)
            )

    def start(self, batch):
        self.across[batch].start()
        self.beside[batch].start()

    def forward(self):
        for batch in range(2):
            self.across[batch].wait_recv()
            self.onward[batch].start()

    def arrive(self):
        for copy in self.beside + self.onward:
            copy.wait_recv()

    def finish(self):
        for copy in self.across + self.beside + self.onward:
            copy.wait_send()


def backward_kernel(mids, *refs):
    f32, bf16 = jnp.float32, jnp.bfloat16
    (
        rates,
        onehot,
        gains,
        inverse,
        tokens,
        middle,
        cotangent,
        normed_ffn_hbm,
        upstream_hbm,
        normed_hbm,
        act_hbm,
        partial_hbm,
        result_hbm,
        saved_hbm,
        values_hbm,
        weights_hbm,
        weights_go_hbm,
        out_query,
        out_key,
        out_value,
        out_gate,
        out_out,
        out_left,
        out_right,
        out_down,
        out_gain,
        grad_tokens,
        result,
        p_f,
        p_qkv,
        p_go,
        p_gain,
        *rest,
    ) = refs
    crossed, landed, passed, side, rest = rest[:4], rest[4:8], rest[8:12], rest[12:15], rest[15:]
    (
        normed,
        upstream,
        grad_out,
        act,
        stage,
        own_slot,
        cross_slot,
        sum_slot,
        land_slot,
        out_slot,
        turn_slot,
        pass_slot,
        gain_slot,
        side_own,
        side_climb,
        side_sum,
        side_land,
        side_pass,
        side_pass_sum,
        saved,
        values,
        weights,
        projected,
        branch,
        total,
        part,
        part_in,
        across,
        across_in,
        kept,
        grad_middle,
        dot_sum,
        table,
        same,
        columns,
        send,
        receive,
        local,
        row_send,
        row_receive,
        load_sem,
        stage_sem,
        free,
    ) = rest
    rows, width = normed.shape
    half = rows // CORES
    part_rows = half // 4
    length = 2 * part_rows
    heads, units = saved_hbm.shape[0], act_hbm.shape[0]
    here = Place(mids)
    sibling = here.device(here.z, here.m, 1 - here.k)
    other = (here.device(here.z, here.m, here.k)[0], 1 - here.t)

    chunks = []
    lists = []

    def columns_of(target, index, count, place):
        for core in range(CORES):
            where = pl.ds((core * count + index) * LANES, LANES)
            yield (
                lambda out, turn, core=core: out.at[core, :, pl.ds(place * LANES, LANES)],
                target.at[:, where],
            )

    def rows_of(target, index, count):
        for core in range(CORES):
            where = pl.ds((core * count + index) * LANES, LANES)
            yield (lambda out, turn, core=core: turn.at[core], target.at[where])

    order = [index for index in range(units) if index not in CLIMBS]
    for index, place in CLIMBS.items():
        order.insert(place, index)
    for index in order:
        stores = [
            *columns_of(out_left, index, units, 0),
            *columns_of(out_right, index, units, 1),
            *rows_of(out_down, index, units),
        ]
        lists.append((p_f, index, 0, stores, True))
    for index in range(heads):
        stores = []
        for place, target in enumerate((out_query, out_key, out_value)):
            stores += columns_of(target, index, heads, place)
        lists.append((p_qkv, index, 1, stores, False))
        stores = [*columns_of(out_gate, index, heads, 0), *rows_of(out_out, index, heads)]
        lists.append((p_go, index, 2, stores, True))
    lists.append((p_gain, 0, 3, [], False))
    for at, (source, index, kind, stores, turned) in enumerate(lists):
        wide = source.shape[-1]
        if kind == 0 and index in CLIMBS:
            nth = list(CLIMBS).index(index)
            chunks.append(
                Climb(
                    here,
                    source.at[index],
                    *[buffer.at[nth] for buffer in side],
                    stores,
                    (
                        side_own,
                        side_climb,
                        side_sum,
                        side_land,
                        out_slot.at[at % 2],
                        turn_slot.at[at % 2],
                        side_pass,
                        side_pass_sum,
                    ),
                    (send.at[at], receive.at[at], local.at[at]),
                )
            )
            continue
        slots = [
            slot.at[(at % slot.shape[0],) + (slice(None),) * (len(slot.shape) - 2) + (pl.ds(0, wide),)]
            for slot in (own_slot, cross_slot, sum_slot, land_slot, out_slot)
        ]
        slots.append(turn_slot.at[at % 2] if turned else None)
        slots.append(pass_slot.at[:, :, pl.ds(0, wide)])
        chunks.append(
            Reduce(
                here,
                source.at[index],
                crossed[kind].at[index],
                landed[kind].at[index],
                passed[kind].at[index],
                stores,
                slots,
                (send.at[at], receive.at[at], local.at[at]),
            )
        )
    reducer = Reducer(chunks, [(kind, index) for _, index, kind, _, _ in lists])

    def load(source, target, at):
        return pltpu.make_async_copy(source, target, load_sem.at[at])

    loads = {
        "normed_ffn": load(normed_ffn_hbm, normed, 0),
        "upstream": load(upstream_hbm, upstream, 1),
        "part": load(partial_hbm.at[pl.ds(here.k * half, half)], part, 2),
        "normed": load(normed_hbm, normed, 3),
    }
    acts = [load(act_hbm.at[at], act.at[at % 2], 4 + at % 2) for at in range(units)]
    head_loads = [
        (
            load(saved_hbm.at[at], saved.at[0], 6),
            load(values_hbm.at[at], values.at[0], 8),
            load(weights_hbm.at[at], weights.at[0, :, pl.ds(0, 3 * LANES)], 10),
            load(weights_go_hbm.at[at], weights.at[0, :, pl.ds(3 * LANES, 2 * LANES)], 13),
        )
        for at in range(heads)
    ]
    loads["normed_ffn"].start()
    acts[0].start()
    loads["upstream"].start()
    loads["part"].start()
    greet(here.weight_peers() + [other])

    def swap_beside(source, at):
        return remote(source, part_in, row_send.at[12 + at], row_receive.at[12 + at], sibling)

    def swap_across(batch, at):
        block = pl.ds(batch * part_rows, part_rows)
        return remote(
            across.at[block],
            across_in.at[block],
            row_send.at[15 + 2 * at + batch],
            row_receive.at[15 + 2 * at + batch],
            other,
        )

    beside = swap_beside(partial_hbm.at[pl.ds((1 - here.k) * half, half)], 0)
    beside.start()

    per_block = 2 * LANES
    group = per_block // (CORES * p_f.shape[4])
    turns = mids // group

    def store_block(slot, at, first, value):
        layer, chip = lax.div(at, turns), lax.rem(at, turns) * group
        shaped = value.astype(bf16).reshape(group, CORES, p_f.shape[4], value.shape[-1])
        stage[slot, layer, pl.ds(chip, group), :, :, pl.ds(first, value.shape[-1])] = shaped

    def stage_out(slot, target):
        wide = target.shape[-1]
        return pltpu.make_async_copy(
            stage.at[slot, :, :, :, :, pl.ds(0, wide)], target, stage_sem.at[slot]
        )

    pending = [None, None]

    def send_stage(slot, target, kind, index):
        copy = stage_out(slot, target.at[index])
        copy.start()
        pending[slot] = (copy, (kind, index))

    def flush(slot):
        if pending[slot] is not None:
            copy, key = pending[slot]
            copy.wait()
            pending[slot] = None
            reducer.produce(key)

    def unit_chunk(at):
        slot = at % 2
        if at + 1 < units:
            acts[at + 1].start()
        acts[at].wait()
        flush(slot)

        @pl.loop(0, width // per_block)
        def _(block):
            where = pl.ds(pl.multiple_of(block * per_block, per_block), per_block)
            store_block(slot, block, 0, dots(normed[:, where], act[slot, :, : 2 * LANES], 0, 0))
            store_block(
                slot, block, 2 * LANES, dots(upstream[:, where], act[slot, :, 2 * LANES :], 0, 0)
            )

        flush(1 - slot)
        send_stage(slot, p_f, 0, at)
        if at < 2:
            flush(slot)

    step_rows = 16

    def row_loop(count):
        return pl.loop(0, count // step_rows)

    def at_rows(base, index):
        return pl.ds(pl.multiple_of(base + index * step_rows, step_rows), step_rows)

    def reduce_beside(own):
        def leave(batch):
            @row_loop(part_rows)
            def _(index):
                base = batch * length + (1 - here.t) * part_rows
                value = own(base, index) + part_in[at_rows(base, index), :].astype(f32)
                across[at_rows(batch * part_rows, index), :] = value.astype(bf16)

        def keep(batch):
            @row_loop(part_rows)
            def _(index):
                base = batch * length + here.t * part_rows
                value = own(base, index) + part_in[at_rows(base, index), :].astype(f32)
                kept[at_rows(batch * part_rows, index), :] = value

        return leave, keep

    loads["normed_ffn"].wait()
    loads["upstream"].wait()
    unit_chunk(0)
    unit_chunk(1)
    down = lax.broadcasted_iota(jnp.int32, (length, length), 0)
    right = lax.broadcasted_iota(jnp.int32, (length, length), 1)
    offset = (down - right).astype(f32)
    for head in range(heads):
        decay = jnp.exp(-rates[head] * jnp.maximum(offset, 0.0))
        table[head] = jnp.where(down >= right, decay, 0.0)
    for sequence in range(rows // length):
        marks = onehot[pl.ds(sequence * length, length), :]
        same[sequence] = dots(marks, marks, 1, 1)

    loads["part"].wait()
    beside.wait_recv()
    leave, keep = reduce_beside(lambda base, index: part[at_rows(base, index), :].astype(f32))
    crossings = [swap_across(batch, 0) for batch in range(2)]
    for batch in range(2):
        leave(batch)
        crossings[batch].start()
    for batch in range(2):
        keep(batch)
    for at in range(2, 6):
        unit_chunk(at)
        if at % 2 == 1:
            reducer.tick()
    columns[...] = jnp.zeros_like(columns)
    rows_go = Spread(here, grad_out, part_rows, row_send.at[pl.ds(0, 6)], row_receive.at[pl.ds(0, 6)])
    rows_dot = Spread(here, dot_sum, part_rows, row_send.at[pl.ds(6, 6)], row_receive.at[pl.ds(6, 6)])

    for batch in range(2):
        crossings[batch].wait_recv()
        base = here.row(here.k, batch, here.t, part_rows)

        @row_loop(part_rows)
        def _(index):
            here_rows = at_rows(batch * part_rows, index)
            grad = kept[here_rows, :] + across_in[here_rows, :].astype(f32)
            mid = middle[here_rows, :]
            scale = lax.rsqrt(jnp.mean(mid * mid, axis=-1, keepdims=True) + EPSILON)
            unit = mid * scale
            weighted = grad * unit
            columns[1] += weighted[:8] + weighted[8:]
            scaled = grad * gains[1:2, :]
            slope = cotangent[here_rows, :].astype(f32) + scale * (
                scaled - unit * jnp.mean(scaled * unit, axis=-1, keepdims=True)
            )
            grad_middle[here_rows, :] = slope
            rounded = slope.astype(bf16)
            grad_out[at_rows(base, index), :] = rounded
            attended = mid - tokens[here_rows, :].astype(f32)
            inner = jnp.mean(rounded.astype(f32) * attended, axis=-1, keepdims=True)
            dot_sum[at_rows(base, index), :] = jnp.broadcast_to(inner, (step_rows, LANES))

        rows_go.start(batch)
        rows_dot.start(batch)
    for at in range(6, 9):
        unit_chunk(at)
        if at == 7:
            reducer.tick()
    rows_go.forward()
    rows_dot.forward()
    for at in range(9, units):
        unit_chunk(at)
    for copy in head_loads[0]:
        copy.start()
    loads["normed"].start()
    reducer.tick()
    rows_go.arrive()
    rows_dot.arrive()
    loads["normed"].wait()
    beside.wait_send()
    beside = swap_beside(result_hbm.at[pl.ds((1 - here.k) * half, half)], 1)
    beside.start()
    load_part = load(result_hbm.at[pl.ds(here.k * half, half)], part, 2)
    load_part.start()

    for head in range(heads):
        for copy in head_loads[head]:
            copy.wait()

        @pl.loop(0, rows // length)
        def _(sequence):
            where = pl.ds(pl.multiple_of(sequence * length, length), length)
            query_pre = saved[0, where, 0:LANES]
            key_pre = saved[0, where, LANES : 2 * LANES]
            gate = saved[0, where, 2 * LANES : 3 * LANES]
            scale = inverse[where, :]
            unit = saved[0, where, 3 * LANES : 4 * LANES] * scale
            grad_branch = dots(grad_out[where, :], weights[0, :, 4 * LANES :], 1, 0)
            grad_unit = grad_branch * gate
            branch[where, :] = (unit * gate).astype(bf16)
            projected[where, 3 * LANES :] = (grad_branch * unit).astype(bf16)
            grad_mixed = (scale * (grad_unit - unit * dot_sum[where, :])).astype(bf16)
            query_gate = 1.0 / (1.0 + jnp.exp(-query_pre))
            key_gate = 1.0 / (1.0 + jnp.exp(-key_pre))
            queries = (query_pre * query_gate).astype(bf16)
            keys = (key_pre * key_gate).astype(bf16)
            masked = table[head] * same[sequence]
            mixing = (dots(queries, keys, 1, 1) * masked).astype(bf16)
            grad_scores = (
                dots(grad_mixed, values[0, where, :], 1, 1) * masked
            ).astype(bf16)
            grad_queries = dots(grad_scores, keys, 1, 0)
            grad_keys = dots(grad_scores, queries, 0, 0)
            projected[where, 0:LANES] = (
                grad_queries * (query_gate * (1.0 + query_pre * (1.0 - query_gate)))
            ).astype(bf16)
            projected[where, LANES : 2 * LANES] = (
                grad_keys * (key_gate * (1.0 + key_pre * (1.0 - key_gate)))
            ).astype(bf16)
            projected[where, 2 * LANES : 3 * LANES] = dots(mixing, grad_mixed, 0, 0).astype(bf16)
            product = dots(projected[where, :], weights[0, :, : 4 * LANES], 1, 1)
            if head == 0:
                total[where, :] = product
            else:
                total[where, :] += product

        if head + 1 < heads:
            for copy in head_loads[head + 1]:
                copy.start()
        flush(0)
        flush(1)
        reducer.tick()

        @pl.loop(0, width // per_block)
        def _(block):
            where = pl.ds(pl.multiple_of(block * per_block, per_block), per_block)
            product = dots(normed[:, where], projected[...], 0, 0)
            store_block(0, block, 0, product[:, : 3 * LANES])
            store_block(1, block, 0, product[:, 3 * LANES :])
            store_block(1, block, LANES, dots(grad_out[:, where], branch[...], 0, 0))

        send_stage(0, p_qkv, 1, head)
        send_stage(1, p_go, 2, head)
        if head == heads - 1:
            beside.wait_send()

            @row_loop(half)
            def _(index):
                part[at_rows(0, index), :] = total[
                    at_rows((1 - here.k) * half, index), :
                ].astype(bf16)

            pl.semaphore_wait(free.at[0], 1)
            beside = swap_beside(part, 2)
            beside.start()
        flush(0)
        flush(1)
        if head == 0:
            load_part.wait()
            beside.wait_recv()
            leave, keep = reduce_beside(
                lambda base, index: part[at_rows(base, index), :].astype(f32)
            )
            for crossing in crossings:
                crossing.wait_send()
            crossings = [swap_across(batch, 1) for batch in range(2)]
            for batch in range(2):
                leave(batch)
                crossings[batch].start()
            for batch in range(2):
                keep(batch)
            pl.semaphore_signal(free.at[0], inc=1, device_id=sibling, device_id_type=MESH)
        if head == 2:
            for crossing in crossings:
                crossing.wait_recv()
                crossing.wait_send()

            @row_loop(2 * part_rows)
            def _(index):
                here_rows = at_rows(0, index)
                value = kept[here_rows, :] + across_in[here_rows, :].astype(f32)
                across[here_rows, :] = (middle[here_rows, :] + value).astype(bf16)

            store_result = load(across, result, 12)
            store_result.start()
            pl.semaphore_signal(free.at[1], inc=1, device_id=other, device_id_type=MESH)
        reducer.tick()

    beside.wait_recv()
    leave, keep = reduce_beside(
        lambda base, index: total[at_rows(here.k * half + base, index), :]
    )
    crossings = [swap_across(batch, 2) for batch in range(2)]
    store_result.wait()
    pl.semaphore_wait(free.at[1], 1)
    for batch in range(2):
        leave(batch)
        crossings[batch].start()
    for batch in range(2):
        keep(batch)
    reducer.tick()
    for batch in range(2):
        crossings[batch].wait_recv()

        @row_loop(part_rows)
        def _(index):
            here_rows = at_rows(batch * part_rows, index)
            grad = kept[here_rows, :] + across_in[here_rows, :].astype(f32)
            value = tokens[here_rows, :].astype(f32)
            scale = lax.rsqrt(jnp.mean(value * value, axis=-1, keepdims=True) + EPSILON)
            unit = value * scale
            weighted = grad * unit
            columns[0] += weighted[:8] + weighted[8:]
            scaled = grad * gains[0:1, :]
            grad_tokens[here_rows, :] = grad_middle[here_rows, :] + scale * (
                scaled - unit * jnp.mean(scaled * unit, axis=-1, keepdims=True)
            )

    lane = lax.broadcasted_iota(jnp.int32, (8, LANES), 1)

    @pl.loop(0, width // per_block)
    def _(block):
        where = pl.ds(pl.multiple_of(block * per_block, per_block), per_block)
        first = jnp.where(lane == 0, 1.0, 0.0).astype(bf16)
        second = jnp.where(lane == 1, 1.0, 0.0).astype(bf16)
        value = dots(columns[0, :, where].astype(bf16), first, 0, 0)
        value += dots(columns[1, :, where].astype(bf16), second, 0, 0)
        store_block(0, block, 0, value)

    send_stage(0, p_gain, 3, 0)
    flush(0)
    reducer.drain()
    gain_sum = chunks[-1].out_slot[0] + chunks[-1].out_slot[1]
    gain_slot[0] = gain_sum
    gain_copy = remote(
        gain_slot.at[0], gain_slot.at[1], row_send.at[21], row_receive.at[21], other
    )
    gain_copy.start()
    gain_copy.wait_recv()
    out_gain[...] = (gain_sum + gain_slot[1]).T[:8]
    gain_copy.wait_send()
    beside.wait_send()
    for crossing in crossings:
        crossing.wait_send()
    rows_go.finish()
    rows_dot.finish()


def backward(mids, small, large):
    f32, bf16 = jnp.float32, jnp.bfloat16
    shape = jax.ShapeDtypeStruct
    rates, onehot, gains, inverse, tokens, middle, cotangent = small
    normed_ffn, upstream, normed, act, partial, result, saved, values, weights, weights_go = large
    rows, width = normed.shape
    heads, units = saved.shape[0], act.shape[0]
    block_rows = width // (LAYERS * mids * CORES)
    widths = ((units, 3 * LANES), (heads, 3 * LANES), (heads, 2 * LANES), (1, LANES))
    chunks = sum(count for count, _ in widths)
    hops = Reduce.semaphores(mids)
    anywhere = pl.BlockSpec(memory_space=pl.ANY)
    vmem = pl.BlockSpec(memory_space=pltpu.VMEM)
    smem = pl.BlockSpec(memory_space=pltpu.SMEM)
    widest = 3 * LANES
    half, own = rows // CORES, rows // (2 * CORES)
    length = own
    inner, outer = CORES * heads * LANES, CORES * units * LANES
    outs = [shape((block_rows, inner), f32)] * 4 + [shape((inner, block_rows), f32)]
    outs += [shape((block_rows, outer), f32)] * 2 + [shape((outer, block_rows), f32)]
    outs.append(shape((8, block_rows), f32))
    passed = [shape((count, CORES, block_rows, wide), bf16) for count, wide in widths]
    sums = [shape((count, LAYERS, mids, CORES, block_rows, wide), bf16) for count, wide in widths]
    cross = [
        shape((count, mids - 1, LAYERS, CORES, block_rows, wide), bf16) for count, wide in widths
    ]
    land = [shape((count, CORES, LAYERS, block_rows, wide), bf16) for count, wide in widths]
    few = max(len(CLIMBS), 1)
    side = [
        shape((few, LAYERS, mids, CORES, block_rows, widest), bf16),
        shape((few, CORES, mids, block_rows, widest), bf16),
        shape((few, mids, CORES, block_rows, widest), bf16),
    ]
    return pl.pallas_call(
        functools.partial(backward_kernel, mids),
        name="backward",
        out_shape=(*outs, shape((own, width), f32), shape((own, width), bf16), *sums, *cross, *land, *passed, *side),
        in_specs=[smem] + [vmem] * 6 + [anywhere] * 10,
        out_specs=(anywhere,) * 8 + (vmem,) * 2 + (anywhere,) * 20,
        scratch_shapes=[
            pltpu.VMEM((rows, width), bf16),
            pltpu.VMEM((rows, width), bf16),
            pltpu.VMEM((rows, width), bf16),
            pltpu.VMEM((2, rows, widest), bf16),
            pltpu.VMEM((2, LAYERS, mids, CORES, block_rows, widest), bf16),
            pltpu.VMEM((1, LAYERS, CORES, block_rows, widest), bf16),
            pltpu.VMEM((1, mids - 1, LAYERS, CORES, block_rows, widest), bf16),
            pltpu.VMEM((SUMS, LAYERS, CORES, block_rows, widest), bf16),
            pltpu.VMEM((1, CORES, LAYERS, block_rows, widest), bf16),
            pltpu.VMEM((2, CORES, block_rows, widest), f32),
            pltpu.VMEM((2, CORES, LANES, block_rows), f32),
            pltpu.VMEM((CORES, block_rows, widest), bf16),
            pltpu.VMEM((2, block_rows, LANES), f32),
            pltpu.VMEM((mids, CORES, block_rows, widest), bf16),
            pltpu.VMEM((LAYERS, mids, CORES, block_rows, widest), bf16),
            pltpu.VMEM((mids, CORES, block_rows, widest), bf16),
            pltpu.VMEM((CORES, mids, block_rows, widest), bf16),
            pltpu.VMEM((mids, CORES, block_rows, widest), bf16),
            pltpu.VMEM((mids, CORES, block_rows, widest), bf16),
            pltpu.VMEM((1, rows, 4 * LANES), f32),
            pltpu.VMEM((1, rows, LANES), bf16),
            pltpu.VMEM((1, width, 5 * LANES), bf16),
            pltpu.VMEM((rows, 4 * LANES), bf16),
            pltpu.VMEM((rows, LANES), bf16),
            pltpu.VMEM((rows, width), f32),
            pltpu.VMEM((half, width), bf16),
            pltpu.VMEM((half, width), bf16),
            pltpu.VMEM((own, width), bf16),
            pltpu.VMEM((own, width), bf16),
            pltpu.VMEM((own, width), f32),
            pltpu.VMEM((own, width), f32),
            pltpu.VMEM((rows, LANES), f32),
            pltpu.VMEM((heads, length, length), f32),
            pltpu.VMEM((rows // length, length, length), f32),
            pltpu.VMEM((2, 8, width), f32),
            pltpu.SemaphoreType.DMA((chunks, hops)),
            pltpu.SemaphoreType.DMA((chunks, hops)),
            pltpu.SemaphoreType.DMA((chunks, 12)),
            pltpu.SemaphoreType.DMA((22,)),
            pltpu.SemaphoreType.DMA((22,)),
            pltpu.SemaphoreType.DMA((15,)),
            pltpu.SemaphoreType.DMA((2,)),
            pltpu.SemaphoreType.REGULAR((2,)),
        ],
        compiler_params=pltpu.CompilerParams(
            collective_id=1, has_side_effects=True, vmem_limit_bytes=63 * 2**20
        ),
    )(*small, *large)[:11]


class Gatherer:
    def __init__(self, chunks):
        self.chunks = chunks
        self.started = self.crossed = self.passed = self.climbed = 0

    def relay_on(self, last):
        while self.climbed < last:
            self.chunks[self.climbed].relay_on()
            self.climbed += 1

    def relay(self, at):
        if at < len(self.chunks) and self.passed == at:
            self.chunks[at].relay()
            self.passed += 1

    def launch(self):
        while self.started < min(len(self.chunks), self.crossed + BEFORE + 1):
            self.chunks[self.started].start()
            self.started += 1

    def cross(self, count=1):
        for _ in range(count):
            if self.crossed < len(self.chunks):
                self.relay(self.crossed)
                self.chunks[self.crossed].cross()
                self.crossed += 1
                self.launch()
                self.relay(self.crossed)
                self.relay_on(self.crossed - 1)

    def arrive(self, at):
        self.cross(at + 1 - self.crossed)
        self.relay_on(at + 1)
        self.chunks[at].arrive()


def forward_kernel(mids, *refs):
    f32, bf16 = jnp.float32, jnp.bfloat16
    (
        rates,
        own_marks,
        tokens,
        cotangent,
        shard_g,
        shard_go,
        shard_qkv,
        shard_f,
        full_g,
        full_go,
        full_qkv,
        full_f,
        normed_hbm,
        normed_ffn_hbm,
        upstream_hbm,
        act_hbm,
        partial_hbm,
        result_hbm,
        saved_hbm,
        values_hbm,
        marks,
        gains,
        inverse,
        middle,
        normed,
        normed_ffn,
        upstream,
        total,
        grad_total,
        weights,
        out_weights,
        saved,
        values,
        act,
        branch,
        part,
        part_in,
        across,
        across_in,
        kept,
        squares,
        squares_in,
        squares_across,
        squares_across_in,
        table,
        same,
        gain_columns,
        send,
        receive,
        local,
        row_send,
        row_receive,
        load_sem,
        store_sem,
    ) = refs
    rows, width = normed.shape
    half = rows // CORES
    part_rows = half // 4
    length = 2 * part_rows
    heads, units = full_qkv.shape[0], full_f.shape[0]
    here = Place(mids)
    sibling = here.device(here.z, here.m, 1 - here.k)
    other = (here.device(here.z, here.m, here.k)[0], 1 - here.t)
    greet(here.weight_peers() + [other])

    chunks = []
    pairs = [(shard_g, full_g, 0)]
    for index in range(heads):
        pairs += [(shard_go, full_go, index), (shard_qkv, full_qkv, index)]
    pairs += [(shard_f, full_f, index) for index in range(units)]
    for at, (source, target, index) in enumerate(pairs):
        chunks.append(
            Gather(
                here,
                source.at[index],
                target.at[index],
                (send.at[at], receive.at[at], local.at[at]),
                at in SIDEWAYS,
            )
        )
    gatherer = Gatherer(chunks)
    gatherer.launch()

    step_rows = 16

    def row_loop(count):
        return pl.loop(0, count // step_rows)

    def at_rows(base, index):
        return pl.ds(pl.multiple_of(base + index * step_rows, step_rows), step_rows)

    def spread(buffer, at):
        window = pl.ds(6 * at, 6)
        return Spread(here, buffer, part_rows, row_send.at[window], row_receive.at[window])

    rows_normed, rows_up = spread(normed, 0), spread(upstream, 1)
    rows_ffn, rows_inverse = spread(normed_ffn, 2), spread(inverse, 3)
    lone = lambda source, target, at, peer: remote(
        source, target, row_send.at[24 + at], row_receive.at[24 + at], peer
    )

    own_half = pl.ds(pl.multiple_of(here.k * half, half), half)
    far_half = pl.ds(pl.multiple_of((1 - here.k) * half, half), half)
    marks[own_half, :] = own_marks[...]
    marks_copy = lone(own_marks, marks.at[own_half], 0, sibling)
    marks_copy.start()

    gatherer.arrive(0)
    load_gain = pltpu.make_async_copy(full_g.at[0], gain_columns, load_sem.at[0])
    load_gain.start()
    load_gain.wait()
    down = lax.broadcasted_iota(jnp.int32, (8, LANES), 0)
    right = lax.broadcasted_iota(jnp.int32, (8, LANES), 1)
    pick = jnp.where(down == right, 1.0, 0.0).astype(bf16)
    gains[...] = dots(pick, gain_columns[...].reshape(width, LANES), 1, 1)

    for batch in range(2):
        base = here.row(here.k, batch, here.t, part_rows)

        @row_loop(part_rows)
        def _(index):
            here_rows = at_rows(batch * part_rows, index)
            value = tokens[here_rows, :].astype(f32)
            scale = lax.rsqrt(jnp.mean(value * value, axis=-1, keepdims=True) + EPSILON)
            normed[at_rows(base, index), :] = (value * scale * gains[0:1, :]).astype(bf16)

        rows_normed.start(batch)
    for batch in range(2):
        base = here.row(here.k, batch, here.t, part_rows)
        upstream[pl.ds(base, part_rows), :] = cotangent[pl.ds(batch * part_rows, part_rows), :]
        rows_up.start(batch)

    down = lax.broadcasted_iota(jnp.int32, (length, length), 0)
    right = lax.broadcasted_iota(jnp.int32, (length, length), 1)
    offset = (down - right).astype(f32)
    for head in range(heads):
        decay = jnp.exp(-rates[head] * jnp.maximum(offset, 0.0))
        table[head] = jnp.where(down >= right, decay, 0.0)
    marks_copy.wait_recv()
    for sequence in range(rows // length):
        mark = marks[pl.ds(sequence * length, length), :]
        same[sequence] = dots(mark, mark, 1, 1)
    squares[...] = jnp.zeros_like(squares)

    def weight(slot, first, last):
        return weights[slot, :, :, :, :, first * LANES : last * LANES].reshape(
            width, (last - first) * LANES
        )

    def store(source, target, at):
        copy = pltpu.make_async_copy(source, target, store_sem.at[at])
        copy.start()
        return copy

    stores = []
    gatherer.cross()
    rows_normed.forward()
    rows_normed.arrive()
    stores.append(store(normed, normed_hbm, 0))
    gatherer.cross()
    rows_up.forward()

    pending = [[], []]
    for head in range(heads):
        slot = head % 2
        gatherer.cross(3 + 2 * head + LEAD - gatherer.crossed)
        gatherer.arrive(1 + 2 * head)
        load_out = pltpu.make_async_copy(
            full_go.at[head, :, :, :, :, pl.ds(LANES, LANES)],
            out_weights.at[:, :, :, :, pl.ds(head * LANES, LANES)],
            load_sem.at[4 + head],
        )
        load_gate = pltpu.make_async_copy(
            full_go.at[head, :, :, :, :, pl.ds(0, LANES)],
            weights.at[slot, :, :, :, :, pl.ds(3 * LANES, LANES)],
            load_sem.at[2 + slot],
        )
        load_gate.start()
        gatherer.cross(3 + 2 * head + LEAD - gatherer.crossed)
        gatherer.arrive(2 + 2 * head)
        load = pltpu.make_async_copy(
            full_qkv.at[head],
            weights.at[slot, :, :, :, :, pl.ds(0, 3 * LANES)],
            load_sem.at[slot],
        )
        load.start()
        load_out.start()
        for copy in pending[slot]:
            copy.wait()
        load_gate.wait()
        load.wait()

        @pl.loop(0, rows // length)
        def _(sequence):
            where = pl.ds(pl.multiple_of(sequence * length, length), length)
            product = dots(normed[where, :], weight(slot, 0, 4), 1, 0)
            query_pre, key_pre = product[:, :LANES], product[:, LANES : 2 * LANES]
            value = product[:, 2 * LANES : 3 * LANES].astype(bf16)
            gate = product[:, 3 * LANES :]
            queries = (query_pre / (1.0 + jnp.exp(-query_pre))).astype(bf16)
            keys = (key_pre / (1.0 + jnp.exp(-key_pre))).astype(bf16)
            masked = table[head] * same[sequence]
            mixing = (dots(queries, keys, 1, 1) * masked).astype(bf16)
            mixed = dots(mixing, value, 1, 0)
            saved[slot, where, : 2 * LANES] = product[:, : 2 * LANES]
            saved[slot, where, 2 * LANES : 3 * LANES] = gate
            saved[slot, where, 3 * LANES :] = mixed
            values[slot, where, :] = value
            branch[where, head * LANES : (head + 1) * LANES] = (mixed * gate).astype(bf16)
            squares[where, :] += jnp.broadcast_to(
                jnp.sum(mixed * mixed, axis=-1, keepdims=True), (length, LANES)
            )

        pending[slot] = [
            store(saved.at[slot], saved_hbm.at[head], 4 + slot),
            store(values.at[slot], values_hbm.at[head], 6 + slot),
        ]
        load_out.wait()
    stores += pending[0] + pending[1]

    @pl.loop(0, half // length)
    def _(block):
        base = (1 - here.k) * half + block * length
        where = pl.ds(pl.multiple_of(base, length), length)
        to = pl.ds(pl.multiple_of(block * length, length), length)
        part[to, :] = dots(branch[where, :], out_weights[...].reshape(width, -1), 1, 1).astype(bf16)

    beside = lone(part, part_in, 1, sibling)
    beside.start()
    beside_squares = lone(squares.at[far_half], squares_in, 2, sibling)
    beside_squares.start()

    @pl.loop(0, half // length)
    def _(block):
        base = here.k * half + block * length
        where = pl.ds(pl.multiple_of(base, length), length)
        total[where, :] = dots(branch[where, :], out_weights[...].reshape(width, -1), 1, 1)

    beside.wait_recv()
    beside_squares.wait_recv()
    crossings = []
    for batch in range(2):
        block = pl.ds(batch * part_rows, part_rows)
        crossings.append(
            (
                lone(across.at[block], across_in.at[block], 3 + batch, other),
                lone(squares_across.at[block], squares_across_in.at[block], 5 + batch, other),
            )
        )

        @row_loop(part_rows)
        def _(index):
            base = batch * length + (1 - here.t) * part_rows
            value = total[at_rows(here.k * half + base, index), :]
            value += part_in[at_rows(base, index), :].astype(f32)
            to = at_rows(batch * part_rows, index)
            across[to, :] = value.astype(bf16)
            squares_across[to, :] = (
                squares[at_rows(here.k * half + base, index), :]
                + squares_in[at_rows(base, index), :]
            )

        for copy in crossings[batch]:
            copy.start()
    for batch in range(2):

        @row_loop(part_rows)
        def _(index):
            base = batch * length + here.t * part_rows
            value = total[at_rows(here.k * half + base, index), :]
            to = at_rows(batch * part_rows, index)
            kept[to, :] = value + part_in[at_rows(base, index), :].astype(f32)

    gatherer.cross()
    rows_up.arrive()
    stores.append(store(upstream, upstream_hbm, 1))
    for batch in range(2):
        for copy in crossings[batch]:
            copy.wait_recv()
        base = here.row(here.k, batch, here.t, part_rows)

        @row_loop(part_rows)
        def _(index):
            here_rows = at_rows(batch * part_rows, index)
            from_rows = batch * length + here.t * part_rows
            square = (
                squares[at_rows(here.k * half + from_rows, index), :]
                + squares_in[at_rows(from_rows, index), :]
                + squares_across_in[here_rows, :]
            )
            scale = lax.rsqrt(square / width + EPSILON)
            inverse[at_rows(base, index), :] = scale
            attended = (kept[here_rows, :] + across_in[here_rows, :].astype(f32)) * scale[:, :1]
            mid = tokens[here_rows, :].astype(f32) + attended
            middle[here_rows, :] = mid
            scale = lax.rsqrt(jnp.mean(mid * mid, axis=-1, keepdims=True) + EPSILON)
            normed_ffn[at_rows(base, index), :] = (mid * scale * gains[1:2, :]).astype(bf16)

        rows_ffn.start(batch)
        rows_inverse.start(batch)
    gatherer.cross()
    rows_ffn.forward()
    rows_inverse.forward()
    gatherer.cross()
    rows_ffn.arrive()
    rows_inverse.arrive()
    stores.append(store(normed_ffn, normed_ffn_hbm, 2))

    pending = [None, None]
    for at in range(units):
        slot = at % 2
        gatherer.cross(2 + 2 * heads + at + 1 - gatherer.crossed)
        gatherer.arrive(1 + 2 * heads + at)
        load = pltpu.make_async_copy(
            full_f.at[at], weights.at[slot, :, :, :, :, pl.ds(0, 3 * LANES)], load_sem.at[slot]
        )
        load.start()
        if pending[slot] is not None:
            pending[slot].wait()
        gatherer.cross()
        if at == units - 1:
            for copy in stores:
                copy.wait()
            rows_normed.finish()
            rows_ffn.finish()
        load.wait()

        @pl.loop(0, rows // length)
        def _(block):
            where = pl.ds(pl.multiple_of(block * length, length), length)
            product = dots(normed_ffn[where, :], weight(slot, 0, 2), 1, 0)
            left, right = product[:, :LANES], product[:, LANES:]
            grad_joined = dots(upstream[where, :], weight(slot, 2, 3), 1, 0)
            act[slot, where, :LANES] = (grad_joined * right).astype(bf16)
            act[slot, where, LANES : 2 * LANES] = (grad_joined * left).astype(bf16)
            act[slot, where, 2 * LANES :] = (left * right).astype(bf16)
            out = dots(act[slot, where, 2 * LANES :], weight(slot, 2, 3), 1, 1)
            grad = dots(act[slot, where, : 2 * LANES], weight(slot, 0, 2), 1, 1)
            if at == 0:
                total[where, :] = out
                grad_total[where, :] = grad
            elif at == units - 1:
                normed[where, :] = (total[where, :] + out).astype(bf16)
                normed_ffn[where, :] = (grad_total[where, :] + grad).astype(bf16)
            else:
                total[where, :] += out
                grad_total[where, :] += grad

        pending[slot] = store(act.at[slot], act_hbm.at[at], 8 + slot)

    grads = store(normed_ffn, partial_hbm, 0)
    outs = store(normed, result_hbm, 1)
    for copy in pending + [grads, outs]:
        copy.wait()
    for chunk in chunks:
        chunk.finish()
    rows_up.finish()
    rows_inverse.finish()
    marks_copy.wait_send()
    beside.wait_send()
    beside_squares.wait_send()
    for pair in crossings:
        for copy in pair:
            copy.wait_send()


def forward(mids, rates, marks, tokens, cotangent, shards):
    f32, bf16 = jnp.float32, jnp.bfloat16
    shape = jax.ShapeDtypeStruct
    own, width = tokens.shape
    rows, half = 4 * own, 2 * own
    length = own
    heads, units = shards[1].shape[0], shards[3].shape[0]
    block_rows = shards[0].shape[2]
    full = [shape((w.shape[0], LAYERS, mids) + w.shape[1:], bf16) for w in shards]
    chunks = 1 + 2 * heads + units
    hops = Gather.semaphores(mids)
    anywhere = pl.BlockSpec(memory_space=pl.ANY)
    vmem = pl.BlockSpec(memory_space=pltpu.VMEM)
    smem = pl.BlockSpec(memory_space=pltpu.SMEM)
    block = (LAYERS, mids, CORES, block_rows)
    return pl.pallas_call(
        functools.partial(forward_kernel, mids),
        name="forward",
        out_shape=(
            *full,
            *[shape((rows, width), bf16)] * 3,
            shape((units, rows, 3 * LANES), bf16),
            *[shape((rows, width), bf16)] * 2,
            shape((heads, rows, 4 * LANES), f32),
            shape((heads, rows, LANES), bf16),
            shape((rows, LANES), bf16),
            shape((8, width), f32),
            shape((rows, LANES), f32),
            shape((own, width), f32),
        ),
        in_specs=[smem] + [vmem] * 3 + [anywhere] * 4,
        out_specs=(anywhere,) * 12 + (vmem,) * 4,
        scratch_shapes=[
            pltpu.VMEM((rows, width), bf16),
            pltpu.VMEM((rows, width), bf16),
            pltpu.VMEM((rows, width), bf16),
            pltpu.VMEM((rows, width), f32),
            pltpu.VMEM((rows, width), f32),
            pltpu.VMEM((2, *block, 4 * LANES), bf16),
            pltpu.VMEM((*block, heads * LANES), bf16),
            pltpu.VMEM((2, rows, 4 * LANES), f32),
            pltpu.VMEM((2, rows, LANES), bf16),
            pltpu.VMEM((2, rows, 3 * LANES), bf16),
            pltpu.VMEM((rows, heads * LANES), bf16),
            pltpu.VMEM((half, width), bf16),
            pltpu.VMEM((half, width), bf16),
            pltpu.VMEM((own, width), bf16),
            pltpu.VMEM((own, width), bf16),
            pltpu.VMEM((own, width), f32),
            pltpu.VMEM((rows, LANES), f32),
            pltpu.VMEM((half, LANES), f32),
            pltpu.VMEM((own, LANES), f32),
            pltpu.VMEM((own, LANES), f32),
            pltpu.VMEM((heads, length, length), f32),
            pltpu.VMEM((rows // length, length, length), f32),
            pltpu.VMEM((*block, LANES), bf16),
            pltpu.SemaphoreType.DMA((chunks, hops)),
            pltpu.SemaphoreType.DMA((chunks, hops)),
            pltpu.SemaphoreType.DMA((chunks,)),
            pltpu.SemaphoreType.DMA((31,)),
            pltpu.SemaphoreType.DMA((31,)),
            pltpu.SemaphoreType.DMA((4 + heads,)),
            pltpu.SemaphoreType.DMA((10,)),
        ],
        compiler_params=pltpu.CompilerParams(
            collective_id=0, has_side_effects=True, vmem_limit_bytes=63 * 2**20
        ),
    )(rates, marks, tokens, cotangent, *shards)


def split_heads(weight, halves):
    return weight.reshape(weight.shape[0], CORES, -1, LANES)


def pack(parts):
    joined = jnp.concatenate([split_heads(part, CORES) for part in parts], axis=-1)
    return joined.transpose(2, 1, 0, 3)


def local(
    mids,
    tokens,
    segment_ids,
    decay_rates,
    gain_attn,
    w_query,
    w_key,
    w_value,
    w_gate,
    w_out,
    gain_ffn,
    w_left,
    w_right,
    w_down,
    cotangent,
):
    f32, bf16 = jnp.float32, jnp.bfloat16
    batches, local_rows, model_width = tokens.shape
    core = lax.rem(lax.axis_index("dp"), CORES)
    heads = decay_rates.shape[0] // CORES
    rates = lax.dynamic_slice_in_dim(decay_rates, core * heads, heads)
    own = lambda values: values.reshape(batches * local_rows, model_width)
    marks = (segment_ids.reshape(-1)[:, None] == jnp.arange(LANES)[None, :]).astype(bf16)
    gain_columns = jnp.pad(
        jnp.stack([gain_attn, gain_ffn], axis=1), ((0, 0), (0, LANES - 2))
    )
    shards = (
        jnp.stack([gain_columns] * CORES)[None],
        pack([w_gate, w_out.T]),
        pack([w_query, w_key, w_value]),
        pack([w_left, w_right, w_down.T]),
    )
    (
        _,
        full_go,
        full_qkv,
        _,
        normed,
        normed_ffn,
        upstream,
        act,
        partial,
        result,
        saved,
        values,
        marks,
        gains,
        inverse,
        middle,
    ) = forward(mids, rates, marks, own(tokens), own(cotangent), shards)
    full_go = full_go.reshape(heads, model_width, -1)
    full_qkv = full_qkv.reshape(heads, model_width, -1)
    *grads, grad_gains, grad_tokens, result = backward(
        mids,
        (rates, marks, gains, inverse, own(tokens), middle, own(cotangent)),
        (normed_ffn, upstream, normed, act, partial, result, saved, values, full_qkv, full_go),
    )
    result = result.reshape(tokens.shape)
    return (
        result,
        grad_tokens.reshape(tokens.shape),
        grad_gains[0],
        *grads[:5],
        grad_gains[1],
        *grads[5:],
    )


def solution(mesh):
    return jax.shard_map(
        functools.partial(local, mesh.shape["dp"] // (LAYERS * CORES)),
        mesh=mesh,
        in_specs=(
            P(None, ("dp", "tensor"), None),
            P(None, "dp"),
            P("tensor"),
            P("dp"),
            P("dp", "tensor"),
            P("dp", "tensor"),
            P("dp", "tensor"),
            P("dp", "tensor"),
            P("tensor", "dp"),
            P("dp"),
            P("dp", "tensor"),
            P("dp", "tensor"),
            P("tensor", "dp"),
            P(None, ("dp", "tensor"), None),
        ),
        out_specs=(
            P(None, ("dp", "tensor"), None),
            P(None, ("dp", "tensor"), None),
            P("dp"),
            P("dp", "tensor"),
            P("dp", "tensor"),
            P("dp", "tensor"),
            P("dp", "tensor"),
            P("tensor", "dp"),
            P("dp"),
            P("dp", "tensor"),
            P("dp", "tensor"),
            P("tensor", "dp"),
        ),
        check_vma=False,
    )
```
